32 devices in a mesh: expert: 4 (over x, core), context: 4 (over z), dp: 2 (over y).
Axes of the slice: x: 2, y: 2, z: 4, core: 2. Of those that a mesh axis runs over, the one named last changes fastest.
Arguments:
- tokens: bfloat16 [8, 1024, 1536], P(('expert', 'dp'), 'context'), may hold values from -6 to 6
- routes: int32 [8, 1024, 8], P(('expert', 'dp'), 'context'), may hold values from 0 to 19, all different within a row
- cotangent: bfloat16 [8, 1024, 1536], P(('expert', 'dp'), 'context'), may hold values from -6 to 6
- norm_attn: bfloat16 [1536], replicated, may hold values from 0.5 to 1.5
- w_query: bfloat16 [1536, 1536], replicated, may hold values from -0.15625 to 0.15625
- w_key: bfloat16 [1536, 512], replicated, may hold values from -0.15625 to 0.15625
- w_value: bfloat16 [1536, 512], replicated, may hold values from -0.15625 to 0.15625
- w_out: bfloat16 [1536, 1536], replicated, may hold values from -1.25 to 1.25
- norm_ffn: bfloat16 [1536], replicated, may hold values from 0.5 to 1.5
- w_router: bfloat16 [1536, 20], replicated, may hold values from -0.078125 to 0.078125
- w_gate: bfloat16 [20, 1536, 512], P('expert'), may hold values from -0.15625 to 0.15625
- w_up: bfloat16 [20, 1536, 512], P('expert'), may hold values from -0.15625 to 0.15625
- w_down: bfloat16 [20, 512, 1536], P('expert'), may hold values from -0.75 to 0.75
Outputs:
- layer_out: bfloat16 [8, 1024, 1536], P(('expert', 'dp'), 'context')
- grad_tokens: bfloat16 [8, 1024, 1536], P(('expert', 'dp'), 'context')
- grad_norm_attn: float32 [1536], P(('expert', 'context', 'dp'))
- grad_w_query: float32 [1536, 1536], P(('expert', 'context', 'dp'))
- grad_w_key: float32 [1536, 512], P(('expert', 'context', 'dp'))
- grad_w_value: float32 [1536, 512], P(('expert', 'context', 'dp'))
- grad_w_out: float32 [1536, 1536], P(('expert', 'context', 'dp'))
- grad_norm_ffn: float32 [1536], P(('expert', 'context', 'dp'))
- grad_w_router: float32 [1536, 20], P(('expert', 'context', 'dp'))
- grad_w_gate: float32 [20, 1536, 512], P('expert', ('context', 'dp'))
- grad_w_up: float32 [20, 1536, 512], P('expert', ('context', 'dp'))
- grad_w_down: float32 [20, 512, 1536], P('expert', ('context', 'dp'))
The draws below stay inside these ranges and needn't reach their ends.
Inputs may be any that keep to these rules, and one draw needn't show every extreme that they name: `routes`: each token names 8 different experts; every expert is named by some token.
All inputs are finite; a program needn't handle non-finite values.
Results may differ from the reference program's by a relative error of at most 0.018.
Values may be sent and summed in bfloat16 or wider, within the bound.
No kernel may reach another device: no remote copies, remote signals or barrier semaphores. Data moves between devices by JAX's collectives and lax.ppermute only.
A program may use at most 256 MiB of HBM per device.

```python
import jax
import jax.numpy as jnp
from jax import lax

D = 1536
HEADS = 24
KV_HEADS = 8
HEAD_DIM = 64
FF = 512
TOP = 8
TOK_DEV = 256
EXPERTS = 20
QD = 1536
KVD = 512
SEQ_LEN = 1024
SEQS = 8
CAP = 116
N_CONTEXT = 4


def block_scale(stream_key, dims, pieces, least, high):
    level = 1.0
    for axis_at, shards_of in pieces:
        steps = jax.random.uniform(jax.random.fold_in(jax.random.fold_in(stream_key, 6), axis_at), (shards_of,), jnp.float32, least / len(pieces), high / len(pieces))
        level = level * jnp.repeat(jnp.exp(steps), dims[axis_at] // shards_of).reshape((-1,) + (1,) * (len(dims) - 1 - axis_at))
    return level


def different_ones(rng, rows, count, top, lift):
    order = jax.random.permutation(jax.random.fold_in(rng, 1), count)
    favour = order
    for power in range(3):
        favour = favour * favour // count
    favour = favour * lift // count
    chance = jax.random.randint(jax.random.fold_in(rng, 2), (rows, count), 0, 4096) + favour
    holders = jax.random.permutation(jax.random.fold_in(rng, 3), rows)[jnp.arange(count) % rows]
    chance = jnp.where(jnp.arange(rows)[:, None] == holders[None, :], 1 << 14, chance)
    priority = chance * count + jnp.arange(count)
    return lax.top_k(priority.astype(jnp.int32), top)[1].astype(jnp.int32)


def normal_values(key, dims, width, bound, split=(), kind=jnp.bfloat16):
    gain = block_scale(key, dims, split, -0.22, 0.18) if split else 1.0
    values = jax.random.normal(key, dims, jnp.float32) * width * gain
    return jnp.minimum(jnp.maximum(values, -bound), bound).astype(kind)


def setup_inputs(seed: int = 0) -> dict:
    arg_keys = jax.random.split(jax.random.key(seed), 14)
    return {
        "tokens": normal_values(arg_keys[0], (SEQS, SEQ_LEN, D), 1.0, 6.0, ((0, 8), (1, 4))),
        "routes": different_ones(arg_keys[1], SEQS * SEQ_LEN, EXPERTS, TOP, 3276).reshape((SEQS, SEQ_LEN, TOP)),
        "cotangent": normal_values(arg_keys[2], (SEQS, SEQ_LEN, D), 1.0, 6.0, ((0, 8), (1, 4))),
        "norm_attn": jnp.clip(1.0 + 0.1 * jax.random.normal(arg_keys[3], (D,), jnp.float32), 0.5, 1.5).astype(jnp.bfloat16),
        "w_query": normal_values(arg_keys[4], (D, QD), D ** -0.5, 0.15625),
        "w_key": normal_values(arg_keys[5], (D, KVD), D ** -0.5, 0.15625),
        "w_value": normal_values(arg_keys[6], (D, KVD), D ** -0.5, 0.15625),
        "w_out": normal_values(arg_keys[7], (QD, D), (QD // 64) ** -0.5, 1.25),
        "norm_ffn": jnp.clip(1.0 + 0.1 * jax.random.normal(arg_keys[8], (D,), jnp.float32), 0.5, 1.5).astype(jnp.bfloat16),
        "w_router": normal_values(arg_keys[9], (D, EXPERTS), (4 * D) ** -0.5, 0.078125),
        "w_gate": normal_values(arg_keys[10], (EXPERTS, D, FF), D ** -0.5, 0.15625, ((0, 4),)),
        "w_up": normal_values(arg_keys[11], (EXPERTS, D, FF), D ** -0.5, 0.15625, ((0, 4),)),
        "w_down": normal_values(arg_keys[12], (EXPERTS, FF, D), (FF // 8) ** -0.5, 0.75, ((0, 4),)),
    }


EPS = 1e-05
ROPE_BASE = 10000.0
NEG_LARGE = -1e+30
HIGHEST = lax.Precision.HIGHEST

@jax.custom_vjp
def low(v):
    return lax.optimization_barrier(v.astype(jnp.bfloat16)).astype(jnp.float32)

@jax.custom_vjp
def low_back(v):
    return v

def low_keep(v):
    return (low(v), None)

def low_pass(kept, grad):
    return (grad,)

def back_keep(v):
    return (v, None)

def back_low(kept, grad):
    return (low(grad),)
low.defvjp(low_keep, low_pass)
low_back.defvjp(back_keep, back_low)

def rope_tables(positions):
    half_dim = HEAD_DIM // 2
    frequency = ROPE_BASE ** (-2.0 * jnp.arange(half_dim, dtype=jnp.float32) / HEAD_DIM)
    angles = positions.astype(jnp.float32)[:, None] * frequency[None, :]
    angles = jnp.concatenate([angles, angles], -1)
    return (jnp.cos(angles), jnp.sin(angles))

def rotate(values, cosine, sine_table):
    half_dim = values.shape[-1] // 2
    turned = jnp.concatenate([-values[..., half_dim:], values[..., :half_dim]], -1)
    return values * cosine[:, None, :] + turned * sine_table[:, None, :]

def attend(queries, keys, values):
    length = queries.shape[0]
    grouping = HEADS // KV_HEADS
    blocks = length // TOK_DEV
    stacked = queries.reshape(blocks, TOK_DEV, KV_HEADS, grouping, HEAD_DIM)
    starts = jnp.arange(blocks, dtype=jnp.int32) * TOK_DEV

    def one_block(inputs):
        query_block, start = inputs
        scores = low_back(HEAD_DIM ** (-0.5) * jnp.einsum('qhgd,khd->hgqk', query_block, keys, precision=HIGHEST))
        visible = (start + jnp.arange(TOK_DEV, dtype=jnp.int32))[:, None] >= jnp.arange(length, dtype=jnp.int32)[None, :]
        scores = jnp.where(visible, scores, NEG_LARGE)
        prob_block = low(jax.nn.softmax(scores, -1))
        return jnp.einsum('hgqk,khd->qhgd', prob_block, values, precision=HIGHEST)
    outputs = lax.map(jax.checkpoint(one_block), (stacked, starts))
    return outputs.reshape(length, HEADS * HEAD_DIM)

def expert_mix(normed, route, w_router, w_gate, w_up, w_down):
    logits = low_back(jnp.dot(normed, w_router, precision=HIGHEST))
    chosen = jnp.take_along_axis(logits, route, 1)
    gate_probs = jax.nn.softmax(chosen, -1)
    flat_route = route.reshape(-1)
    one_hot = (flat_route[:, None] == jnp.arange(EXPERTS, dtype=jnp.int32)[None, :]).astype(jnp.int32)
    ranking = lax.optimization_barrier(jnp.sum((jnp.cumsum(one_hot, 0) - one_hot) * one_hot, 1))
    dest_slot = jnp.where(ranking < CAP, flat_route * CAP + ranking, EXPERTS * CAP).astype(jnp.int32)
    repeated = jnp.repeat(normed, TOP, axis=0)
    buffer = jnp.zeros((EXPERTS * CAP + 1, D), jnp.float32).at[dest_slot].add(repeated)[:EXPERTS * CAP]
    slots_in = low_back(buffer).reshape(EXPERTS, CAP, D)
    gate_act = low_back(jnp.einsum('ecd,edf->ecf', slots_in, w_gate, precision=HIGHEST))
    up_act = low_back(jnp.einsum('ecd,edf->ecf', slots_in, w_up, precision=HIGHEST))
    hidden_act = low(jax.nn.silu(gate_act) * up_act)
    expert_out = low(low_back(jnp.einsum('ecf,efd->ecd', hidden_act, w_down, precision=HIGHEST)))
    padded = jnp.concatenate([expert_out.reshape(EXPERTS * CAP, D), jnp.zeros((1, D), jnp.float32)], 0)
    picked = padded[dest_slot].reshape(normed.shape[0], TOP, D)
    return lax.optimization_barrier(jnp.sum(gate_probs[:, :, None] * picked, 1))

def block_layer(hidden, route, params):
    norm_attn, w_query, w_key, w_value, w_out, norm_ffn, w_router, w_gate, w_up, w_down = params
    length = hidden.shape[0]
    grouping = HEADS // KV_HEADS
    scale_attn = lax.rsqrt(lax.optimization_barrier(jnp.mean(hidden * hidden, -1, keepdims=True)) + EPS)
    normed_attn = low(hidden * scale_attn * norm_attn)
    query_raw = low_back(jnp.dot(normed_attn, w_query, precision=HIGHEST))
    key_raw = low_back(jnp.dot(normed_attn, w_key, precision=HIGHEST))
    value_raw = low_back(jnp.dot(normed_attn, w_value, precision=HIGHEST))
    cosine, sine_table = rope_tables(jnp.arange(length, dtype=jnp.int32))
    queries = low(rotate(query_raw.reshape(length, HEADS, HEAD_DIM), cosine, sine_table))
    queries = queries.reshape(length, KV_HEADS, grouping, HEAD_DIM)
    keys = low(rotate(key_raw.reshape(length, KV_HEADS, HEAD_DIM), cosine, sine_table))
    values = low(value_raw).reshape(length, KV_HEADS, HEAD_DIM)
    attn_out = low(low_back(attend(queries, keys, values)))
    middle = hidden + low_back(jnp.dot(attn_out, w_out, precision=HIGHEST))
    scale_ffn = lax.rsqrt(lax.optimization_barrier(jnp.mean(middle * middle, -1, keepdims=True)) + EPS)
    normed_ffn = low(middle * scale_ffn * norm_ffn)
    ffn_sum = jax.vmap(expert_mix, in_axes=(0, 0, None, None, None, None))(normed_ffn.reshape(N_CONTEXT, TOK_DEV, D), route.reshape(N_CONTEXT, TOK_DEV, TOP), w_router, w_gate, w_up, w_down)
    return middle + ffn_sum.reshape(length, D)

def reference(tokens, routes, cotangent, norm_attn, w_query, w_key, w_value, w_out, norm_ffn, w_router, w_gate, w_up, w_down):
    weights = tuple((array_in.astype(jnp.float32) for array_in in (norm_attn, w_query, w_key, w_value, w_out, norm_ffn, w_router, w_gate, w_up, w_down)))

    def per_sequence(summed, inputs):
        hidden, route, upstream = inputs
        result, pullback = jax.vjp(lambda values_in, params: block_layer(values_in, route, params), hidden.astype(jnp.float32), weights)
        grad_hidden, grad_params = pullback(upstream.astype(jnp.float32))
        summed = jax.tree.map(lambda first_sum, other_sum: first_sum + other_sum, summed, grad_params)
        return (summed, (result.astype(jnp.bfloat16), grad_hidden.astype(jnp.bfloat16)))
    start_sums = jax.tree.map(jnp.zeros_like, weights)
    summed, (outputs, grad_in) = lax.scan(per_sequence, start_sums, (tokens, routes, cotangent))
    return (outputs, grad_in, summed[0], summed[1], summed[2], summed[3], summed[4], summed[5], summed[6], summed[7], summed[8], summed[9])
```

```python
import functools

import jax
import jax.numpy as jnp
from jax import lax
from jax.experimental import pallas as pl
from jax.experimental.pallas import tpu as pltpu
from jax.sharding import PartitionSpec as P

HEADS = 24
KV_HEADS = 8
HEAD_DIM = 64
GROUP = HEADS // KV_HEADS


EPS = 1e-05
ROPE_BASE = 10000.0
NEG_LARGE = -1e30
F32 = jnp.float32
BF16 = jnp.bfloat16
LANES = 128


def rms_scale(values):
    return lax.rsqrt(jnp.mean(values * values, 0, keepdims=True) + EPS)


def norm_back(grad_out, values, scale, gain):
    weighted = gain * grad_out
    return scale * weighted - values * scale**3 * jnp.mean(weighted * values, 0, keepdims=True)


def mm(a, b, da, db):
    return lax.dot_general(a, b, (((da,), (db,)), ((), ())), preferred_element_type=F32)


class Comm:
    def __init__(self):
        self.n_expert = lax.axis_size("expert")
        self.n_context = lax.axis_size("context")
        self.n_dp = lax.axis_size("dp")
        self.cores = 2 if self.n_expert % 2 == 0 else 1
        self.columns = self.n_expert // self.cores
        self.share = 2 if self.n_context % 2 == 0 else 1

    def peer(self, i, k, j):
        column, core = divmod(i, self.cores)
        return ((column + k) % self.columns) * self.cores + (core + j) % self.cores

    def pull(self, value, k, j):
        pairs = [(self.peer(i, k, j), i) for i in range(self.n_expert)]
        return lax.ppermute(value, "expert", pairs)

    def push(self, value, k, j):
        pairs = [(i, self.peer(i, k, j)) for i in range(self.n_expert)]
        return lax.ppermute(value, "expert", pairs)

    def pair(self, value):
        return lax.ppermute(value, "context", [(i, i ^ 1) for i in range(self.n_context)])

    def gather_expert(self, value):
        row = [value] + [self.pull(value, k, 0) for k in range(1, self.columns)]
        row = jnp.concatenate(row, 1)
        if self.cores == 2:
            row = jnp.concatenate([row, self.pull(row, 0, 1)], 1)
        return row

    def gather_group(self, value):
        if self.share == 1:
            return self.gather_expert(value)
        half = value.shape[0] // 2
        column_blocks = [self.pull(value, k, 0) for k in range(1, self.columns)]
        across = self.pair(value)
        far = []
        for k in range(1, self.columns):
            top = self.pull(across[:half], k, 0)
            bottom = self.pair(column_blocks[k - 1][half:])
            far.append(jnp.concatenate([top, bottom]))
        row = jnp.concatenate([value] + column_blocks + [across] + far, 1)
        if self.cores == 2:
            row = jnp.concatenate([row, self.pull(row, 0, 1)], 1)
        return row

    def return_near(self, parts):
        n = parts.shape[0]
        if self.cores == 1:
            return parts
        other = self.push(parts[n // 2 :], 0, 1)
        return (parts[: n // 2].astype(F32) + other.astype(F32)).astype(BF16)

    def return_far(self, near):
        columns = self.columns
        if self.share == 1:
            total = near[0].astype(F32)
            for k in range(1, columns):
                total = total + self.push(near[k], k, 0).astype(F32)
            return total
        half = near.shape[1] // 2
        near = near.reshape((2, columns) + near.shape[1:])
        top = near[:, 0, :half].astype(F32)
        for k in range(1, columns):
            top = top + self.push(near[:, k, :half], k, 0).astype(F32)
        bottom = near[0, :, half:].astype(F32) + self.pair(near[1, :, half:]).astype(F32)
        top = top[0] + self.pair(top[1].astype(BF16)).astype(F32)
        bottom_low = bottom.astype(BF16)
        bottom = bottom[0]
        for k in range(1, columns):
            bottom = bottom + self.push(bottom_low[k], k, 0).astype(F32)
        return jnp.concatenate([top, bottom])

    def scatter_dp(self, parts):
        me = lax.axis_index("dp")
        n = self.n_dp
        total = lax.dynamic_index_in_dim(parts, me, 0, False).astype(F32)
        for s in range(1, n):
            send = lax.dynamic_index_in_dim(parts, (me + s) % n, 0, False).astype(BF16)
            pairs = [(i, (i + s) % n) for i in range(n)]
            total = total + lax.ppermute(send, "dp", pairs).astype(F32)
        return total

    def scatter_context(self, parts, stride):
        n = self.n_context // stride
        me = lax.axis_index("context") // stride
        total = lax.dynamic_index_in_dim(parts, me, 0, False).astype(F32)
        for s in range(1, n):
            send = lax.dynamic_index_in_dim(parts, (me + s) % n, 0, False).astype(BF16)
            pairs = []
            for i in range(self.n_context):
                k, r = divmod(i, stride)
                pairs.append((i, ((k + s) % n) * stride + r))
            total = total + lax.ppermute(send, "context", pairs).astype(F32)
        return total


def attn_fwd_kernel(blocks, c_ref, q_ref, *refs):
    k_refs, v_refs = refs[:blocks], refs[blocks : 2 * blocks]
    o_ref, ob_ref, lse_ref, scores_ref = refs[2 * blocks :]
    c = c_ref[0]
    n = q_ref.shape[1]
    hd = HEAD_DIM
    for s in range(blocks):
        rows = slice(s * n, (s + 1) * n)

        def fill(s=s, rows=rows):
            for g in range(GROUP):
                scores = mm(k_refs[s][...], q_ref[g * hd : (g + 1) * hd, :], 0, 0)
                if s == 0:
                    key = lax.broadcasted_iota(jnp.int32, scores.shape, 0)
                    query = lax.broadcasted_iota(jnp.int32, scores.shape, 1)
                    scores = jnp.where(key <= query, scores, NEG_LARGE)
                scores_ref[g, rows, :] = scores

        def blank(rows=rows):
            for g in range(GROUP):
                scores_ref[g, rows, :] = jnp.full((n, n), NEG_LARGE, F32)

        if s == 0:
            fill()
        else:
            pl.when(c >= s)(fill)
            pl.when(c < s)(blank)
    lse_ref[...] = jnp.zeros_like(lse_ref)
    for g in range(GROUP):
        scores = scores_ref[g]
        top = jnp.max(scores, 0, keepdims=True)
        weights = jnp.exp(scores - top)
        total = jnp.sum(weights, 0, keepdims=True)
        weights = weights.astype(BF16)
        out = jnp.zeros((hd, n), F32)
        for s in range(blocks):
            out = out + mm(v_refs[s][...], weights[s * n : (s + 1) * n], 1, 0)
        out = out / total
        o_ref[g * hd : (g + 1) * hd, :] = out
        ob_ref[g * hd : (g + 1) * hd, :] = out.astype(BF16)
        lse_ref[0, g : g + 1, :] = top + jnp.log(total)


def kv_specs(blocks, n):
    keys = [pl.BlockSpec((HEAD_DIM, n), lambda h, c: (h, 0))] * blocks
    values = [pl.BlockSpec((HEAD_DIM, n), lambda h, c: (h + KV_HEADS, 0))] * blocks
    return keys + values


def attention_forward(context_index, query_t, kv_blocks):
    blocks = len(kv_blocks)
    n = query_t.shape[1]
    wide = GROUP * HEAD_DIM
    head = pl.BlockSpec((wide, n), lambda h, c: (h, 0))
    return pl.pallas_call(
        functools.partial(attn_fwd_kernel, blocks),
        out_shape=(
            jax.ShapeDtypeStruct(query_t.shape, F32),
            jax.ShapeDtypeStruct(query_t.shape, BF16),
            jax.ShapeDtypeStruct((KV_HEADS, 8, n), F32),
        ),
        grid_spec=pltpu.PrefetchScalarGridSpec(
            num_scalar_prefetch=1,
            grid=(KV_HEADS,),
            in_specs=[head] + kv_specs(blocks, n),
            out_specs=(head, head, pl.BlockSpec((1, 8, n), lambda h, c: (h, 0, 0))),
            scratch_shapes=[pltpu.VMEM((GROUP, blocks * n, n), F32)],
        ),
        compiler_params=pltpu.CompilerParams(vmem_limit_bytes=40 << 20),
        cost_estimate=pl.CostEstimate(
            flops=HEADS * blocks * n * n * 256 * 4,
            transcendentals=HEADS * blocks * n * n,
            bytes_accessed=16 * query_t.size,
        ),
        name="attn_fwd",
    )(context_index.reshape(1), query_t, *kv_blocks, *kv_blocks)


def attn_bwd_kernel(blocks, c_ref, q_ref, do_ref, o_ref, lse_ref, *refs):
    k_refs, v_refs = refs[:blocks], refs[blocks : 2 * blocks]
    dq_ref, dkv_ref = refs[2 * blocks :]
    c = c_ref[0]
    n = q_ref.shape[1]
    hd = HEAD_DIM
    deltas = []
    for g in range(GROUP):
        head = slice(g * hd, (g + 1) * hd)
        both = do_ref[head, :].astype(F32) * o_ref[head, :]
        deltas.append(jnp.sum(both, 0, keepdims=True))
    for s in range(blocks):

        def work(s=s):
            dk = jnp.zeros((hd, n), F32)
            dv = jnp.zeros((hd, n), F32)
            key_t = k_refs[s][...]
            value_t = v_refs[s][...]
            for g in range(GROUP):
                head = slice(g * hd, (g + 1) * hd)
                query, grad = q_ref[head, :], do_ref[head, :]
                scores = mm(key_t, query, 0, 0)
                weights = jnp.exp(scores - lse_ref[0, g : g + 1, :])
                if s == 0:
                    key = lax.broadcasted_iota(jnp.int32, scores.shape, 0)
                    place = lax.broadcasted_iota(jnp.int32, scores.shape, 1)
                    weights = jnp.where(key <= place, weights, 0.0)
                grad_weights = mm(value_t, grad, 0, 0)
                grad_scores = (weights * (grad_weights - deltas[g])).astype(BF16)
                dv = dv + mm(grad, weights.astype(BF16), 1, 1)
                dk = dk + mm(query, grad_scores, 1, 1)
                step = mm(key_t, grad_scores, 1, 0) * (HEAD_DIM**-0.5)
                if s == 0:
                    dq_ref[head, :] = step
                else:
                    dq_ref[head, :] += step
            dkv_ref[s, 0] = dk.astype(BF16)
            dkv_ref[s, 1] = dv.astype(BF16)

        def skip(s=s):
            dkv_ref[s] = jnp.zeros(dkv_ref.shape[1:], BF16)

        if s == 0:
            work()
        else:
            pl.when(c >= s)(work)
            pl.when(c < s)(skip)


def attention_backward(context_index, query_t, grad_t, out_t, lse, kv_blocks):
    blocks = len(kv_blocks)
    n = query_t.shape[1]
    wide = GROUP * HEAD_DIM
    head = pl.BlockSpec((wide, n), lambda h, c: (h, 0))
    return pl.pallas_call(
        functools.partial(attn_bwd_kernel, blocks),
        out_shape=(
            jax.ShapeDtypeStruct(query_t.shape, F32),
            jax.ShapeDtypeStruct((blocks, 2, KV_HEADS * HEAD_DIM, n), BF16),
        ),
        grid_spec=pltpu.PrefetchScalarGridSpec(
            num_scalar_prefetch=1,
            grid=(KV_HEADS,),
            in_specs=[head, head, head, pl.BlockSpec((1, 8, n), lambda h, c: (h, 0, 0))]
            + kv_specs(blocks, n),
            out_specs=(
                head,
                pl.BlockSpec((blocks, 2, HEAD_DIM, n), lambda h, c: (0, 0, h, 0)),
            ),
        ),
        compiler_params=pltpu.CompilerParams(vmem_limit_bytes=40 << 20),
        cost_estimate=pl.CostEstimate(
            flops=HEADS * blocks * n * n * 256 * 10,
            transcendentals=HEADS * blocks * n * n,
            bytes_accessed=20 * query_t.size,
        ),
        name="attn_bwd",
    )(context_index.reshape(1), query_t, grad_t, out_t, lse, *kv_blocks, *kv_blocks)


def rope_tables(positions):
    half_dim = HEAD_DIM // 2
    frequency = ROPE_BASE ** (-2.0 * jnp.arange(half_dim, dtype=F32) / HEAD_DIM)
    angles = frequency[:, None] * positions.astype(F32)[None, :]
    return jnp.cos(angles), jnp.sin(angles)


def rotate_t(values_t, cosine, sine):
    shaped = values_t.reshape(-1, 2, HEAD_DIM // 2, values_t.shape[1])
    low, high = shaped[:, 0], shaped[:, 1]
    turned = jnp.stack([low * cosine - high * sine, high * cosine + low * sine], 1)
    return turned.reshape(values_t.shape)


def prepare_kernel(p_ref, gate_ref, up_ref, down_ref, *outs):
    in_t_ref, gate_out, up_out, down_out, down_t_out = outs
    gate, up, down = gate_ref[0], up_ref[0], down_ref[0]
    in_t_ref[0, 0, 0] = gate.astype(F32).T.astype(BF16)
    in_t_ref[0, 1, 0] = up.astype(F32).T.astype(BF16)
    gate_out[...] = gate
    up_out[...] = up
    down_out[...] = down
    down_t_out[...] = down.astype(F32).T.astype(BF16)


def prepare_weights(parity, w_gate, w_up, w_down, chunk, share):
    experts, width, hidden = w_gate.shape
    chunks = hidden // chunk // share
    units = chunks * chunk

    def column(e, q, p):
        return (e, 0, q * share + p[0])

    def flat(e, q, p):
        return (0, e * chunks + q)

    return pl.pallas_call(
        prepare_kernel,
        out_shape=(
            jax.ShapeDtypeStruct((experts, 2, chunks, chunk, width), BF16),
            jax.ShapeDtypeStruct((width, experts * units), BF16),
            jax.ShapeDtypeStruct((width, experts * units), BF16),
            jax.ShapeDtypeStruct((experts * units, width), BF16),
            jax.ShapeDtypeStruct((width, experts * units), BF16),
        ),
        grid_spec=pltpu.PrefetchScalarGridSpec(
            num_scalar_prefetch=1,
            grid=(experts, chunks),
            in_specs=[
                pl.BlockSpec((1, width, chunk), column),
                pl.BlockSpec((1, width, chunk), column),
                pl.BlockSpec((1, chunk, width), lambda e, q, p: (e, q * share + p[0], 0)),
            ],
            out_specs=(
                pl.BlockSpec((1, 2, 1, chunk, width), lambda e, q, p: (e, 0, q, 0, 0)),
                pl.BlockSpec((width, chunk), flat),
                pl.BlockSpec((width, chunk), flat),
                pl.BlockSpec((chunk, width), lambda e, q, p: (e * chunks + q, 0)),
                pl.BlockSpec((width, chunk), flat),
            ),
        ),
        compiler_params=pltpu.CompilerParams(vmem_limit_bytes=32 << 20),
        cost_estimate=pl.CostEstimate(
            flops=0, transcendentals=0, bytes_accessed=18 * experts * width * units
        ),
        name="prepare_weights",
    )(parity.reshape(1), w_gate, w_up, w_down)


def experts_kernel(
    experts,
    e_ref,
    rows_ref,
    cot_ref,
    chosen_ref,
    kept_ref,
    router_ref,
    in_t_ref,
    gate_w_ref,
    up_w_ref,
    down_ref,
    down_t_ref,
    message_ref,
    back_ref,
    gates_ref,
    act_ref,
    dgate_ref,
    dup_ref,
    kept_gates_ref,
    grads_ref,
):
    width, count = rows_ref.shape
    units = down_ref.shape[0] // experts
    first = e_ref[0] * experts
    chosen = chosen_ref[...] > 0
    logits = jnp.dot(router_ref[...], rows_ref[...], preferred_element_type=F32)
    logits = jnp.where(chosen, logits, NEG_LARGE)
    gates = jnp.exp(logits - jnp.max(logits, 0, keepdims=True))
    gates = jnp.where(chosen, gates, 0.0)
    gates = gates / jnp.sum(gates, 0, keepdims=True)
    gates_ref[...] = gates
    kept_gates_ref[...] = gates * kept_ref[...]
    grads_ref[...] = jnp.zeros_like(grads_ref)

    def one(e, carry):
        both = pl.ds(pl.multiple_of(e * 2 * units, 2 * units), 2 * units)
        mine = pl.ds(pl.multiple_of(e * units, units), units)
        acts = jnp.dot(in_t_ref[both, :], rows_ref[...], preferred_element_type=F32)
        gate, up = acts[:units], acts[units:]
        grad = jnp.dot(down_ref[mine, :], cot_ref[...], preferred_element_type=F32)
        scale = kept_gates_ref[pl.ds(first + e, 1), :]
        keep = kept_ref[pl.ds(first + e, 1), :]
        sigmoid = jax.nn.sigmoid(gate)
        silu = gate * sigmoid
        hidden = silu * up
        grads_ref[pl.ds(first + e, 1), :] = keep * jnp.sum(hidden * grad, 0, keepdims=True)
        act_ref[mine, :] = (hidden * scale).astype(BF16)
        grad = grad * scale
        dup_ref[mine, :] = (grad * silu).astype(BF16)
        dgate_ref[mine, :] = (grad * up * sigmoid * (1.0 + gate * (1.0 - sigmoid))).astype(BF16)
        return carry

    lax.fori_loop(0, experts, one, 0)
    half = width // 2

    def out(i, carry):
        rows = pl.ds(pl.multiple_of(i * half, half), half)
        message_ref[0, rows, :] = jnp.dot(
            down_t_ref[rows, :], act_ref[...], preferred_element_type=F32
        ).astype(BF16)
        back = jnp.dot(gate_w_ref[rows, :], dgate_ref[...], preferred_element_type=F32)
        back = back + jnp.dot(up_w_ref[rows, :], dup_ref[...], preferred_element_type=F32)
        back_ref[0, rows, :] = back.astype(BF16)
        return carry

    lax.fori_loop(0, 2, out, 0)
    grads = grads_ref[...]
    lanes = grads.shape[0]
    high = grads.astype(BF16)
    message_ref[0, width : width + lanes, :] = high
    message_ref[0, width + lanes :, :] = (grads - high.astype(F32)).astype(BF16)


def run_experts(expert_index, experts, count, rows, cots, chosen, kept, router_t, weights):
    in_t, gate_w, up_w, down, down_t = weights
    width, tokens = rows.shape
    blocks = tokens // count
    lanes = router_t.shape[0]
    held = down.shape[0]
    in_t = in_t.reshape(2 * held, width)

    def whole(array):
        return pl.BlockSpec(
            array.shape, lambda b, e: (0, 0), pipeline_mode=pl.Buffered(buffer_count=1)
        )

    def part(height):
        return pl.BlockSpec((height, count), lambda b, e: (0, b))

    return pl.pallas_call(
        functools.partial(experts_kernel, experts),
        out_shape=(
            jax.ShapeDtypeStruct((blocks, width + 2 * lanes, count), BF16),
            jax.ShapeDtypeStruct((blocks, width, count), BF16),
            jax.ShapeDtypeStruct((lanes, tokens), F32),
            jax.ShapeDtypeStruct((held, tokens), BF16),
            jax.ShapeDtypeStruct((held, tokens), BF16),
            jax.ShapeDtypeStruct((held, tokens), BF16),
        ),
        grid_spec=pltpu.PrefetchScalarGridSpec(
            num_scalar_prefetch=1,
            grid=(blocks,),
            in_specs=[
                part(width),
                part(width),
                part(lanes),
                part(lanes),
                whole(router_t),
                whole(in_t),
                whole(gate_w),
                whole(up_w),
                whole(down),
                whole(down_t),
            ],
            out_specs=(
                pl.BlockSpec((1, width + 2 * lanes, count), lambda b, e: (b, 0, 0)),
                pl.BlockSpec((1, width, count), lambda b, e: (b, 0, 0)),
                part(lanes),
                part(held),
                part(held),
                part(held),
            ),
            scratch_shapes=[pltpu.VMEM((lanes, count), F32)] * 2,
        ),
        compiler_params=pltpu.CompilerParams(vmem_limit_bytes=56 << 20),
        cost_estimate=pl.CostEstimate(
            flops=12 * width * held * tokens,
            transcendentals=held * tokens,
            bytes_accessed=12 * width * held + 8 * width * tokens,
        ),
        name="experts",
    )(
        expert_index.reshape(1),
        rows,
        cots,
        chosen,
        kept,
        router_t,
        in_t,
        gate_w,
        up_w,
        down,
        down_t,
    )


def down_grad_kernel(act_ref, cot_ref, out_ref):
    owners, chunks, _, size, _ = out_ref.shape
    grad = mm(act_ref[...], cot_ref[...], 1, 1).astype(BF16)
    for q in range(chunks):
        for d in range(owners):
            at = (q * owners + d) * size
            out_ref[d, q, 0] = grad[at : at + size]


def down_grads(act, cots, experts, width, chunks, owners):
    held, tokens = act.shape
    units = held // experts
    size = units // chunks // owners
    return pl.pallas_call(
        down_grad_kernel,
        out_shape=jax.ShapeDtypeStruct((owners, chunks, experts, size, width), BF16),
        grid=(experts,),
        in_specs=[
            pl.BlockSpec((units, tokens), lambda e: (e, 0)),
            pl.BlockSpec(
                (width, tokens), lambda e: (0, 0), pipeline_mode=pl.Buffered(buffer_count=1)
            ),
        ],
        out_specs=pl.BlockSpec(
            (owners, chunks, 1, size, width), lambda e: (0, 0, e, 0, 0)
        ),
        compiler_params=pltpu.CompilerParams(vmem_limit_bytes=40 << 20),
        cost_estimate=pl.CostEstimate(
            flops=2 * width * held * tokens,
            transcendentals=0,
            bytes_accessed=2 * (held + width) * tokens + 2 * held * width,
        ),
        name="down_grads",
    )(act, cots)


def in_grad_kernel(rows_ref, act_ref, out_ref):
    owners, chunks, _, share, size, _ = out_ref.shape
    for k in range(chunks):
        for q in range(share):
            for d in range(owners):
                at = ((k * share + q) * owners + d) * size
                out_ref[d, k, 0, q] = mm(rows_ref[at : at + size, :], act_ref[...], 1, 1).astype(
                    BF16
                )


def in_grads(rows, grad_act, experts, chunks, share, owners):
    held, tokens = grad_act.shape
    width = rows.shape[0]
    units = held // experts
    size = width // chunks // share // owners
    return pl.pallas_call(
        in_grad_kernel,
        out_shape=jax.ShapeDtypeStruct((owners, chunks, experts, share, size, units), BF16),
        grid=(experts,),
        in_specs=[
            pl.BlockSpec(
                (width, tokens), lambda e: (0, 0), pipeline_mode=pl.Buffered(buffer_count=1)
            ),
            pl.BlockSpec((units, tokens), lambda e: (e, 0)),
        ],
        out_specs=pl.BlockSpec(
            (owners, chunks, 1, share, size, units), lambda e: (0, 0, e, 0, 0, 0)
        ),
        compiler_params=pltpu.CompilerParams(vmem_limit_bytes=40 << 20),
        cost_estimate=pl.CostEstimate(
            flops=2 * width * held * tokens,
            transcendentals=0,
            bytes_accessed=2 * (held + width) * tokens + 2 * held * width,
        ),
        name="in_grads",
    )(rows, grad_act)


def body(
    tokens,
    routes,
    cotangent,
    norm_attn,
    w_query,
    w_key,
    w_value,
    w_out,
    norm_ffn,
    w_router,
    w_gate,
    w_up,
    w_down,
):
    comm = Comm()
    count, width = tokens.shape[1], tokens.shape[2]
    top_k = routes.shape[2]
    experts, _, hidden_units = w_gate.shape
    all_experts = experts * comm.n_expert
    capacity = (9 * count * top_k + 8 * all_experts - 1) // (8 * all_experts)
    n_context, n_dp, share = comm.n_context, comm.n_dp, comm.share
    expert_index = lax.axis_index("expert")
    context_index = lax.axis_index("context")
    dp_index = lax.axis_index("dp")
    parity = context_index % share
    chunks = n_context // share
    lanes = -(-all_experts // 32) * 32

    hidden = tokens[0].T.astype(F32)
    gain_attn = norm_attn.astype(F32)[:, None]
    gain_ffn = norm_ffn.astype(F32)[:, None]
    scale_attn = rms_scale(hidden)
    normed_attn = (hidden * scale_attn * gain_attn).astype(BF16)
    positions = context_index * count + jnp.arange(count, dtype=jnp.int32)
    cosine, sine = rope_tables(positions)
    key_t = rotate_t(mm(w_key, normed_attn, 0, 0), cosine, sine).astype(BF16)
    value_t = mm(w_value, normed_attn, 0, 0).astype(BF16)
    kv_own = jnp.concatenate([key_t, value_t], 0)
    kv_blocks = [kv_own]
    for s in range(1, n_context):
        pairs = [(i, i + s) for i in range(n_context - s)]
        kv_blocks.append(lax.ppermute(kv_own, "context", pairs))
    query_t = rotate_t(mm(w_query, normed_attn, 0, 0), cosine, sine)
    query_t = (query_t * HEAD_DIM**-0.5).astype(BF16)

    cot_t = cotangent[0].T
    routed = (
        routes[0].T[:, None, :] == jnp.arange(lanes, dtype=jnp.int32)[None, :, None]
    ).astype(F32)
    cots_all = comm.gather_group(jnp.concatenate([cot_t, routed.sum(0).astype(BF16)]))
    routed_all = cots_all[width:]
    n_tokens = routed_all.shape[1]
    before = jnp.triu(jnp.ones((count, count), BF16), 1)
    ranking = mm(routed_all.reshape(-1, count), before, 1, 0).reshape(lanes, n_tokens)
    chosen = routed_all.astype(F32)
    kept = jnp.where(ranking < capacity, chosen, 0.0)
    weights = prepare_weights(parity, w_gate, w_up, w_down, hidden_units // n_context, share)
    router_t = jnp.zeros((lanes, width), BF16).at[:all_experts].set(w_router.T)

    out_t, out_low, lse = attention_forward(context_index, query_t, kv_blocks)
    middle = hidden + mm(w_out, out_low, 0, 0)
    scale_ffn = rms_scale(middle)
    normed_ffn = (middle * scale_ffn * gain_ffn).astype(BF16)

    def rows_of(array):
        size = array.shape[0] // comm.n_expert
        blocks = []
        for j in range(comm.cores):
            for k in range(comm.columns):
                column, core = expert_index // comm.cores, expert_index % comm.cores
                column = (column - k) % comm.columns
                target = column * comm.cores + (core + j) % comm.cores
                piece = lax.dynamic_slice_in_dim(array, target * size, size, 0)
                blocks.append(piece if (j, k) == (0, 0) else comm.pull(piece, k, j))
        return jnp.concatenate(blocks, 1)

    h1_rows = rows_of(normed_attn)
    ob_rows = rows_of(out_low)

    rows_all = comm.gather_group(normed_ffn)
    message, back, gates_all, act, grad_gate, grad_up = run_experts(
        expert_index, experts, count, rows_all, cots_all, chosen, kept, router_t, weights
    )
    near = comm.return_near(message)
    near_back = comm.return_near(back)
    down_parts = comm.scatter_dp(down_grads(act, cots_all, experts, width, chunks, n_dp))
    gate_parts = comm.scatter_dp(in_grads(rows_all, grad_gate, experts, chunks, share, n_dp))
    up_parts = comm.scatter_dp(in_grads(rows_all, grad_up, experts, chunks, share, n_dp))
    returned = comm.return_far(near)
    grad_normed_ffn = comm.return_far(near_back)
    result = (middle + returned[:width]).astype(BF16)
    grad_gates = returned[width : width + lanes] + returned[width + lanes :]
    gates_own = gates_all[:, :count]

    upstream = cot_t.astype(F32)
    mean_grad = jnp.sum(gates_own * grad_gates, 0, keepdims=True)
    grad_logits = (gates_own * (grad_gates - mean_grad)).astype(BF16)
    grad_normed_ffn = grad_normed_ffn + mm(router_t, grad_logits, 0, 0)
    grad_gain_ffn = jnp.sum(grad_normed_ffn * middle * scale_ffn, 1)
    grad_middle = upstream + norm_back(grad_normed_ffn, middle, scale_ffn, gain_ffn)
    grad_branch = grad_middle.astype(BF16)

    grad_attn_t = mm(w_out, grad_branch, 1, 0).astype(BF16)
    grad_query_t, grad_kv = attention_backward(
        context_index, query_t, grad_attn_t, out_t, lse, kv_blocks
    )
    kv_width = KV_HEADS * HEAD_DIM
    kv_sum = grad_kv[0].astype(F32)
    for s in range(1, n_context):
        pairs = [(i, i - s) for i in range(s, n_context)]
        kv_sum = kv_sum + lax.ppermute(grad_kv[s], "context", pairs).astype(F32)
    grad_query_raw = rotate_t(grad_query_t, cosine, -sine).astype(BF16)
    grad_key_raw = rotate_t(kv_sum[0], cosine, -sine).astype(BF16)
    grad_value_raw = kv_sum[1].astype(BF16)
    grad_kv_raw = jnp.concatenate([grad_key_raw, grad_value_raw], 0)

    def finish_in(parts):
        total = comm.scatter_context(parts, share)
        if share == 1:
            return total[:, 0]
        keep = lax.dynamic_index_in_dim(total, parity, 1, False)
        send = lax.dynamic_index_in_dim(total, 1 - parity, 1, False)
        other = comm.pair(send.astype(BF16)).astype(F32)
        first = jnp.where(parity == 0, keep, other)
        second = jnp.where(parity == 0, other, keep)
        size = hidden_units // n_context
        pieces = []
        for q in range(chunks):
            pieces += [x[..., q * size : (q + 1) * size] for x in (first, second)]
        return jnp.concatenate(pieces, -1)

    down_sum = comm.scatter_context(down_parts, share)
    gate_sum = finish_in(gate_parts)
    up_sum = finish_in(up_parts)

    def reduce_rows(local):
        parts = local.reshape(n_context, n_dp, -1, local.shape[1])
        total = comm.scatter_dp(jnp.moveaxis(parts, 1, 0))
        return comm.scatter_context(total, 1)

    branch_all = comm.gather_expert(jnp.concatenate([grad_branch, grad_logits]))
    row_count = width // comm.n_expert
    gain_total = grad_gain_ffn.reshape(-1, LANES)
    if comm.cores == 2:
        gain_total = gain_total + comm.pull(gain_total, 0, 1)
    gain_total = sum([comm.pull(gain_total, k, 0) for k in range(1, comm.columns)], gain_total)
    gain_rows = lax.dynamic_slice_in_dim(
        gain_total.reshape(width), expert_index * row_count, row_count, 0
    )
    out_rows = mm(ob_rows, branch_all[:width], 1, 1)
    h2_rows = lax.dynamic_slice_in_dim(rows_all, expert_index * row_count, row_count, 0)
    h2_rows = h2_rows.reshape(row_count, comm.cores, share, comm.columns * count)[:, :, 0]
    router_rows = mm(h2_rows.reshape(row_count, -1), branch_all[width:], 1, 1)
    rest = jnp.zeros((row_count, LANES - lanes - 1), F32)
    first_sum = reduce_rows(
        jnp.concatenate([out_rows, router_rows, gain_rows[:, None], rest], 1)
    )

    def projection_rows(grad_t):
        return reduce_rows(mm(h1_rows, comm.gather_expert(grad_t), 1, 1))

    query_sum = projection_rows(grad_query_raw)
    kv_rows = projection_rows(grad_kv_raw)
    key_sum, value_sum = kv_rows[:, :kv_width], kv_rows[:, kv_width:]

    shard = (expert_index * n_context + context_index) * n_dp + dp_index
    shard_rows = query_sum.shape[0]

    def shard_of(array):
        return lax.dynamic_slice_in_dim(array, shard * shard_rows, shard_rows, 0).astype(F32)

    gain_sum = (
        jnp.sum(shard_of(w_query) * query_sum, 1)
        + jnp.sum(shard_of(w_key) * key_sum, 1)
        + jnp.sum(shard_of(w_value) * value_sum, 1)
    ) / shard_of(norm_attn)

    grad_normed_attn = mm(w_query, grad_query_raw, 1, 0)
    grad_normed_attn = grad_normed_attn + mm(w_key, grad_key_raw, 1, 0)
    grad_normed_attn = grad_normed_attn + mm(w_value, grad_value_raw, 1, 0)
    grad_hidden = grad_middle + norm_back(grad_normed_attn, hidden, scale_attn, gain_attn)
    return (
        result.T[None],
        grad_hidden.astype(BF16).T[None],
        gain_sum,
        query_sum,
        key_sum,
        value_sum,
        first_sum[:, :width],
        first_sum[:, width + lanes],
        first_sum[:, width : width + all_experts],
        gate_sum,
        up_sum,
        down_sum,
    )


def solution(mesh):
    rows = P(("expert", "dp"), "context", None)
    dense = P(("expert", "context", "dp"), None)
    vector = P(("expert", "context", "dp"))
    experts = P("expert", None, None)
    expert_grads = P("expert", ("context", "dp"), None)
    return jax.shard_map(
        body,
        mesh=mesh,
        in_specs=(rows, rows, rows) + (P(),) * 7 + (experts,) * 3,
        out_specs=(rows, rows, vector, dense, dense, dense, dense, vector, dense)
        + (expert_grads,) * 3,
        check_vma=False,
    )
```

```python
import functools

import jax
import jax.numpy as jnp
from jax import lax
from jax.experimental import pallas as pl
from jax.experimental.pallas import tpu as pltpu
from jax.sharding import PartitionSpec as P

HEADS = 24
KV_HEADS = 8
HEAD_DIM = 64
GROUP = HEADS // KV_HEADS


EPS = 1e-05
ROPE_BASE = 10000.0
NEG_LARGE = -1e30
F32 = jnp.float32
BF16 = jnp.bfloat16
LANES = 128


def cost(flops, bytes_accessed, transcendentals=0):
    scale = 64
    return pl.CostEstimate(
        flops=flops // scale,
        bytes_accessed=bytes_accessed // scale,
        transcendentals=transcendentals // scale,
    )


def rms_scale(values):
    return lax.rsqrt(jnp.mean(values * values, 0, keepdims=True) + EPS)


def norm_back(grad_out, values, scale, gain):
    weighted = gain * grad_out
    return scale * weighted - values * scale**3 * jnp.mean(weighted * values, 0, keepdims=True)


def mm(a, b, da, db):
    return lax.dot_general(a, b, (((da,), (db,)), ((), ())), preferred_element_type=F32)


class Comm:
    def __init__(self):
        self.n_expert = lax.axis_size("expert")
        self.n_context = lax.axis_size("context")
        self.n_dp = lax.axis_size("dp")
        self.cores = 2 if self.n_expert % 2 == 0 else 1
        self.columns = self.n_expert // self.cores
        self.share = 2 if self.n_context % 2 == 0 else 1

    def peer(self, i, k, j):
        column, core = divmod(i, self.cores)
        return ((column + k) % self.columns) * self.cores + (core + j) % self.cores

    def pull(self, value, k, j):
        pairs = [(self.peer(i, k, j), i) for i in range(self.n_expert)]
        return lax.ppermute(value, "expert", pairs)

    def push(self, value, k, j):
        pairs = [(i, self.peer(i, k, j)) for i in range(self.n_expert)]
        return lax.ppermute(value, "expert", pairs)

    def pair(self, value):
        return lax.ppermute(value, "context", [(i, i ^ 1) for i in range(self.n_context)])

    def from_core(self, blocks):
        arrays = [array for block in blocks for _, array, _ in block]
        moved = self.pull(jnp.concatenate(arrays) if len(arrays) > 1 else arrays[0], 0, 1)
        out, at = [], 0
        for block in blocks:
            pieces = []
            for row, array, _ in block:
                pieces.append((row, moved, at))
                at += array.shape[0]
            out.append(pieces)
        return out

    def gather_columns(self, value):
        return [value] + [self.pull(value, k, 0) for k in range(1, self.columns)]

    def gather_cores(self, near):
        if self.cores == 2:
            near = near + [self.pull(block, 0, 1) for block in near]
        return near

    def gather_expert(self, value):
        return self.gather_cores(self.gather_columns(value))

    def gather_group(self, value):
        columns = [self.pull(value, k, 0) for k in range(1, self.columns)]
        first = [[(0, value, 0)]] + [[(0, block, 0)] for block in columns]
        far = []
        if self.share == 2:
            half = value.shape[0] // 2
            across = self.pair(value)
            first.append([(0, across, 0)])
            for k in range(1, self.columns):
                top = self.pull(across[:half], k, 0)
                bottom = self.pair(columns[k - 1][half:])
                far.append([(0, top, 0), (half, bottom, 0)])
        blocks = first + far
        if self.cores == 2:
            blocks = blocks + self.from_core(first)
            blocks = blocks + (self.from_core(far) if far else [])
        return blocks

    def return_hops(self, near, other):
        columns = self.columns
        shape = (self.share, columns) + near.shape[1:]
        arrays = [x.reshape(shape) for x in (near, other) if x is not None]

        def part(*at):
            return sum(array[at].astype(F32) for array in arrays)

        if self.share == 1:
            sent = [self.push(part(0, k).astype(BF16), k, 0) for k in range(1, columns)]
            return [part(0, 0)] + sent
        half = near.shape[1] // 2
        low, high = slice(0, half), slice(half, 2 * half)
        every = slice(None)
        by_column = [
            self.push(part(every, k, low).astype(BF16), k, 0) for k in range(1, columns)
        ]
        by_pair = self.pair(part(1, every, high).astype(BF16))
        return [part(every, 0, low)] + by_column + [part(0, every, high), by_pair]

    def return_last(self, terms):
        columns = self.columns
        if self.share == 1:
            return sum(term.astype(F32) for term in terms)
        top = terms[:columns]
        bottom = terms[columns : columns + 2]

        def total(parts, at):
            return sum(part[at].astype(F32) for part in parts)

        top_other = self.pair(total(top, 1).astype(BF16))
        others = [
            self.push(total(bottom, k).astype(BF16), k, 0).astype(F32)
            for k in range(1, columns)
        ]
        return jnp.concatenate(
            [total(top, 0) + top_other.astype(F32), sum(others, total(bottom, 0))]
        )

    def send_dp(self, parts):
        n = self.n_dp
        return [
            lax.ppermute(parts[s - 1], "dp", [(i, (i + s) % n) for i in range(n)])
            for s in range(1, n)
        ]

    def send_context(self, parts, stride):
        n = self.n_context // stride
        out = []
        for s in range(1, n):
            pairs = []
            for i in range(self.n_context):
                k, r = divmod(i, stride)
                pairs.append((i, ((k + s) % n) * stride + r))
            out.append(lax.ppermute(parts[s - 1], "context", pairs))
        return out

    def scatter_rows(self, left, right, width):
        n, m = self.n_context, self.n_dp
        c, d = lax.axis_index("context"), lax.axis_index("dp")
        size = left[0].shape[0] // (n * m)
        if size % 16 == 0:
            mine, *parts = row_products(jnp.stack([c, d]), left, right, width, n, m)
        else:
            local = sum(mm(a, b[:width], 1, 1) for a, b in zip(left, right))
            local = local.reshape(n, m, size, width)
            local = jnp.stack(
                [lax.dynamic_index_in_dim(local, (c + k) % n, 0, False) for k in range(n)]
            )
            mine, *parts = [
                lax.dynamic_index_in_dim(local, (d + s) % m, 1, False) for s in range(m)
            ]
        came = self.send_dp([part.astype(BF16) for part in parts])

        def of_context(k):
            return mine[k].astype(F32) + sum(x[k].astype(F32) for x in came)

        came_far = self.send_context([of_context(k).astype(BF16) for k in range(1, n)], 1)
        return of_context(0) + sum(x.astype(F32) for x in came_far)


def row_products_kernel(count, place_ref, *refs):
    left, right, outs, total_s = refs[:count], refs[count : 2 * count], refs[2 * count : -1], refs[-1]
    width = total_s.shape[1]
    total = mm(left[0][...], right[0][:width, :], 1, 1)
    for a, b in zip(left[1:], right[1:]):
        total = total + mm(a[...], b[:width, :], 1, 1)
    total_s[...] = total
    n, size, _ = outs[0].shape
    m = len(outs)
    for k in range(n):
        for s in range(m):
            owner = lax.rem(place_ref[0] + k, n) * m + lax.rem(place_ref[1] + s, m)
            rows = pl.ds(pl.multiple_of(owner * size, size), size)
            outs[s][k] = total_s[rows, :].astype(outs[s].dtype)


def row_products(place, left, right, width, n, m):
    rows = left[0].shape[0]
    size = rows // (n * m)

    def whole(shape):
        return pl.BlockSpec(shape, lambda i, p: (0,) * len(shape))

    return pl.pallas_call(
        functools.partial(row_products_kernel, len(left)),
        out_shape=tuple(
            jax.ShapeDtypeStruct((n, size, width), BF16 if s else F32) for s in range(m)
        ),
        grid_spec=pltpu.PrefetchScalarGridSpec(
            num_scalar_prefetch=1,
            grid=(1,),
            in_specs=[whole(x.shape) for x in left + right],
            out_specs=tuple(whole((n, size, width)) for _ in range(m)),
            scratch_shapes=[pltpu.VMEM((rows, width), F32)],
        ),
        compiler_params=pltpu.CompilerParams(vmem_limit_bytes=32 << 20),
        cost_estimate=cost(
            flops=2 * rows * width * right[0].shape[1] * len(left),
            bytes_accessed=8 * width * right[0].shape[1] + 6 * rows * width,
        ),
        name="row_products",
    )(place, *left, *right)


def attn_fwd_kernel(blocks, c_ref, q_ref, *refs):
    k_refs, v_refs = refs[:blocks], refs[blocks : 2 * blocks]
    o_ref, ob_ref, lse_ref, scores_ref = refs[2 * blocks :]
    c = c_ref[0]
    n = q_ref.shape[1]
    hd = HEAD_DIM
    for s in range(blocks):
        rows = slice(s * n, (s + 1) * n)

        def fill(s=s, rows=rows):
            for g in range(GROUP):
                scores = mm(k_refs[s][...], q_ref[g * hd : (g + 1) * hd, :], 0, 0)
                if s == 0:
                    key = lax.broadcasted_iota(jnp.int32, scores.shape, 0)
                    query = lax.broadcasted_iota(jnp.int32, scores.shape, 1)
                    scores = jnp.where(key <= query, scores, NEG_LARGE)
                scores_ref[g, rows, :] = scores

        def blank(rows=rows):
            for g in range(GROUP):
                scores_ref[g, rows, :] = jnp.full((n, n), NEG_LARGE, F32)

        if s == 0:
            fill()
        else:
            pl.when(c >= s)(fill)
            pl.when(c < s)(blank)
    lse_ref[...] = jnp.zeros_like(lse_ref)
    for g in range(GROUP):
        scores = scores_ref[g]
        top = jnp.max(scores, 0, keepdims=True)
        weights = jnp.exp(scores - top)
        total = jnp.sum(weights, 0, keepdims=True)
        weights = weights.astype(BF16)
        out = jnp.zeros((hd, n), F32)
        for s in range(blocks):
            out = out + mm(v_refs[s][...], weights[s * n : (s + 1) * n], 1, 0)
        out = out / total
        o_ref[g * hd : (g + 1) * hd, :] = out
        ob_ref[g * hd : (g + 1) * hd, :] = out.astype(BF16)
        lse_ref[0, g : g + 1, :] = top + jnp.log(total)


def kv_specs(blocks, n, first=0):
    keys = [pl.BlockSpec((HEAD_DIM, n), lambda h, c: (first + h, 0))] * blocks
    values = [pl.BlockSpec((HEAD_DIM, n), lambda h, c: (first + h + KV_HEADS, 0))] * blocks
    return keys + values


def attention_forward(context_index, query_t, kv_blocks):
    blocks = len(kv_blocks)
    n = query_t.shape[1]
    wide = GROUP * HEAD_DIM
    heads = query_t.shape[0] // wide
    head = pl.BlockSpec((wide, n), lambda h, c: (h, 0))
    return pl.pallas_call(
        functools.partial(attn_fwd_kernel, blocks),
        out_shape=(
            jax.ShapeDtypeStruct(query_t.shape, F32),
            jax.ShapeDtypeStruct(query_t.shape, BF16),
            jax.ShapeDtypeStruct((heads, 8, n), F32),
        ),
        grid_spec=pltpu.PrefetchScalarGridSpec(
            num_scalar_prefetch=1,
            grid=(heads,),
            in_specs=[head] + kv_specs(blocks, n),
            out_specs=(head, head, pl.BlockSpec((1, 8, n), lambda h, c: (h, 0, 0))),
            scratch_shapes=[pltpu.VMEM((GROUP, blocks * n, n), F32)],
        ),
        compiler_params=pltpu.CompilerParams(vmem_limit_bytes=40 << 20),
        cost_estimate=cost(
            flops=heads * GROUP * blocks * n * n * 256 * 4,
            transcendentals=heads * GROUP * blocks * n * n,
            bytes_accessed=16 * query_t.size,
        ),
        name="attn_fwd",
    )(context_index.reshape(1), query_t, *kv_blocks, *kv_blocks)


def attn_bwd_kernel(blocks, c_ref, q_ref, do_ref, o_ref, lse_ref, *refs):
    k_refs, v_refs = refs[:blocks], refs[blocks : 2 * blocks]
    dq_ref, dkv_ref = refs[2 * blocks :]
    c = c_ref[0]
    n = q_ref.shape[1]
    hd = HEAD_DIM
    deltas = []
    for g in range(GROUP):
        head = slice(g * hd, (g + 1) * hd)
        both = do_ref[head, :].astype(F32) * o_ref[head, :]
        deltas.append(jnp.sum(both, 0, keepdims=True))
    for s in range(blocks):

        def work(s=s):
            dk = jnp.zeros((hd, n), F32)
            dv = jnp.zeros((hd, n), F32)
            key_t = k_refs[s][...]
            value_t = v_refs[s][...]
            for g in range(GROUP):
                head = slice(g * hd, (g + 1) * hd)
                query, grad = q_ref[head, :], do_ref[head, :]
                scores = mm(key_t, query, 0, 0)
                weights = jnp.exp(scores - lse_ref[0, g : g + 1, :])
                if s == 0:
                    key = lax.broadcasted_iota(jnp.int32, scores.shape, 0)
                    place = lax.broadcasted_iota(jnp.int32, scores.shape, 1)
                    weights = jnp.where(key <= place, weights, 0.0)
                grad_weights = mm(value_t, grad, 0, 0)
                grad_scores = (weights * (grad_weights - deltas[g])).astype(BF16)
                dv = dv + mm(grad, weights.astype(BF16), 1, 1)
                dk = dk + mm(query, grad_scores, 1, 1)
                step = mm(key_t, grad_scores, 1, 0) * (HEAD_DIM**-0.5)
                if s == 0:
                    dq_ref[head, :] = step
                else:
                    dq_ref[head, :] += step
            owner = lax.rem(c - s + blocks, blocks)
            dkv_ref[owner, 0] = dk.astype(BF16)
            dkv_ref[owner, 1] = dv.astype(BF16)

        def skip(s=s):
            owner = lax.rem(c - s + blocks, blocks)
            dkv_ref[owner] = jnp.zeros(dkv_ref.shape[1:], BF16)

        if s == 0:
            work()
        else:
            pl.when(c >= s)(work)
            pl.when(c < s)(skip)


def attention_backward(context_index, query_t, grad_t, out_t, lse, kv_blocks, first, heads):
    blocks = len(kv_blocks)
    n = query_t.shape[1]
    wide = GROUP * HEAD_DIM
    head = pl.BlockSpec((wide, n), lambda h, c: (first + h, 0))
    out = pl.BlockSpec((wide, n), lambda h, c: (h, 0))
    return pl.pallas_call(
        functools.partial(attn_bwd_kernel, blocks),
        out_shape=(
            jax.ShapeDtypeStruct((heads * wide, n), F32),
            jax.ShapeDtypeStruct((blocks, 2, heads * HEAD_DIM, n), BF16),
        ),
        grid_spec=pltpu.PrefetchScalarGridSpec(
            num_scalar_prefetch=1,
            grid=(heads,),
            in_specs=[head, head, head, pl.BlockSpec((1, 8, n), lambda h, c: (first + h, 0, 0))]
            + kv_specs(blocks, n, first),
            out_specs=(
                out,
                pl.BlockSpec((blocks, 2, HEAD_DIM, n), lambda h, c: (0, 0, h, 0)),
            ),
        ),
        compiler_params=pltpu.CompilerParams(vmem_limit_bytes=40 << 20),
        cost_estimate=cost(
            flops=heads * GROUP * blocks * n * n * 256 * 10,
            transcendentals=heads * GROUP * blocks * n * n,
            bytes_accessed=20 * query_t.size,
        ),
        name="attn_bwd",
    )(context_index.reshape(1), query_t, grad_t, out_t, lse, *kv_blocks, *kv_blocks)


def rope_tables(positions):
    half_dim = HEAD_DIM // 2
    frequency = ROPE_BASE ** (-2.0 * jnp.arange(half_dim, dtype=F32) / HEAD_DIM)
    angles = frequency[:, None] * positions.astype(F32)[None, :]
    return jnp.cos(angles), jnp.sin(angles)


def rotate_t(values_t, cosine, sine):
    shaped = values_t.reshape(-1, 2, HEAD_DIM // 2, values_t.shape[1])
    low, high = shaped[:, 0], shaped[:, 1]
    turned = jnp.stack([low * cosine - high * sine, high * cosine + low * sine], 1)
    return turned.reshape(values_t.shape)


def prepare_kernel(p_ref, gate_ref, up_ref, down_ref, *outs):
    in_t_ref, gate_out, up_out, down_out, down_t_out = outs
    gate, up, down = gate_ref[0], up_ref[0], down_ref[0]
    in_t_ref[0, 0, 0] = gate.astype(F32).T.astype(BF16)
    in_t_ref[0, 1, 0] = up.astype(F32).T.astype(BF16)
    gate_out[...] = gate
    up_out[...] = up
    down_out[...] = down
    down_t_out[...] = down.astype(F32).T.astype(BF16)


def prepare_weights(parity, w_gate, w_up, w_down, chunk, share):
    experts, width, hidden = w_gate.shape
    chunks = hidden // chunk // share
    units = chunks * chunk

    def column(e, q, p):
        return (e, 0, q * share + p[0])

    def flat(e, q, p):
        return (0, e * chunks + q)

    return pl.pallas_call(
        prepare_kernel,
        out_shape=(
            jax.ShapeDtypeStruct((experts, 2, chunks, chunk, width), BF16),
            jax.ShapeDtypeStruct((width, experts * units), BF16),
            jax.ShapeDtypeStruct((width, experts * units), BF16),
            jax.ShapeDtypeStruct((experts * units, width), BF16),
            jax.ShapeDtypeStruct((width, experts * units), BF16),
        ),
        grid_spec=pltpu.PrefetchScalarGridSpec(
            num_scalar_prefetch=1,
            grid=(experts, chunks),
            in_specs=[
                pl.BlockSpec((1, width, chunk), column),
                pl.BlockSpec((1, width, chunk), column),
                pl.BlockSpec((1, chunk, width), lambda e, q, p: (e, q * share + p[0], 0)),
            ],
            out_specs=(
                pl.BlockSpec((1, 2, 1, chunk, width), lambda e, q, p: (e, 0, q, 0, 0)),
                pl.BlockSpec((width, chunk), flat),
                pl.BlockSpec((width, chunk), flat),
                pl.BlockSpec((chunk, width), lambda e, q, p: (e * chunks + q, 0)),
                pl.BlockSpec((width, chunk), flat),
            ),
        ),
        compiler_params=pltpu.CompilerParams(vmem_limit_bytes=60 << 20),
        cost_estimate=cost(
            flops=0, transcendentals=0, bytes_accessed=18 * experts * width * units
        ),
        name="prepare_weights",
    )(parity.reshape(1), w_gate, w_up, w_down)


def piece_copies(blocks, refs, target_ref, sems):
    out, at = [], 0
    count = refs[0].shape[1]
    for b, pieces in enumerate(blocks):
        copies = []
        for i, (first, ref, row) in enumerate(pieces):
            last = pieces[i + 1][0] if i + 1 < len(pieces) else target_ref.shape[0]
            copies.append(
                pltpu.make_async_copy(
                    refs[ref].at[row : row + last - first],
                    target_ref.at[first:last, b * count : (b + 1) * count],
                    sems.at[at],
                )
            )
            at += 1
        out.append(copies)
    return out


def write_grads(rows_ref, cots_ref, act, dgate, dup, place_ref, outs, down_s, in_s, share):
    owners = len(outs)
    chunks, _, _, units = outs[0].shape
    width = rows_ref.shape[0]
    size = units // chunks // owners
    tiles = width // units

    def place(k, s):
        return lax.rem(place_ref[2] + k, chunks), lax.rem(place_ref[1] + s, owners)

    down_s[...] = mm(act, cots_ref[...], 1, 1).astype(BF16)
    for k in range(chunks):
        for s in range(owners):
            at_k, at_d = place(k, s)
            start = pl.multiple_of((at_k * owners + at_d) * size, size)
            for t in range(tiles):
                outs[s][k, 0, t * size : (t + 1) * size, :] = down_s[
                    pl.ds(start, size), t * units : (t + 1) * units
                ]
    base = tiles * size
    size = width // (chunks * share * owners)
    for grad_act in (dgate, dup):
        in_s[...] = mm(rows_ref[...], grad_act, 1, 1).astype(BF16)
        for k in range(chunks):
            for q in range(share):
                for s in range(owners):
                    at_k, at_d = place(k, s)
                    start = pl.multiple_of(((at_k * share + q) * owners + at_d) * size, size)
                    to = base + q * size
                    outs[s][k, 0, to : to + size, :] = in_s[pl.ds(start, size), :]
        base += share * size


class Experts:
    def __init__(self, rows, cots, width, units, share, chunks, owners):
        self.arrays, self.plans = [], []
        for blocks in (rows, cots):
            arrays, plan = [], []
            for block in blocks:
                pieces = []
                for first, array, row in block:
                    known = [i for i, x in enumerate(arrays) if x is array]
                    if not known:
                        arrays.append(array)
                    pieces.append((first, known[0] if known else len(arrays) - 1, row))
                plan.append(pieces)
            self.arrays.append(arrays)
            self.plans.append(plan)
        self.blocks = len(rows)
        self.width, self.count = width, rows[0][0][1].shape[1]
        self.tokens = self.blocks * self.count
        self.units, self.share, self.chunks, self.owners = units, share, chunks, owners
        self.height = self.width // chunks // owners * 3

    def n_arrays(self):
        return sum(map(len, self.arrays))

    def scratch(self):
        wide = pltpu.VMEM((self.width, self.tokens), BF16)
        sems = [pltpu.SemaphoreType.DMA((sum(map(len, plan)),)) for plan in self.plans]
        return [wide, wide] + sems

    def copies(self, refs, rows_ref, cots_ref, row_sems, cot_sems):
        n = len(self.arrays[0])
        row_copies = piece_copies(self.plans[0], refs[:n], rows_ref, row_sems)
        cot_copies = piece_copies(self.plans[1], refs[n:], cots_ref, cot_sems)
        return [a + b for a, b in zip(row_copies, cot_copies)]

    def grads_structs(self, n):
        shape = (self.chunks, n, self.height, self.units)
        spec = pl.BlockSpec(
            (self.chunks, 1, self.height, self.units), lambda i, *_: (0, i, 0, 0)
        )
        return [jax.ShapeDtypeStruct(shape, BF16)] * self.owners, [spec] * self.owners

    def act_kernel(self, first, n, make_gates, e_ref, *refs):
        n_arrays = self.n_arrays()
        kept_ref, scales_ref, in_t_ref, down_ref = refs[:4]
        piece_refs, outs, scratch = refs[4 : 4 + n_arrays], refs[4 + n_arrays : -6], refs[-6:]
        if make_gates:
            chosen_ref = scales_ref
            gates_ref, scales_ref = outs[:2]
            outs = outs[2:]
        act_ref, dgate_ref, dup_ref, dscale_ref = outs[:4]
        rows_ref, cots_ref = scratch[:2]
        units, count, blocks = self.units, self.count, self.blocks
        copies = self.copies(piece_refs, *scratch[:4])
        step = pl.program_id(0)
        row = e_ref[0] + first + step

        def move(wait, start):
            def run():
                for b in start:
                    for copy in copies[b] if b < blocks else ():
                        copy.start()
                for copy in copies[wait]:
                    copy.wait()

            if n == 1:
                run()
            else:
                pl.when(step == 0)(run)

        def products(b):
            move(b, (0, 1, 2) if b == 0 else (b + 2,))
            cols = slice(b * count, (b + 1) * count)
            acts = jnp.dot(in_t_ref[...], rows_ref[:, cols], preferred_element_type=F32)
            grad = jnp.dot(down_ref[...], cots_ref[:, cols], preferred_element_type=F32)
            return acts, grad

        def finish(b, acts, grad):
            cols = slice(b * count, (b + 1) * count)
            gate, up = acts[:units], acts[units : 2 * units]
            if make_gates:
                chosen = chosen_ref[:, cols] > 0
                logits = jnp.where(chosen, acts[2 * units :], NEG_LARGE)
                gates = jnp.exp(logits - jnp.max(logits, 0, keepdims=True))
                gates = jnp.where(chosen, gates, 0.0)
                gates = gates / jnp.sum(gates, 0, keepdims=True)
                gates_ref[:, cols] = gates
                scales_ref[:, cols] = gates * kept_ref[:, cols]
            scale = scales_ref[pl.ds(row, 1), cols]
            keep = kept_ref[pl.ds(row, 1), cols]
            sigmoid = jax.nn.sigmoid(gate)
            silu = gate * sigmoid
            hidden = silu * up
            dscale_ref[0, 0:1, cols] = keep * jnp.sum(hidden * grad, 0, keepdims=True)
            act_ref[:, cols] = (hidden * scale).astype(BF16)
            grad = grad * scale
            dup_ref[:, cols] = (grad * silu).astype(BF16)
            dgate_ref[:, cols] = (grad * up * (sigmoid + silu * (1.0 - sigmoid))).astype(BF16)

        dscale_ref[...] = jnp.zeros_like(dscale_ref)
        ready = products(0)
        for b in range(blocks):
            done = ready
            if b + 1 < blocks:
                ready = products(b + 1)
            finish(b, *done)
        write_grads(
            rows_ref,
            cots_ref,
            act_ref[...],
            dgate_ref[...],
            dup_ref[...],
            e_ref,
            outs[4:],
            *scratch[4:],
            self.share,
        )

    def act(self, places, first, n, kept, scales, in_t, down, make_gates=False):
        units, width, tokens = self.units, self.width, self.tokens
        lanes = kept.shape[0]
        in_rows = 2 * units + (lanes if make_gates else 0)
        table = pl.BlockSpec((lanes, tokens), lambda i, e: (0, 0))
        one = pl.BlockSpec((units, tokens), lambda i, e: (i, 0))
        outs, specs = [], []
        if make_gates:
            outs += [jax.ShapeDtypeStruct((lanes, tokens), F32)] * 2
            specs += [table] * 2
        outs += [jax.ShapeDtypeStruct((n * units, tokens), BF16)] * 3
        specs += [one] * 3
        outs.append(jax.ShapeDtypeStruct((n, 8, tokens), F32))
        specs.append(pl.BlockSpec((1, 8, tokens), lambda i, e: (i, 0, 0)))
        structs, grad_specs = self.grads_structs(n)
        extra = [pltpu.VMEM((units, width), BF16), pltpu.VMEM((width, units), BF16)]
        return pl.pallas_call(
            functools.partial(self.act_kernel, first, n, make_gates),
            out_shape=tuple(outs + structs),
            grid_spec=pltpu.PrefetchScalarGridSpec(
                num_scalar_prefetch=1,
                grid=(n,),
                in_specs=[
                    table,
                    table,
                    pl.BlockSpec((in_rows, width), lambda i, e: (first + i, 0)),
                    pl.BlockSpec((units, width), lambda i, e: (first + i, 0)),
                ]
                + [pl.BlockSpec(memory_space=pl.ANY)] * self.n_arrays(),
                out_specs=tuple(specs + grad_specs),
                scratch_shapes=self.scratch() + extra,
            ),
            compiler_params=pltpu.CompilerParams(vmem_limit_bytes=60 << 20),
            cost_estimate=cost(
                flops=12 * width * units * tokens * n,
                transcendentals=units * tokens * n,
                bytes_accessed=4 * width * tokens + 6 * n * units * (width + tokens),
            ),
            name="experts_act",
        )(places, kept, scales, in_t, down, *self.arrays[0], *self.arrays[1])

    def out_kernel(self, parts, e_ref, weight_ref, *refs):
        act_refs, dscale_refs = refs[:parts], refs[parts : 2 * parts]
        message_ref, act_s, dscale_s = refs[2 * parts :]
        at = row = 0
        dscale_s[...] = jnp.zeros_like(dscale_s)
        for act_ref, dscale_ref in zip(act_refs, dscale_refs):
            act_s[at : at + act_ref.shape[0], :] = act_ref[...]
            at += act_ref.shape[0]
            for i in range(dscale_ref.shape[0]):
                dscale_s[pl.ds(e_ref[0] + row, 1), :] = dscale_ref[i, 0:1, :]
                row += 1
        width, lanes = self.width, dscale_s.shape[0]
        message_ref[0, :width, :] = jnp.dot(
            weight_ref[...], act_s[...], preferred_element_type=F32
        ).astype(BF16)
        grads = dscale_s[...]
        high = grads.astype(BF16)
        message_ref[0, width : width + lanes, :] = high
        message_ref[0, width + lanes :, :] = (grads - high.astype(F32)).astype(BF16)

    def out(self, places, lanes, weight, acts, dscales, first_block, n_blocks):
        rows = weight.shape[1]
        parts = len(acts)
        width, count = self.width, self.count

        def column(shape):
            return pl.BlockSpec(
                shape, lambda b, e: (0,) * (len(shape) - 1) + (first_block + b,)
            )

        return pl.pallas_call(
            functools.partial(self.out_kernel, parts),
            out_shape=jax.ShapeDtypeStruct((n_blocks, width + 2 * lanes, count), BF16),
            grid_spec=pltpu.PrefetchScalarGridSpec(
                num_scalar_prefetch=1,
                grid=(n_blocks,),
                in_specs=[
                    pl.BlockSpec(
                        (width, rows),
                        lambda b, e: (0, 0),
                        pipeline_mode=pl.Buffered(buffer_count=1),
                    )
                ]
                + [column((a.shape[0], count)) for a in acts]
                + [column((a.shape[0], 8, count)) for a in dscales],
                out_specs=pl.BlockSpec((1, width + 2 * lanes, count), lambda b, e: (b, 0, 0)),
                scratch_shapes=[pltpu.VMEM((rows, count), BF16), pltpu.VMEM((lanes, count), F32)],
            ),
            compiler_params=pltpu.CompilerParams(vmem_limit_bytes=60 << 20),
            cost_estimate=cost(
                flops=2 * width * rows * count * n_blocks,
                transcendentals=0,
                bytes_accessed=2 * width * rows + 4 * width * count * n_blocks,
            ),
            name="experts_out",
        )(places, weight, *acts, *dscales)

    def back_kernel(self, parts, gate_w_ref, up_w_ref, *refs):
        dgate_refs, dup_refs = refs[:parts], refs[parts : 2 * parts]
        back_ref, dgate_s, dup_s = refs[2 * parts :]
        for target, pieces in ((dgate_s, dgate_refs), (dup_s, dup_refs)):
            at = 0
            for piece in pieces:
                target[at : at + piece.shape[0], :] = piece[...]
                at += piece.shape[0]
        back = jnp.dot(gate_w_ref[...], dgate_s[...], preferred_element_type=F32)
        back = back + jnp.dot(up_w_ref[...], dup_s[...], preferred_element_type=F32)
        back_ref[0] = back.astype(BF16)

    def back(self, gate_w, up_w, dgates, dups, first_block, n_blocks):
        width, count = self.width, self.count
        rows = gate_w.shape[1]
        parts = len(dgates)
        whole = pl.BlockSpec(
            (width, rows), lambda b: (0, 0), pipeline_mode=pl.Buffered(buffer_count=1)
        )
        column = [pl.BlockSpec((a.shape[0], count), lambda b: (0, first_block + b)) for a in dgates]
        return pl.pallas_call(
            functools.partial(self.back_kernel, parts),
            out_shape=jax.ShapeDtypeStruct((n_blocks, width, count), BF16),
            grid=(n_blocks,),
            in_specs=[whole, whole] + column * 2,
            out_specs=pl.BlockSpec((1, width, count), lambda b: (b, 0, 0)),
            scratch_shapes=[pltpu.VMEM((rows, count), BF16)] * 2,
            compiler_params=pltpu.CompilerParams(vmem_limit_bytes=60 << 20),
            cost_estimate=cost(
                flops=4 * width * rows * count * n_blocks,
                transcendentals=0,
                bytes_accessed=4 * width * rows + 4 * width * count * n_blocks,
            ),
            name="experts_back",
        )(gate_w, up_w, *dgates, *dups)


def body(
    tokens,
    routes,
    cotangent,
    norm_attn,
    w_query,
    w_key,
    w_value,
    w_out,
    norm_ffn,
    w_router,
    w_gate,
    w_up,
    w_down,
):
    comm = Comm()
    hold = lax.optimization_barrier
    count, width = tokens.shape[1], tokens.shape[2]
    top_k = routes.shape[2]
    n_experts, _, hidden_units = w_gate.shape
    all_experts = n_experts * comm.n_expert
    capacity = (9 * count * top_k + 8 * all_experts - 1) // (8 * all_experts)
    n_context, n_dp, share = comm.n_context, comm.n_dp, comm.share
    expert_index = lax.axis_index("expert")
    context_index = lax.axis_index("context")
    dp_index = lax.axis_index("dp")
    parity = context_index % share
    chunks = n_context // share
    units = hidden_units // share
    lanes = -(-all_experts // 32) * 32
    places = jnp.stack([expert_index * n_experts, dp_index, context_index // share])

    hidden = tokens[0].T.astype(F32)
    gain_attn = norm_attn.astype(F32)[:, None]
    gain_ffn = norm_ffn.astype(F32)[:, None]
    scale_attn = rms_scale(hidden)
    normed_attn = (hidden * scale_attn * gain_attn).astype(BF16)
    positions = context_index * count + jnp.arange(count, dtype=jnp.int32)
    cosine, sine = rope_tables(positions)
    key_t = rotate_t(mm(w_key, normed_attn, 0, 0), cosine, sine).astype(BF16)
    value_t = mm(w_value, normed_attn, 0, 0).astype(BF16)
    kv_width = key_t.shape[0]
    kv_own = jnp.concatenate([key_t, value_t], 0)
    kv_blocks = [kv_own]
    for s in range(1, n_context):
        pairs = [(i, i + s) for i in range(n_context - s)]
        kv_blocks.append(lax.ppermute(kv_own, "context", pairs))
    query_t = rotate_t(mm(w_query, normed_attn, 0, 0), cosine, sine)
    query_t = (query_t * HEAD_DIM**-0.5).astype(BF16)

    cot_t = cotangent[0].T
    routed = (
        routes[0].T[:, None, :] == jnp.arange(lanes, dtype=jnp.int32)[None, :, None]
    ).astype(F32)
    cot_message = jnp.concatenate([cot_t, routed.sum(0).astype(BF16)])
    cots = [cot_message] + [comm.pull(cot_message, k, 0) for k in range(1, comm.columns)]
    weights = prepare_weights(parity, w_gate, w_up, w_down, hidden_units // n_context, share)
    router_t = jnp.zeros((lanes, width), BF16).at[:all_experts].set(w_router.T)
    in_t, gate_w, up_w, down, down_t = weights
    in_t = in_t.reshape(n_experts * 2 * units, width)
    in_first = jnp.concatenate([in_t[: 2 * units], router_t])
    far = []
    if share == 2:
        across = comm.pair(cot_message)
        cots, across, in_t, in_first = hold((cots, across, in_t, in_first))
        far = [comm.pull(across, k, 0) for k in range(1, comm.columns)]
        cots = cots + [across]
    cots, far = [[[(0, x, 0)] for x in part] for part in (cots, far)]
    others = comm.from_core(cots) if comm.cores == 2 else []
    kv_blocks, in_t, in_first, gate_w, up_w, down, down_t = hold(
        (kv_blocks, in_t, in_first, gate_w, up_w, down, down_t)
    )
    out_t, out_low, lse = attention_forward(context_index, query_t, kv_blocks)
    middle = hidden + mm(w_out, out_low, 0, 0)
    scale_ffn = rms_scale(middle)
    normed_ffn = (middle * scale_ffn * gain_ffn).astype(BF16)
    if comm.cores == 2 and far:
        far_arrays, normed_ffn = hold(([block[0][1] for block in far], normed_ffn))
        far = [[(0, array, 0)] for array in far_arrays]
        others = others + comm.from_core(far)
    cots = cots + far + others
    rows = comm.gather_group(normed_ffn)

    routed_all = jnp.concatenate(
        [block[0][1][block[0][2] + width : block[0][2] + width + lanes] for block in cots]
    )
    n_blocks = len(cots)
    before = jnp.triu(jnp.ones((count, count), BF16), 1)
    ranking = mm(routed_all, before, 1, 0)
    chosen = routed_all.astype(F32)
    kept = jnp.where(ranking < capacity, chosen, 0.0)

    def side_by_side(array):
        array = array.reshape(n_blocks, lanes, count)
        return jnp.concatenate([array[b] for b in range(n_blocks)], 1)

    chosen, kept = side_by_side(chosen), side_by_side(kept)

    row_count = width // comm.n_expert

    def to_experts(*arrays):
        blocks = []
        for j in range(comm.cores):
            for k in range(comm.columns):
                column, core = expert_index // comm.cores, expert_index % comm.cores
                column = (column - k) % comm.columns
                target = column * comm.cores + (core + j) % comm.cores
                pieces = jnp.concatenate(
                    [
                        lax.dynamic_slice_in_dim(array, target * row_count, row_count, 0)
                        for array in arrays
                    ]
                )
                blocks.append(pieces if (j, k) == (0, 0) else comm.pull(pieces, k, j))
        return blocks

    own = Experts(rows, cots, width, units, share, chunks, n_dp)
    groups, at = [], 0
    for n in (1, (n_experts - 1) // 2, n_experts - 1 - (n_experts - 1) // 2):
        if n:
            groups.append((at, n))
            at += n
    acts, dgates, dups, dscales, kept_parts, arrived, crossing = ([] for _ in range(7))
    scales = None

    def pass_on(g, values):
        if g >= len(groups):
            return values
        terms, values = hold((arrived[g], values))
        terms = [kept_parts[g]] + terms

        def part(k):
            return sum(term[k].astype(F32) for term in terms)

        sent = comm.send_context([part(k).astype(BF16) for k in range(1, chunks)], share)
        crossing.append([part(0).astype(BF16)] + sent)
        return values

    for g, (first, n) in enumerate(groups):
        if g == 0:
            gates_all, scales, *done = own.act(
                places, first, n, kept, chosen, in_first, down, make_gates=True
            )
        else:
            done = own.act(places, first, n, kept, scales, in_t, down)
        for target, value in zip((acts, dgates, dups, dscales, kept_parts), done):
            target.append(value)
        arrived.append(comm.send_dp(done[5:]))
        if g == 0:
            scales, normed_attn, out_low = hold((scales, normed_attn, out_low))
            columns_got = to_experts(normed_attn, out_low)
        if g == 1:
            scales = pass_on(0, scales)

    columns_got, acts = hold((columns_got, acts))
    h1_rows = [x[:row_count] for x in columns_got]
    ob_rows = [x[row_count:] for x in columns_got]
    near_count = n_blocks // comm.cores

    def both_cores(call):
        other = None
        if comm.cores == 2:
            other = comm.push(call(near_count, near_count), 0, 1)
        return call(0, near_count), other

    message = both_cores(
        lambda first, n: own.out(places, lanes, down_t, acts, dscales, first, n)
    )
    back_other = None
    if comm.cores == 2:
        back_other = own.back(gate_w, up_w, dgates, dups, near_count, near_count)
        back_other = comm.push(back_other, 0, 1)
    message, dgates = hold((message, dgates))
    dgates, crossing[0] = pass_on(1, (dgates, crossing[0]))
    back_near = own.back(gate_w, up_w, dgates, dups, 0, near_count)
    message = comm.return_hops(*message)
    message, back_near = hold((message, back_near))
    back = comm.return_hops(back_near, back_other)
    returned = comm.return_last(message)
    back = pass_on(2, back)
    grad_normed_ffn = comm.return_last(back)
    result = (middle + returned[:width]).astype(BF16)
    grad_gates = returned[width : width + lanes] + returned[width + lanes :]
    gates_own = gates_all[:, :count]

    upstream = cot_t.astype(F32)
    mean_grad = jnp.sum(gates_own * grad_gates, 0, keepdims=True)
    grad_logits = (gates_own * (grad_gates - mean_grad)).astype(BF16)
    grad_normed_ffn = grad_normed_ffn + mm(router_t, grad_logits, 0, 0)
    grad_gain_ffn = jnp.sum(grad_normed_ffn * middle * scale_ffn, 1)
    grad_middle = upstream + norm_back(grad_normed_ffn, middle, scale_ffn, gain_ffn)
    grad_branch = grad_middle.astype(BF16)

    gain_grid = grad_gain_ffn.reshape(-1, count)
    gain_lines = gain_grid.shape[0]
    gain_high = lax.reduce_precision(gain_grid, 8, 7)
    gain_rows = jnp.concatenate([gain_high, gain_grid - gain_high]).astype(BF16)
    gain_rows = jnp.pad(gain_rows, ((0, -2 * gain_lines % 16), (0, 0)))
    branch_all = comm.gather_columns(jnp.concatenate([grad_branch, grad_logits, gain_rows]))
    grad_attn_t = mm(w_out, grad_branch, 1, 0).astype(BF16)

    def attention_half(first, heads):
        return attention_backward(
            context_index, query_t, grad_attn_t, out_t, lse, kv_blocks, first, heads
        )

    def to_keys(grad_kv):
        return lax.all_to_all(grad_kv, "context", 0, 0, tiled=True)

    size_down = units // chunks // n_dp
    tiles = width // units

    def total_of(terms):
        total = jnp.concatenate([sum(x.astype(F32) for x in group) for group in terms])
        n = total.shape[0]
        part = total[:, : tiles * size_down].reshape(n, tiles, size_down, units)
        down = jnp.swapaxes(part, 1, 2).reshape(n, size_down, width)
        part = total[:, tiles * size_down :]
        return down, part.reshape(n, 2, share, part.shape[1] // 2 // share, units)

    def send_pair(part):
        if share == 1:
            return part[:, :, 0], None
        keep = lax.dynamic_index_in_dim(part, parity, 2, False)
        send = lax.dynamic_index_in_dim(part, 1 - parity, 2, False)
        return keep, comm.pair(send.astype(BF16))

    def both_columns(keep, other):
        if other is None:
            return keep
        other = other.astype(F32)
        first = jnp.where(parity == 0, keep, other)
        second = jnp.where(parity == 0, other, keep)
        chunk = hidden_units // n_context
        pieces = []
        for q in range(chunks):
            pieces += [x[..., q * chunk : (q + 1) * chunk] for x in (first, second)]
        return jnp.concatenate(pieces, -1)

    early = crossing[:-1]
    early, grad_attn_t = hold((early, grad_attn_t))
    totals = [total_of(early)] if early else []
    pairs = [send_pair(part) for _, part in totals]
    half = KV_HEADS // 2
    grad_query_a, grad_kv_a = attention_half(0, half)
    kv_a = to_keys(grad_kv_a)
    branch_all, grad_attn_t = hold((branch_all, grad_attn_t))
    branch_all = comm.gather_cores(branch_all)
    grad_query_b, grad_kv_b = attention_half(half, half)
    kv_a, grad_kv_b, branch_all, pairs, crossing[-1] = hold(
        (kv_a, grad_kv_b, branch_all, pairs, crossing[-1])
    )
    kv_b = to_keys(grad_kv_b)

    out_sum = comm.scatter_rows(ob_rows, branch_all, width)
    h2_rows = [
        lax.dynamic_slice_in_dim(array, at + expert_index * row_count, row_count, 0)
        for j in range(comm.cores)
        for ((_, array, at),) in rows[j * near_count : j * near_count + comm.columns]
    ]
    router_rows = sum(mm(a, b[width : width + lanes], 1, 1) for a, b in zip(h2_rows, branch_all))
    gain_total = sum(x[width + lanes :].astype(F32) for x in branch_all)
    gain_total = gain_total[:gain_lines] + gain_total[gain_lines : 2 * gain_lines]
    gain_part = lax.dynamic_slice_in_dim(
        gain_total.reshape(width), expert_index * row_count, row_count, 0
    )
    rest = jnp.zeros((row_count, LANES - lanes - 1), F32)
    extra = jnp.concatenate([router_rows, gain_part[:, None], rest], 1).astype(BF16)
    extra = extra.reshape(n_context * n_dp, -1, LANES)
    extra, kv_b = hold((extra, kv_b))
    extra = lax.all_to_all(extra, ("context", "dp"), 0, 0, tiled=True)
    extra = jnp.sum(extra.astype(F32), 0)

    grad_query_raw = jnp.concatenate(
        [rotate_t(x, cosine, -sine).astype(BF16) for x in (grad_query_a, grad_query_b)]
    )
    query_sum = comm.scatter_rows(h1_rows, comm.gather_expert(grad_query_raw), width)
    late, kv_b = hold((crossing[-1], kv_b))
    totals.append(total_of([late]))
    pairs.append(send_pair(totals[-1][1]))
    kv_sums = [jnp.sum(x.astype(F32), 0) for x in (kv_a, kv_b)]
    grad_key_raw = [rotate_t(kv_sum[0], cosine, -sine).astype(BF16) for kv_sum in kv_sums]
    grad_kv_raw = jnp.concatenate(grad_key_raw + [kv_sum[1].astype(BF16) for kv_sum in kv_sums])
    kv_rows = comm.scatter_rows(h1_rows, comm.gather_expert(grad_kv_raw), 2 * kv_width)
    key_sum, value_sum = kv_rows[:, :kv_width], kv_rows[:, kv_width:]

    down_sum = jnp.concatenate([down for down, _ in totals])
    parts = [both_columns(*pair) for pair in pairs]
    gate_sum = jnp.concatenate([part[:, 0] for part in parts])
    up_sum = jnp.concatenate([part[:, 1] for part in parts])

    shard = (expert_index * n_context + context_index) * n_dp + dp_index
    shard_rows = query_sum.shape[0]

    def shard_of(array):
        return lax.dynamic_slice_in_dim(array, shard * shard_rows, shard_rows, 0).astype(F32)

    gain_sum = (
        jnp.sum(shard_of(w_query) * query_sum, 1)
        + jnp.sum(shard_of(w_key) * key_sum, 1)
        + jnp.sum(shard_of(w_value) * value_sum, 1)
    ) / shard_of(norm_attn)

    grad_normed_attn = mm(w_query, grad_query_raw, 1, 0)
    grad_normed_attn = grad_normed_attn + mm(w_key, grad_kv_raw[:kv_width], 1, 0)
    grad_normed_attn = grad_normed_attn + mm(w_value, grad_kv_raw[kv_width:], 1, 0)
    grad_hidden = grad_middle + norm_back(grad_normed_attn, hidden, scale_attn, gain_attn)
    return (
        result.T[None],
        grad_hidden.astype(BF16).T[None],
        gain_sum,
        query_sum,
        key_sum,
        value_sum,
        out_sum,
        extra[:, lanes],
        extra[:, :all_experts],
        gate_sum,
        up_sum,
        down_sum,
    )


def solution(mesh):
    rows = P(("expert", "dp"), "context", None)
    dense = P(("expert", "context", "dp"), None)
    vector = P(("expert", "context", "dp"))
    experts = P("expert", None, None)
    expert_grads = P("expert", ("context", "dp"), None)
    return jax.shard_map(
        body,
        mesh=mesh,
        in_specs=(rows, rows, rows) + (P(),) * 7 + (experts,) * 3,
        out_specs=(rows, rows, vector, dense, dense, dense, dense, vector, dense)
        + (expert_grads,) * 3,
        check_vma=False,
    )
```

```python
import functools

import jax
import jax.numpy as jnp
from jax import lax
from jax.experimental import pallas as pl
from jax.experimental.pallas import tpu as pltpu
from jax.sharding import PartitionSpec as P

HEADS = 24
KV_HEADS = 8
HEAD_DIM = 64
GROUP = HEADS // KV_HEADS


EPS = 1e-05
ROPE_BASE = 10000.0
NEG_LARGE = -1e30
F32 = jnp.float32
BF16 = jnp.bfloat16
LANES = 128


def cost(flops, bytes_accessed, transcendentals=0):
    scale = 64
    return pl.CostEstimate(
        flops=flops // scale,
        bytes_accessed=bytes_accessed // scale,
        transcendentals=transcendentals // scale,
    )


def rms_scale(values):
    return lax.rsqrt(jnp.mean(values * values, 0, keepdims=True) + EPS)


def norm_back(grad_out, values, scale, gain):
    weighted = gain * grad_out
    return scale * weighted - values * scale**3 * jnp.mean(weighted * values, 0, keepdims=True)


def mm(a, b, da, db):
    return lax.dot_general(a, b, (((da,), (db,)), ((), ())), preferred_element_type=F32)


class Comm:
    def __init__(self):
        self.n_expert = lax.axis_size("expert")
        self.n_context = lax.axis_size("context")
        self.n_dp = lax.axis_size("dp")
        self.cores = 2 if self.n_expert % 2 == 0 else 1
        self.columns = self.n_expert // self.cores
        self.share = 2 if self.n_context % 2 == 0 else 1

    def peer(self, i, k, j):
        column, core = divmod(i, self.cores)
        return ((column + k) % self.columns) * self.cores + (core + j) % self.cores

    def pull(self, value, k, j):
        pairs = [(self.peer(i, k, j), i) for i in range(self.n_expert)]
        return lax.ppermute(value, "expert", pairs)

    def push(self, value, k, j):
        pairs = [(i, self.peer(i, k, j)) for i in range(self.n_expert)]
        return lax.ppermute(value, "expert", pairs)

    def pair(self, value):
        return lax.ppermute(value, "context", [(i, i ^ 1) for i in range(self.n_context)])

    def from_core(self, blocks):
        arrays = [array for block in blocks for _, array, _ in block]
        moved = self.pull(jnp.concatenate(arrays) if len(arrays) > 1 else arrays[0], 0, 1)
        out, at = [], 0
        for block in blocks:
            pieces = []
            for row, array, _ in block:
                pieces.append((row, moved, at))
                at += array.shape[0]
            out.append(pieces)
        return out

    def gather_columns(self, value):
        return [value] + [self.pull(value, k, 0) for k in range(1, self.columns)]

    def gather_cores(self, near):
        if self.cores == 2:
            near = near + [self.pull(block, 0, 1) for block in near]
        return near

    def gather_expert(self, value):
        return self.gather_cores(self.gather_columns(value))

    def gather_group(self, value, beside):
        columns = [self.pull(value, k, 0) for k in range(1, self.columns)]
        far = []
        if self.share == 2:
            half = value.shape[0] // 2
            across = self.pair(value)
            columns, across, beside = lax.optimization_barrier((columns, across, beside))
        first = [[(0, value, 0)]] + [[(0, block, 0)] for block in columns]
        if self.share == 2:
            first.append([(0, across, 0)])
            for k in range(1, self.columns):
                top = self.pull(across[:half], k, 0)
                bottom = self.pair(columns[k - 1][half:])
                far.append([(0, top, 0), (half, bottom, 0)])
        blocks = first + far
        if self.cores == 2:
            blocks = blocks + self.from_core(first)
            blocks = blocks + (self.from_core(far) if far else [])
        return blocks, beside

    def return_hops(self, near, other):
        columns = self.columns
        shape = (self.share, columns) + near.shape[1:]
        arrays = [x.reshape(shape) for x in (near, other) if x is not None]

        def part(*at):
            return sum(array[at].astype(F32) for array in arrays)

        if self.share == 1:
            sent = [self.push(part(0, k).astype(BF16), k, 0) for k in range(1, columns)]
            return [part(0, 0)] + sent
        half = near.shape[1] // 2
        low, high = slice(0, half), slice(half, 2 * half)
        every = slice(None)
        by_column = [
            self.push(part(every, k, low).astype(BF16), k, 0) for k in range(1, columns)
        ]
        by_pair = self.pair(part(1, every, high).astype(BF16))
        return [part(every, 0, low)] + by_column + [part(0, every, high), by_pair]

    def return_last(self, terms):
        columns = self.columns
        if self.share == 1:
            return sum(term.astype(F32) for term in terms)
        top = terms[:columns]
        bottom = terms[columns : columns + 2]

        def total(parts, at):
            return sum(part[at].astype(F32) for part in parts)

        top_other = self.pair(total(top, 1).astype(BF16))
        others = [
            self.push(total(bottom, k).astype(BF16), k, 0).astype(F32)
            for k in range(1, columns)
        ]
        return jnp.concatenate(
            [total(top, 0) + top_other.astype(F32), sum(others, total(bottom, 0))]
        )

    def send_dp(self, parts):
        n = self.n_dp
        return [
            lax.ppermute(parts[s - 1], "dp", [(i, (i + s) % n) for i in range(n)])
            for s in range(1, n)
        ]

    def send_context(self, parts, stride):
        n = self.n_context // stride
        out = []
        for s in range(1, n):
            pairs = []
            for i in range(self.n_context):
                k, r = divmod(i, stride)
                pairs.append((i, ((k + s) % n) * stride + r))
            out.append(lax.ppermute(parts[s - 1], "context", pairs))
        return out

    def scatter_rows(self, left, right, width):
        n, m = self.n_context, self.n_dp
        c, d = lax.axis_index("context"), lax.axis_index("dp")
        size = left[0].shape[0] // (n * m)
        if size % 16 == 0:
            mine, *parts = row_products(jnp.stack([c, d]), left, right, width, n, m)
        else:
            local = sum(mm(a, b[:width], 1, 1) for a, b in zip(left, right))
            local = local.reshape(n, m, size, width)
            local = jnp.stack(
                [lax.dynamic_index_in_dim(local, (c + k) % n, 0, False) for k in range(n)]
            )
            mine, *parts = [
                lax.dynamic_index_in_dim(local, (d + s) % m, 1, False) for s in range(m)
            ]
        came = self.send_dp([part.astype(BF16) for part in parts])

        def of_context(k):
            return mine[k].astype(F32) + sum(x[k].astype(F32) for x in came)

        came_far = self.send_context([of_context(k).astype(BF16) for k in range(1, n)], 1)
        return of_context(0) + sum(x.astype(F32) for x in came_far)


def row_products_kernel(count, place_ref, *refs):
    left, right, outs, total_s = refs[:count], refs[count : 2 * count], refs[2 * count : -1], refs[-1]
    width = total_s.shape[1]
    total = mm(left[0][...], right[0][:width, :], 1, 1)
    for a, b in zip(left[1:], right[1:]):
        total = total + mm(a[...], b[:width, :], 1, 1)
    total_s[...] = total
    n, size, _ = outs[0].shape
    m = len(outs)
    for k in range(n):
        for s in range(m):
            owner = lax.rem(place_ref[0] + k, n) * m + lax.rem(place_ref[1] + s, m)
            rows = pl.ds(pl.multiple_of(owner * size, size), size)
            outs[s][k] = total_s[rows, :].astype(outs[s].dtype)


def row_products(place, left, right, width, n, m):
    rows = left[0].shape[0]
    size = rows // (n * m)

    def whole(shape):
        return pl.BlockSpec(shape, lambda i, p: (0,) * len(shape))

    return pl.pallas_call(
        functools.partial(row_products_kernel, len(left)),
        out_shape=tuple(
            jax.ShapeDtypeStruct((n, size, width), BF16 if s else F32) for s in range(m)
        ),
        grid_spec=pltpu.PrefetchScalarGridSpec(
            num_scalar_prefetch=1,
            grid=(1,),
            in_specs=[whole(x.shape) for x in left + right],
            out_specs=tuple(whole((n, size, width)) for _ in range(m)),
            scratch_shapes=[pltpu.VMEM((rows, width), F32)],
        ),
        compiler_params=pltpu.CompilerParams(vmem_limit_bytes=32 << 20),
        cost_estimate=cost(
            flops=2 * rows * width * right[0].shape[1] * len(left),
            bytes_accessed=8 * width * right[0].shape[1] + 6 * rows * width,
        ),
        name="row_products",
    )(place, *left, *right)


def attn_fwd_kernel(blocks, c_ref, q_ref, *refs):
    k_refs, v_refs = refs[:blocks], refs[blocks : 2 * blocks]
    o_ref, ob_ref, lse_ref, scores_ref = refs[2 * blocks :]
    c = c_ref[0]
    n = q_ref.shape[1]
    hd = HEAD_DIM
    for s in range(blocks):
        rows = slice(s * n, (s + 1) * n)

        def fill(s=s, rows=rows):
            for g in range(GROUP):
                scores = mm(k_refs[s][...], q_ref[g * hd : (g + 1) * hd, :], 0, 0)
                if s == 0:
                    key = lax.broadcasted_iota(jnp.int32, scores.shape, 0)
                    query = lax.broadcasted_iota(jnp.int32, scores.shape, 1)
                    scores = jnp.where(key <= query, scores, NEG_LARGE)
                scores_ref[g, rows, :] = scores

        def blank(rows=rows):
            for g in range(GROUP):
                scores_ref[g, rows, :] = jnp.full((n, n), NEG_LARGE, F32)

        if s == 0:
            fill()
        else:
            pl.when(c >= s)(fill)
            pl.when(c < s)(blank)
    lse_ref[...] = jnp.zeros_like(lse_ref)
    for g in range(GROUP):
        scores = scores_ref[g]
        top = jnp.max(scores, 0, keepdims=True)
        weights = jnp.exp(scores - top)
        total = jnp.sum(weights, 0, keepdims=True)
        weights = weights.astype(BF16)
        out = jnp.zeros((hd, n), F32)
        for s in range(blocks):
            out = out + mm(v_refs[s][...], weights[s * n : (s + 1) * n], 1, 0)
        out = out / total
        o_ref[g * hd : (g + 1) * hd, :] = out
        ob_ref[g * hd : (g + 1) * hd, :] = out.astype(BF16)
        lse_ref[0, g : g + 1, :] = top + jnp.log(total)


def kv_specs(blocks, n, first=0):
    keys = [pl.BlockSpec((HEAD_DIM, n), lambda h, c: (first + h, 0))] * blocks
    values = [pl.BlockSpec((HEAD_DIM, n), lambda h, c: (first + h + KV_HEADS, 0))] * blocks
    return keys + values


def attention_forward(context_index, query_t, kv_blocks):
    blocks = len(kv_blocks)
    n = query_t.shape[1]
    wide = GROUP * HEAD_DIM
    heads = query_t.shape[0] // wide
    head = pl.BlockSpec((wide, n), lambda h, c: (h, 0))
    return pl.pallas_call(
        functools.partial(attn_fwd_kernel, blocks),
        out_shape=(
            jax.ShapeDtypeStruct(query_t.shape, F32),
            jax.ShapeDtypeStruct(query_t.shape, BF16),
            jax.ShapeDtypeStruct((heads, 8, n), F32),
        ),
        grid_spec=pltpu.PrefetchScalarGridSpec(
            num_scalar_prefetch=1,
            grid=(heads,),
            in_specs=[head] + kv_specs(blocks, n),
            out_specs=(head, head, pl.BlockSpec((1, 8, n), lambda h, c: (h, 0, 0))),
            scratch_shapes=[pltpu.VMEM((GROUP, blocks * n, n), F32)],
        ),
        compiler_params=pltpu.CompilerParams(vmem_limit_bytes=40 << 20),
        cost_estimate=cost(
            flops=heads * GROUP * blocks * n * n * 256 * 4,
            transcendentals=heads * GROUP * blocks * n * n,
            bytes_accessed=16 * query_t.size,
        ),
        name="attn_fwd",
    )(context_index.reshape(1), query_t, *kv_blocks, *kv_blocks)


def attn_bwd_kernel(blocks, c_ref, q_ref, do_ref, o_ref, lse_ref, *refs):
    k_refs, v_refs = refs[:blocks], refs[blocks : 2 * blocks]
    dq_ref, dkv_ref = refs[2 * blocks :]
    c = c_ref[0]
    n = q_ref.shape[1]
    hd = HEAD_DIM
    deltas = []
    for g in range(GROUP):
        head = slice(g * hd, (g + 1) * hd)
        both = do_ref[head, :].astype(F32) * o_ref[head, :]
        deltas.append(jnp.sum(both, 0, keepdims=True))
    for s in range(blocks):

        def work(s=s):
            dk = jnp.zeros((hd, n), F32)
            dv = jnp.zeros((hd, n), F32)
            key_t = k_refs[s][...]
            value_t = v_refs[s][...]
            for g in range(GROUP):
                head = slice(g * hd, (g + 1) * hd)
                query, grad = q_ref[head, :], do_ref[head, :]
                scores = mm(key_t, query, 0, 0)
                weights = jnp.exp(scores - lse_ref[0, g : g + 1, :])
                if s == 0:
                    key = lax.broadcasted_iota(jnp.int32, scores.shape, 0)
                    place = lax.broadcasted_iota(jnp.int32, scores.shape, 1)
                    weights = jnp.where(key <= place, weights, 0.0)
                grad_weights = mm(value_t, grad, 0, 0)
                grad_scores = (weights * (grad_weights - deltas[g])).astype(BF16)
                dv = dv + mm(grad, weights.astype(BF16), 1, 1)
                dk = dk + mm(query, grad_scores, 1, 1)
                step = mm(key_t, grad_scores, 1, 0) * (HEAD_DIM**-0.5)
                if s == 0:
                    dq_ref[head, :] = step
                else:
                    dq_ref[head, :] += step
            owner = lax.rem(c - s + blocks, blocks)
            dkv_ref[owner, 0] = dk.astype(BF16)
            dkv_ref[owner, 1] = dv.astype(BF16)

        def skip(s=s):
            owner = lax.rem(c - s + blocks, blocks)
            dkv_ref[owner] = jnp.zeros(dkv_ref.shape[1:], BF16)

        if s == 0:
            work()
        else:
            pl.when(c >= s)(work)
            pl.when(c < s)(skip)


def attention_backward(context_index, query_t, grad_t, out_t, lse, kv_blocks, first, heads):
    blocks = len(kv_blocks)
    n = query_t.shape[1]
    wide = GROUP * HEAD_DIM
    head = pl.BlockSpec((wide, n), lambda h, c: (first + h, 0))
    out = pl.BlockSpec((wide, n), lambda h, c: (h, 0))
    return pl.pallas_call(
        functools.partial(attn_bwd_kernel, blocks),
        out_shape=(
            jax.ShapeDtypeStruct((heads * wide, n), F32),
            jax.ShapeDtypeStruct((blocks, 2, heads * HEAD_DIM, n), BF16),
        ),
        grid_spec=pltpu.PrefetchScalarGridSpec(
            num_scalar_prefetch=1,
            grid=(heads,),
            in_specs=[head, head, head, pl.BlockSpec((1, 8, n), lambda h, c: (first + h, 0, 0))]
            + kv_specs(blocks, n, first),
            out_specs=(
                out,
                pl.BlockSpec((blocks, 2, HEAD_DIM, n), lambda h, c: (0, 0, h, 0)),
            ),
        ),
        compiler_params=pltpu.CompilerParams(vmem_limit_bytes=40 << 20),
        cost_estimate=cost(
            flops=heads * GROUP * blocks * n * n * 256 * 10,
            transcendentals=heads * GROUP * blocks * n * n,
            bytes_accessed=20 * query_t.size,
        ),
        name="attn_bwd",
    )(context_index.reshape(1), query_t, grad_t, out_t, lse, *kv_blocks, *kv_blocks)


def rope_tables(positions):
    half_dim = HEAD_DIM // 2
    frequency = ROPE_BASE ** (-2.0 * jnp.arange(half_dim, dtype=F32) / HEAD_DIM)
    angles = frequency[:, None] * positions.astype(F32)[None, :]
    return jnp.cos(angles), jnp.sin(angles)


def rotate_t(values_t, cosine, sine):
    shaped = values_t.reshape(-1, 2, HEAD_DIM // 2, values_t.shape[1])
    low, high = shaped[:, 0], shaped[:, 1]
    turned = jnp.stack([low * cosine - high * sine, high * cosine + low * sine], 1)
    return turned.reshape(values_t.shape)


def prepare_kernel(p_ref, gate_ref, up_ref, down_ref, *outs):
    in_t_ref, gate_out, up_out, down_out, down_t_out = outs
    gate, up, down = gate_ref[0], up_ref[0], down_ref[0]
    in_t_ref[0, 0, 0] = gate.astype(F32).T.astype(BF16)
    in_t_ref[0, 1, 0] = up.astype(F32).T.astype(BF16)
    gate_out[...] = gate
    up_out[...] = up
    down_out[...] = down
    down_t_out[...] = down.astype(F32).T.astype(BF16)


def prepare_weights(parity, w_gate, w_up, w_down, chunk, share):
    experts, width, hidden = w_gate.shape
    chunks = hidden // chunk // share
    units = chunks * chunk

    def column(e, q, p):
        return (e, 0, q * share + p[0])

    def flat(e, q, p):
        return (0, e * chunks + q)

    return pl.pallas_call(
        prepare_kernel,
        out_shape=(
            jax.ShapeDtypeStruct((experts, 2, chunks, chunk, width), BF16),
            jax.ShapeDtypeStruct((width, experts * units), BF16),
            jax.ShapeDtypeStruct((width, experts * units), BF16),
            jax.ShapeDtypeStruct((experts * units, width), BF16),
            jax.ShapeDtypeStruct((width, experts * units), BF16),
        ),
        grid_spec=pltpu.PrefetchScalarGridSpec(
            num_scalar_prefetch=1,
            grid=(experts, chunks),
            in_specs=[
                pl.BlockSpec((1, width, chunk), column),
                pl.BlockSpec((1, width, chunk), column),
                pl.BlockSpec((1, chunk, width), lambda e, q, p: (e, q * share + p[0], 0)),
            ],
            out_specs=(
                pl.BlockSpec((1, 2, 1, chunk, width), lambda e, q, p: (e, 0, q, 0, 0)),
                pl.BlockSpec((width, chunk), flat),
                pl.BlockSpec((width, chunk), flat),
                pl.BlockSpec((chunk, width), lambda e, q, p: (e * chunks + q, 0)),
                pl.BlockSpec((width, chunk), flat),
            ),
        ),
        compiler_params=pltpu.CompilerParams(vmem_limit_bytes=60 << 20),
        cost_estimate=cost(
            flops=0, transcendentals=0, bytes_accessed=18 * experts * width * units
        ),
        name="prepare_weights",
    )(parity.reshape(1), w_gate, w_up, w_down)


def piece_copies(blocks, refs, target_ref, sems):
    out, at = [], 0
    count = refs[0].shape[1]
    for b, pieces in enumerate(blocks):
        copies = []
        for i, (first, ref, row) in enumerate(pieces):
            last = pieces[i + 1][0] if i + 1 < len(pieces) else target_ref.shape[0]
            copies.append(
                pltpu.make_async_copy(
                    refs[ref].at[row : row + last - first],
                    target_ref.at[first:last, b * count : (b + 1) * count],
                    sems.at[at],
                )
            )
            at += 1
        out.append(copies)
    return out


def write_grads(rows_ref, cots_ref, act, dgate, dup, place_ref, outs, down_s, in_s, share):
    owners = len(outs)
    chunks, _, _, units = outs[0].shape
    width = rows_ref.shape[0]
    size = units // chunks // owners
    tiles = width // units

    def place(k, s):
        return lax.rem(place_ref[2] + k, chunks), lax.rem(place_ref[1] + s, owners)

    down_s[...] = mm(act, cots_ref[...], 1, 1).astype(BF16)
    for k in range(chunks):
        for s in range(owners):
            at_k, at_d = place(k, s)
            start = pl.multiple_of((at_k * owners + at_d) * size, size)
            for t in range(tiles):
                outs[s][k, 0, t * size : (t + 1) * size, :] = down_s[
                    pl.ds(start, size), t * units : (t + 1) * units
                ]
    base = tiles * size
    size = width // (chunks * share * owners)
    for grad_act in (dgate, dup):
        in_s[...] = mm(rows_ref[...], grad_act, 1, 1).astype(BF16)
        for k in range(chunks):
            for q in range(share):
                for s in range(owners):
                    at_k, at_d = place(k, s)
                    start = pl.multiple_of(((at_k * share + q) * owners + at_d) * size, size)
                    to = base + q * size
                    outs[s][k, 0, to : to + size, :] = in_s[pl.ds(start, size), :]
        base += share * size


class Experts:
    def __init__(self, rows, cots, width, units, share, chunks, owners):
        self.arrays, self.plans = [], []
        for blocks in (rows, cots):
            arrays, plan = [], []
            for block in blocks:
                pieces = []
                for first, array, row in block:
                    known = [i for i, x in enumerate(arrays) if x is array]
                    if not known:
                        arrays.append(array)
                    pieces.append((first, known[0] if known else len(arrays) - 1, row))
                plan.append(pieces)
            self.arrays.append(arrays)
            self.plans.append(plan)
        self.blocks = len(rows)
        self.width, self.count = width, rows[0][0][1].shape[1]
        self.tokens = self.blocks * self.count
        self.units, self.share, self.chunks, self.owners = units, share, chunks, owners
        self.height = self.width // chunks // owners * 3

    def n_arrays(self):
        return sum(map(len, self.arrays))

    def scratch(self):
        wide = pltpu.VMEM((self.width, self.tokens), BF16)
        sems = [pltpu.SemaphoreType.DMA((sum(map(len, plan)),)) for plan in self.plans]
        return [wide, wide] + sems

    def copies(self, refs, rows_ref, cots_ref, row_sems, cot_sems):
        n = len(self.arrays[0])
        row_copies = piece_copies(self.plans[0], refs[:n], rows_ref, row_sems)
        cot_copies = piece_copies(self.plans[1], refs[n:], cots_ref, cot_sems)
        return [a + b for a, b in zip(row_copies, cot_copies)]

    def grads_structs(self, n):
        shape = (self.chunks, n, self.height, self.units)
        spec = pl.BlockSpec(
            (self.chunks, 1, self.height, self.units), lambda i, *_: (0, i, 0, 0)
        )
        return [jax.ShapeDtypeStruct(shape, BF16)] * self.owners, [spec] * self.owners

    def act_kernel(self, first, n, make_gates, e_ref, *refs):
        n_arrays = self.n_arrays()
        kept_ref, scales_ref, in_t_ref, down_ref = refs[:4]
        piece_refs, outs, scratch = refs[4 : 4 + n_arrays], refs[4 + n_arrays : -6], refs[-6:]
        if make_gates:
            chosen_ref = scales_ref
            gates_ref, scales_ref = outs[:2]
            outs = outs[2:]
        act_ref, dgate_ref, dup_ref, dscale_ref = outs[:4]
        rows_ref, cots_ref = scratch[:2]
        units, count, blocks = self.units, self.count, self.blocks
        copies = self.copies(piece_refs, *scratch[:4])
        step = pl.program_id(0)
        row = e_ref[0] + first + step

        def move(wait, start):
            def run():
                for b in start:
                    for copy in copies[b]:
                        copy.start()
                for copy in copies[wait]:
                    copy.wait()

            if n == 1:
                run()
            else:
                pl.when(step == 0)(run)

        def products(b):
            move(b, range(blocks) if b == 0 else ())
            cols = slice(b * count, (b + 1) * count)
            acts = jnp.dot(in_t_ref[...], rows_ref[:, cols], preferred_element_type=F32)
            grad = jnp.dot(down_ref[...], cots_ref[:, cols], preferred_element_type=F32)
            return acts, grad

        def finish(b, acts, grad):
            cols = slice(b * count, (b + 1) * count)
            gate, up = acts[:units], acts[units : 2 * units]
            if make_gates:
                chosen = chosen_ref[:, cols] > 0
                logits = jnp.where(chosen, acts[2 * units :], NEG_LARGE)
                gates = jnp.exp(logits - jnp.max(logits, 0, keepdims=True))
                gates = jnp.where(chosen, gates, 0.0)
                gates = gates / jnp.sum(gates, 0, keepdims=True)
                gates_ref[:, cols] = gates
                scales_ref[:, cols] = gates * kept_ref[:, cols]
            scale = scales_ref[pl.ds(row, 1), cols]
            keep = kept_ref[pl.ds(row, 1), cols]
            sigmoid = jax.nn.sigmoid(gate)
            silu = gate * sigmoid
            hidden = silu * up
            dscale_ref[0, 0:1, cols] = keep * jnp.sum(hidden * grad, 0, keepdims=True)
            act_ref[:, cols] = (hidden * scale).astype(BF16)
            grad = grad * scale
            dup_ref[:, cols] = (grad * silu).astype(BF16)
            dgate_ref[:, cols] = (grad * up * (sigmoid + silu * (1.0 - sigmoid))).astype(BF16)

        dscale_ref[...] = jnp.zeros_like(dscale_ref)
        for b in range(blocks):
            finish(b, *products(b))
        write_grads(
            rows_ref,
            cots_ref,
            act_ref[...],
            dgate_ref[...],
            dup_ref[...],
            e_ref,
            outs[4:],
            *scratch[4:],
            self.share,
        )

    def act(self, places, first, n, kept, scales, in_t, down, make_gates=False):
        units, width, tokens = self.units, self.width, self.tokens
        lanes = kept.shape[0]
        in_rows = 2 * units + (lanes if make_gates else 0)
        table = pl.BlockSpec((lanes, tokens), lambda i, e: (0, 0))
        one = pl.BlockSpec((units, tokens), lambda i, e: (i, 0))
        outs, specs = [], []
        if make_gates:
            outs += [jax.ShapeDtypeStruct((lanes, tokens), F32)] * 2
            specs += [table] * 2
        outs += [jax.ShapeDtypeStruct((n * units, tokens), BF16)] * 3
        specs += [one] * 3
        outs.append(jax.ShapeDtypeStruct((n, 8, tokens), F32))
        specs.append(pl.BlockSpec((1, 8, tokens), lambda i, e: (i, 0, 0)))
        structs, grad_specs = self.grads_structs(n)
        extra = [pltpu.VMEM((units, width), BF16), pltpu.VMEM((width, units), BF16)]
        return pl.pallas_call(
            functools.partial(self.act_kernel, first, n, make_gates),
            out_shape=tuple(outs + structs),
            grid_spec=pltpu.PrefetchScalarGridSpec(
                num_scalar_prefetch=1,
                grid=(n,),
                in_specs=[
                    table,
                    table,
                    pl.BlockSpec((in_rows, width), lambda i, e: (first + i, 0)),
                    pl.BlockSpec((units, width), lambda i, e: (first + i, 0)),
                ]
                + [pl.BlockSpec(memory_space=pl.ANY)] * self.n_arrays(),
                out_specs=tuple(specs + grad_specs),
                scratch_shapes=self.scratch() + extra,
            ),
            compiler_params=pltpu.CompilerParams(vmem_limit_bytes=60 << 20),
            cost_estimate=cost(
                flops=12 * width * units * tokens * n,
                transcendentals=units * tokens * n,
                bytes_accessed=4 * width * tokens + 6 * n * units * (width + tokens),
            ),
            name="experts_act",
        )(places, kept, scales, in_t, down, *self.arrays[0], *self.arrays[1])

    def out_kernel(self, parts, e_ref, weight_ref, *refs):
        act_refs, dscale_refs = refs[:parts], refs[parts : 2 * parts]
        message_ref, act_s, dscale_s = refs[2 * parts :]
        at = row = 0
        dscale_s[...] = jnp.zeros_like(dscale_s)
        for act_ref, dscale_ref in zip(act_refs, dscale_refs):
            act_s[at : at + act_ref.shape[0], :] = act_ref[...]
            at += act_ref.shape[0]
            for i in range(dscale_ref.shape[0]):
                dscale_s[pl.ds(e_ref[0] + row, 1), :] = dscale_ref[i, 0:1, :]
                row += 1
        width, lanes = self.width, dscale_s.shape[0]
        message_ref[0, :width, :] = jnp.dot(
            weight_ref[...], act_s[...], preferred_element_type=F32
        ).astype(BF16)
        grads = dscale_s[...]
        high = grads.astype(BF16)
        message_ref[0, width : width + lanes, :] = high
        message_ref[0, width + lanes :, :] = (grads - high.astype(F32)).astype(BF16)

    def out(self, places, lanes, weight, acts, dscales, first_block, n_blocks):
        rows = weight.shape[1]
        parts = len(acts)
        width, count = self.width, self.count

        def column(shape):
            return pl.BlockSpec(
                shape, lambda b, e: (0,) * (len(shape) - 1) + (first_block + b,)
            )

        return pl.pallas_call(
            functools.partial(self.out_kernel, parts),
            out_shape=jax.ShapeDtypeStruct((n_blocks, width + 2 * lanes, count), BF16),
            grid_spec=pltpu.PrefetchScalarGridSpec(
                num_scalar_prefetch=1,
                grid=(n_blocks,),
                in_specs=[
                    pl.BlockSpec(
                        (width, rows),
                        lambda b, e: (0, 0),
                        pipeline_mode=pl.Buffered(buffer_count=1),
                    )
                ]
                + [column((a.shape[0], count)) for a in acts]
                + [column((a.shape[0], 8, count)) for a in dscales],
                out_specs=pl.BlockSpec((1, width + 2 * lanes, count), lambda b, e: (b, 0, 0)),
                scratch_shapes=[pltpu.VMEM((rows, count), BF16), pltpu.VMEM((lanes, count), F32)],
            ),
            compiler_params=pltpu.CompilerParams(vmem_limit_bytes=60 << 20),
            cost_estimate=cost(
                flops=2 * width * rows * count * n_blocks,
                transcendentals=0,
                bytes_accessed=2 * width * rows + 4 * width * count * n_blocks,
            ),
            name="experts_out",
        )(places, weight, *acts, *dscales)

    def back_kernel(self, parts, gate_w_ref, up_w_ref, *refs):
        dgate_refs, dup_refs = refs[:parts], refs[parts : 2 * parts]
        back_ref, dgate_s, dup_s = refs[2 * parts :]
        for target, pieces in ((dgate_s, dgate_refs), (dup_s, dup_refs)):
            at = 0
            for piece in pieces:
                target[at : at + piece.shape[0], :] = piece[...]
                at += piece.shape[0]
        back = jnp.dot(gate_w_ref[...], dgate_s[...], preferred_element_type=F32)
        back = back + jnp.dot(up_w_ref[...], dup_s[...], preferred_element_type=F32)
        back_ref[0] = back.astype(BF16)

    def back(self, gate_w, up_w, dgates, dups, first_block, n_blocks):
        width, count = self.width, self.count
        rows = gate_w.shape[1]
        parts = len(dgates)
        whole = pl.BlockSpec(
            (width, rows), lambda b: (0, 0), pipeline_mode=pl.Buffered(buffer_count=1)
        )
        column = [pl.BlockSpec((a.shape[0], count), lambda b: (0, first_block + b)) for a in dgates]
        return pl.pallas_call(
            functools.partial(self.back_kernel, parts),
            out_shape=jax.ShapeDtypeStruct((n_blocks, width, count), BF16),
            grid=(n_blocks,),
            in_specs=[whole, whole] + column * 2,
            out_specs=pl.BlockSpec((1, width, count), lambda b: (b, 0, 0)),
            scratch_shapes=[pltpu.VMEM((rows, count), BF16)] * 2,
            compiler_params=pltpu.CompilerParams(vmem_limit_bytes=60 << 20),
            cost_estimate=cost(
                flops=4 * width * rows * count * n_blocks,
                transcendentals=0,
                bytes_accessed=4 * width * rows + 4 * width * count * n_blocks,
            ),
            name="experts_back",
        )(gate_w, up_w, *dgates, *dups)


def body(
    tokens,
    routes,
    cotangent,
    norm_attn,
    w_query,
    w_key,
    w_value,
    w_out,
    norm_ffn,
    w_router,
    w_gate,
    w_up,
    w_down,
):
    comm = Comm()
    hold = lax.optimization_barrier
    count, width = tokens.shape[1], tokens.shape[2]
    top_k = routes.shape[2]
    n_experts, _, hidden_units = w_gate.shape
    all_experts = n_experts * comm.n_expert
    capacity = (9 * count * top_k + 8 * all_experts - 1) // (8 * all_experts)
    n_context, n_dp, share = comm.n_context, comm.n_dp, comm.share
    expert_index = lax.axis_index("expert")
    context_index = lax.axis_index("context")
    dp_index = lax.axis_index("dp")
    parity = context_index % share
    chunks = n_context // share
    units = hidden_units // share
    lanes = -(-all_experts // 32) * 32
    places = jnp.stack([expert_index * n_experts, dp_index, context_index // share])

    cot_t = cotangent[0].T
    routed = (
        routes[0].T[:, None, :] == jnp.arange(lanes, dtype=jnp.int32)[None, :, None]
    ).astype(F32)
    cot_message = jnp.concatenate([cot_t, routed.sum(0).astype(BF16)])
    tokens, cot_message = hold((tokens, cot_message))
    across = [comm.pair(cot_message)] if share == 2 else []
    cots = [cot_message] + [comm.pull(cot_message, k, 0) for k in range(1, comm.columns)]

    hidden = tokens[0].T.astype(F32)
    gain_attn = norm_attn.astype(F32)[:, None]
    gain_ffn = norm_ffn.astype(F32)[:, None]
    scale_attn = rms_scale(hidden)
    normed_attn = (hidden * scale_attn * gain_attn).astype(BF16)
    positions = context_index * count + jnp.arange(count, dtype=jnp.int32)
    cosine, sine = rope_tables(positions)
    key_t = rotate_t(mm(w_key, normed_attn, 0, 0), cosine, sine).astype(BF16)
    value_t = mm(w_value, normed_attn, 0, 0).astype(BF16)
    kv_width = key_t.shape[0]
    kv_own = jnp.concatenate([key_t, value_t], 0)
    kv_blocks = [kv_own]
    for s in range(1, n_context):
        pairs = [(i, i + s) for i in range(n_context - s)]
        kv_blocks.append(lax.ppermute(kv_own, "context", pairs))
    query_t = rotate_t(mm(w_query, normed_attn, 0, 0), cosine, sine)
    query_t = (query_t * HEAD_DIM**-0.5).astype(BF16)

    weights = prepare_weights(parity, w_gate, w_up, w_down, hidden_units // n_context, share)
    router_t = jnp.zeros((lanes, width), BF16).at[:all_experts].set(w_router.T)
    in_t, gate_w, up_w, down, down_t = weights
    in_t = in_t.reshape(n_experts * 2 * units, width)
    in_first = jnp.concatenate([in_t[: 2 * units], router_t])
    if across:
        across, in_t, in_first = hold((across, in_t, in_first))
        across = across + [comm.pull(across[0], k, 0) for k in range(1, comm.columns)]
        cots, across[0], in_t = hold((cots, across[0], in_t))
    cots, across = [[[(0, x, 0)] for x in part] for part in (cots, across)]
    others = comm.from_core(cots) if comm.cores == 2 else []
    kv_blocks, in_t, in_first, gate_w, up_w, down, down_t = hold(
        (kv_blocks, in_t, in_first, gate_w, up_w, down, down_t)
    )
    out_t, out_low, lse = attention_forward(context_index, query_t, kv_blocks)
    middle = hidden + mm(w_out, out_low, 0, 0)
    scale_ffn = rms_scale(middle)
    normed_ffn = (middle * scale_ffn * gain_ffn).astype(BF16)
    across = [block[0][1] for block in across]
    across, normed_ffn = hold((across, normed_ffn))
    rows, across = comm.gather_group(normed_ffn, across)
    across = [[(0, x, 0)] for x in across]
    if comm.cores == 2 and across:
        others = others + comm.from_core(across)
    cots = cots + across + others

    routed_all = jnp.concatenate(
        [block[0][1][block[0][2] + width : block[0][2] + width + lanes] for block in cots]
    )
    n_blocks = len(cots)
    before = jnp.triu(jnp.ones((count, count), BF16), 1)
    ranking = mm(routed_all, before, 1, 0)
    chosen = routed_all.astype(F32)
    kept = jnp.where(ranking < capacity, chosen, 0.0)

    def side_by_side(array):
        array = array.reshape(n_blocks, lanes, count)
        return jnp.concatenate([array[b] for b in range(n_blocks)], 1)

    chosen, kept = side_by_side(chosen), side_by_side(kept)

    row_count = width // comm.n_expert

    def for_experts(*arrays):
        out = []
        for j in range(comm.cores):
            for k in range(comm.columns):
                column, core = expert_index // comm.cores, expert_index % comm.cores
                column = (column - k) % comm.columns
                target = column * comm.cores + (core + j) % comm.cores
                pieces = [
                    lax.dynamic_slice_in_dim(array, target * row_count, row_count, 0)
                    for array in arrays
                ]
                out.append(jnp.concatenate(pieces))
        return out

    def to_experts(pieces):
        peers = [(j, k) for j in range(comm.cores) for k in range(comm.columns)]
        return pieces[:1] + [comm.pull(x, k, j) for x, (j, k) in zip(pieces[1:], peers[1:])]

    columns_sent = for_experts(normed_attn, out_low)
    chosen, columns_sent = hold((chosen, columns_sent))

    own = Experts(rows, cots, width, units, share, chunks, n_dp)
    groups, at = [], 0
    for n in (1, (n_experts - 1) // 2, n_experts - 1 - (n_experts - 1) // 2):
        if n:
            groups.append((at, n))
            at += n
    acts, dgates, dups, dscales, kept_parts, arrived, crossing = ([] for _ in range(7))
    scales = None

    def pass_on(g, values):
        if g >= len(groups):
            return values
        terms, values = hold((arrived[g], values))
        terms = [kept_parts[g]] + terms

        def part(k):
            return sum(term[k].astype(F32) for term in terms)

        sent = comm.send_context([part(k).astype(BF16) for k in range(1, chunks)], share)
        crossing.append([part(0).astype(BF16)] + sent)
        return values

    for g, (first, n) in enumerate(groups):
        if g == 0:
            gates_all, scales, *done = own.act(
                places, first, n, kept, chosen, in_first, down, make_gates=True
            )
        else:
            done = own.act(places, first, n, kept, scales, in_t, down)
        for target, value in zip((acts, dgates, dups, dscales, kept_parts), done):
            target.append(value)
        arrived.append(comm.send_dp(done[5:]))
        if g == 0:
            scales, columns_sent = hold((scales, columns_sent))
            columns_got = to_experts(columns_sent)
        if g == 1:
            scales = pass_on(0, scales)

    columns_got, acts = hold((columns_got, acts))
    h1_rows = [x[:row_count] for x in columns_got]
    ob_rows = [x[row_count:] for x in columns_got]
    near_count = n_blocks // comm.cores

    def both_cores(call):
        other = None
        if comm.cores == 2:
            other = comm.push(call(near_count, near_count), 0, 1)
        return call(0, near_count), other

    message = both_cores(
        lambda first, n: own.out(places, lanes, down_t, acts, dscales, first, n)
    )
    back_other = None
    if comm.cores == 2:
        back_other = own.back(gate_w, up_w, dgates, dups, near_count, near_count)
        back_other = comm.push(back_other, 0, 1)
    message, dgates = hold((message, dgates))
    dgates, crossing[0] = pass_on(1, (dgates, crossing[0]))
    back_near = own.back(gate_w, up_w, dgates, dups, 0, near_count)
    message = comm.return_hops(*message)
    message, back_near = hold((message, back_near))
    back = comm.return_hops(back_near, back_other)
    returned = comm.return_last(message)
    back = pass_on(2, back)
    grad_normed_ffn = comm.return_last(back)
    result = (middle + returned[:width]).astype(BF16)
    grad_gates = returned[width : width + lanes] + returned[width + lanes :]
    gates_own = gates_all[:, :count]

    upstream = cot_t.astype(F32)
    mean_grad = jnp.sum(gates_own * grad_gates, 0, keepdims=True)
    grad_logits = (gates_own * (grad_gates - mean_grad)).astype(BF16)
    grad_normed_ffn = grad_normed_ffn + mm(router_t, grad_logits, 0, 0)
    grad_gain_ffn = jnp.sum(grad_normed_ffn * middle * scale_ffn, 1)
    grad_middle = upstream + norm_back(grad_normed_ffn, middle, scale_ffn, gain_ffn)
    grad_branch = grad_middle.astype(BF16)

    gain_grid = grad_gain_ffn.reshape(-1, count)
    gain_lines = gain_grid.shape[0]
    gain_high = lax.reduce_precision(gain_grid, 8, 7)
    gain_rows = jnp.concatenate([gain_high, gain_grid - gain_high]).astype(BF16)
    gain_rows = jnp.pad(gain_rows, ((0, -2 * gain_lines % 16), (0, 0)))
    branch_all = comm.gather_columns(jnp.concatenate([grad_branch, grad_logits, gain_rows]))
    grad_attn_t = mm(w_out, grad_branch, 1, 0).astype(BF16)

    def attention_half(first, heads):
        return attention_backward(
            context_index, query_t, grad_attn_t, out_t, lse, kv_blocks, first, heads
        )

    def to_keys(grad_kv):
        return lax.all_to_all(grad_kv, "context", 0, 0, tiled=True)

    size_down = units // chunks // n_dp
    tiles = width // units

    def total_of(terms):
        total = jnp.concatenate([sum(x.astype(F32) for x in group) for group in terms])
        n = total.shape[0]
        part = total[:, : tiles * size_down].reshape(n, tiles, size_down, units)
        down = jnp.swapaxes(part, 1, 2).reshape(n, size_down, width)
        part = total[:, tiles * size_down :]
        return down, part.reshape(n, 2, share, part.shape[1] // 2 // share, units)

    def send_pair(part):
        if share == 1:
            return part[:, :, 0], None
        keep = lax.dynamic_index_in_dim(part, parity, 2, False)
        send = lax.dynamic_index_in_dim(part, 1 - parity, 2, False)
        return keep, comm.pair(send.astype(BF16))

    def both_columns(keep, other):
        if other is None:
            return keep
        other = other.astype(F32)
        first = jnp.where(parity == 0, keep, other)
        second = jnp.where(parity == 0, other, keep)
        chunk = hidden_units // n_context
        pieces = []
        for q in range(chunks):
            pieces += [x[..., q * chunk : (q + 1) * chunk] for x in (first, second)]
        return jnp.concatenate(pieces, -1)

    early = crossing[:-1]
    early, grad_attn_t = hold((early, grad_attn_t))
    totals = [total_of(early)] if early else []
    pairs = [send_pair(part) for _, part in totals]
    half = KV_HEADS // 2
    grad_query_a, grad_kv_a = attention_half(0, half)
    kv_a = to_keys(grad_kv_a)
    branch_all, grad_attn_t = hold((branch_all, grad_attn_t))
    branch_all = comm.gather_cores(branch_all)
    grad_query_b, grad_kv_b = attention_half(half, half)
    kv_a, grad_kv_b, branch_all, crossing[-1] = hold((kv_a, grad_kv_b, branch_all, crossing[-1]))
    kv_b = to_keys(grad_kv_b)

    out_sum = comm.scatter_rows(ob_rows, branch_all, width)
    h2_rows = [
        lax.dynamic_slice_in_dim(array, at + expert_index * row_count, row_count, 0)
        for j in range(comm.cores)
        for ((_, array, at),) in rows[j * near_count : j * near_count + comm.columns]
    ]
    router_rows = sum(mm(a, b[width : width + lanes], 1, 1) for a, b in zip(h2_rows, branch_all))
    gain_total = sum(x[width + lanes :].astype(F32) for x in branch_all)
    gain_total = gain_total[:gain_lines] + gain_total[gain_lines : 2 * gain_lines]
    gain_part = lax.dynamic_slice_in_dim(
        gain_total.reshape(width), expert_index * row_count, row_count, 0
    )
    rest = jnp.zeros((row_count, LANES - lanes - 1), F32)
    extra = jnp.concatenate([router_rows, gain_part[:, None], rest], 1).astype(BF16)
    extra = extra.reshape(n_context * n_dp, -1, LANES)
    extra, kv_b = hold((extra, kv_b))
    extra = lax.all_to_all(extra, ("context", "dp"), 0, 0, tiled=True)
    extra = jnp.sum(extra.astype(F32), 0)

    grad_query_raw = jnp.concatenate(
        [rotate_t(x, cosine, -sine).astype(BF16) for x in (grad_query_a, grad_query_b)]
    )
    query_sum = comm.scatter_rows(h1_rows, comm.gather_expert(grad_query_raw), width)
    late, pairs, kv_b = hold((crossing[-1], pairs, kv_b))
    totals.append(total_of([late]))
    pairs.append(send_pair(totals[-1][1]))
    kv_sums = [jnp.sum(x.astype(F32), 0) for x in (kv_a, kv_b)]
    grad_key_raw = [rotate_t(kv_sum[0], cosine, -sine).astype(BF16) for kv_sum in kv_sums]
    grad_kv_raw = jnp.concatenate(grad_key_raw + [kv_sum[1].astype(BF16) for kv_sum in kv_sums])
    kv_rows = comm.scatter_rows(h1_rows, comm.gather_expert(grad_kv_raw), 2 * kv_width)
    key_sum, value_sum = kv_rows[:, :kv_width], kv_rows[:, kv_width:]

    down_sum = jnp.concatenate([down for down, _ in totals])
    parts = [both_columns(*pair) for pair in pairs]
    gate_sum = jnp.concatenate([part[:, 0] for part in parts])
    up_sum = jnp.concatenate([part[:, 1] for part in parts])

    shard = (expert_index * n_context + context_index) * n_dp + dp_index
    shard_rows = query_sum.shape[0]

    def shard_of(array):
        return lax.dynamic_slice_in_dim(array, shard * shard_rows, shard_rows, 0).astype(F32)

    gain_sum = (
        jnp.sum(shard_of(w_query) * query_sum, 1)
        + jnp.sum(shard_of(w_key) * key_sum, 1)
        + jnp.sum(shard_of(w_value) * value_sum, 1)
    ) / shard_of(norm_attn)

    grad_normed_attn = mm(w_query, grad_query_raw, 1, 0)
    grad_normed_attn = grad_normed_attn + mm(w_key, grad_kv_raw[:kv_width], 1, 0)
    grad_normed_attn = grad_normed_attn + mm(w_value, grad_kv_raw[kv_width:], 1, 0)
    grad_hidden = grad_middle + norm_back(grad_normed_attn, hidden, scale_attn, gain_attn)
    return (
        result.T[None],
        grad_hidden.astype(BF16).T[None],
        gain_sum,
        query_sum,
        key_sum,
        value_sum,
        out_sum,
        extra[:, lanes],
        extra[:, :all_experts],
        gate_sum,
        up_sum,
        down_sum,
    )


def solution(mesh):
    rows = P(("expert", "dp"), "context", None)
    dense = P(("expert", "context", "dp"), None)
    vector = P(("expert", "context", "dp"))
    experts = P("expert", None, None)
    expert_grads = P("expert", ("context", "dp"), None)
    return jax.shard_map(
        body,
        mesh=mesh,
        in_specs=(rows, rows, rows) + (P(),) * 7 + (experts,) * 3,
        out_specs=(rows, rows, vector, dense, dense, dense, dense, vector, dense)
        + (expert_grads,) * 3,
        check_vma=False,
    )
```

```python
import functools

import jax
import jax.numpy as jnp
from jax import lax
from jax.experimental import pallas as pl
from jax.experimental.pallas import tpu as pltpu
from jax.sharding import PartitionSpec as P

HEADS = 24
KV_HEADS = 8
HEAD_DIM = 64
GROUP = HEADS // KV_HEADS


EPS = 1e-05
ROPE_BASE = 10000.0
NEG_LARGE = -1e30
F32 = jnp.float32
BF16 = jnp.bfloat16
LANES = 128


def cost(flops, bytes_accessed, transcendentals=0):
    scale = 64
    return pl.CostEstimate(
        flops=flops // scale,
        bytes_accessed=bytes_accessed // scale,
        transcendentals=transcendentals // scale,
    )


def rms_scale(values):
    return lax.rsqrt(jnp.mean(values * values, 0, keepdims=True) + EPS)


def norm_back(grad_out, values, scale, gain):
    weighted = gain * grad_out
    return scale * weighted - values * scale**3 * jnp.mean(weighted * values, 0, keepdims=True)


def mm(a, b, da, db):
    return lax.dot_general(a, b, (((da,), (db,)), ((), ())), preferred_element_type=F32)


class Comm:
    def __init__(self):
        self.n_expert = lax.axis_size("expert")
        self.n_context = lax.axis_size("context")
        self.n_dp = lax.axis_size("dp")
        self.cores = 2 if self.n_expert % 2 == 0 else 1
        self.columns = self.n_expert // self.cores
        self.share = 2 if self.n_context % 2 == 0 else 1

    def peer(self, i, k, j):
        column, core = divmod(i, self.cores)
        return ((column + k) % self.columns) * self.cores + (core + j) % self.cores

    def pull(self, value, k, j):
        pairs = [(self.peer(i, k, j), i) for i in range(self.n_expert)]
        return lax.ppermute(value, "expert", pairs)

    def push(self, value, k, j):
        pairs = [(i, self.peer(i, k, j)) for i in range(self.n_expert)]
        return lax.ppermute(value, "expert", pairs)

    def pair(self, value):
        return lax.ppermute(value, "context", [(i, i ^ 1) for i in range(self.n_context)])

    def from_core(self, blocks):
        arrays = [array for block in blocks for _, array, _ in block]
        moved = self.pull(jnp.concatenate(arrays) if len(arrays) > 1 else arrays[0], 0, 1)
        out, at = [], 0
        for block in blocks:
            pieces = []
            for row, array, _ in block:
                pieces.append((row, moved, at))
                at += array.shape[0]
            out.append(pieces)
        return out

    def gather_columns(self, value):
        return [value] + [self.pull(value, k, 0) for k in range(1, self.columns)]

    def gather_cores(self, near):
        if self.cores == 2:
            near = near + [self.pull(block, 0, 1) for block in near]
        return near

    def gather_expert(self, value):
        return self.gather_cores(self.gather_columns(value))

    def gather_group(self, value, beside):
        columns = [self.pull(value, k, 0) for k in range(1, self.columns)]
        far = []
        if self.share == 2:
            half = value.shape[0] // 2
            across = self.pair(value)
            columns, across, beside = lax.optimization_barrier((columns, across, beside))
        first = [[(0, value, 0)]] + [[(0, block, 0)] for block in columns]
        if self.share == 2:
            first.append([(0, across, 0)])
            for k in range(1, self.columns):
                top = self.pull(across[:half], k, 0)
                bottom = self.pair(columns[k - 1][half:])
                far.append([(0, top, 0), (half, bottom, 0)])
        blocks = first + far
        if self.cores == 2:
            blocks = blocks + self.from_core(first)
            blocks = blocks + (self.from_core(far) if far else [])
        return blocks, beside

    def return_hops(self, near, other):
        columns = self.columns
        shape = (self.share, columns) + near.shape[1:]
        arrays = [x.reshape(shape) for x in (near, other) if x is not None]

        def part(*at):
            return sum(array[at].astype(F32) for array in arrays)

        if self.share == 1:
            sent = [self.push(part(0, k).astype(BF16), k, 0) for k in range(1, columns)]
            return [part(0, 0)] + sent
        half = near.shape[1] // 2
        low, high = slice(0, half), slice(half, 2 * half)
        every = slice(None)
        by_column = [
            self.push(part(every, k, low).astype(BF16), k, 0) for k in range(1, columns)
        ]
        by_pair = self.pair(part(1, every, high).astype(BF16))
        return [part(every, 0, low)] + by_column + [part(0, every, high), by_pair]

    def return_last(self, terms):
        columns = self.columns
        if self.share == 1:
            return sum(term.astype(F32) for term in terms)
        top = terms[:columns]
        bottom = terms[columns : columns + 2]

        def total(parts, at):
            return sum(part[at].astype(F32) for part in parts)

        top_other = self.pair(total(top, 1).astype(BF16))
        others = [
            self.push(total(bottom, k).astype(BF16), k, 0).astype(F32)
            for k in range(1, columns)
        ]
        return jnp.concatenate(
            [total(top, 0) + top_other.astype(F32), sum(others, total(bottom, 0))]
        )

    def send_dp(self, parts):
        n = self.n_dp
        return [
            lax.ppermute(parts[s - 1], "dp", [(i, (i + s) % n) for i in range(n)])
            for s in range(1, n)
        ]

    def send_context(self, parts, stride):
        n = self.n_context // stride
        out = []
        for s in range(1, n):
            pairs = []
            for i in range(self.n_context):
                k, r = divmod(i, stride)
                pairs.append((i, ((k + s) % n) * stride + r))
            out.append(lax.ppermute(parts[s - 1], "context", pairs))
        return out

    def scatter_rows(self, left, right, width):
        n, m = self.n_context, self.n_dp
        c, d = lax.axis_index("context"), lax.axis_index("dp")
        size = left[0].shape[0] // (n * m)
        if size % 16 == 0:
            mine, *parts = row_products(jnp.stack([c, d]), left, right, width, n, m)
        else:
            local = sum(mm(a, b[:width], 1, 1) for a, b in zip(left, right))
            local = local.reshape(n, m, size, width)
            local = jnp.stack(
                [lax.dynamic_index_in_dim(local, (c + k) % n, 0, False) for k in range(n)]
            )
            mine, *parts = [
                lax.dynamic_index_in_dim(local, (d + s) % m, 1, False) for s in range(m)
            ]
        came = self.send_dp([part.astype(BF16) for part in parts])

        def of_context(k):
            return mine[k].astype(F32) + sum(x[k].astype(F32) for x in came)

        came_far = self.send_context([of_context(k).astype(BF16) for k in range(1, n)], 1)
        return of_context(0) + sum(x.astype(F32) for x in came_far)


def row_products_kernel(count, place_ref, *refs):
    left, right, outs, total_s = refs[:count], refs[count : 2 * count], refs[2 * count : -1], refs[-1]
    width = total_s.shape[1]
    total_s[...] = mm(
        jnp.concatenate([a[...] for a in left], 1),
        jnp.concatenate([b[:width, :] for b in right], 1),
        1,
        1,
    )
    n, size, _ = outs[0].shape
    m = len(outs)
    for k in range(n):
        for s in range(m):
            owner = lax.rem(place_ref[0] + k, n) * m + lax.rem(place_ref[1] + s, m)
            rows = pl.ds(pl.multiple_of(owner * size, size), size)
            outs[s][k] = total_s[rows, :].astype(outs[s].dtype)


def row_products(place, left, right, width, n, m):
    rows = left[0].shape[0]
    size = rows // (n * m)

    def whole(shape):
        return pl.BlockSpec(shape, lambda i, p: (0,) * len(shape))

    return pl.pallas_call(
        functools.partial(row_products_kernel, len(left)),
        out_shape=tuple(
            jax.ShapeDtypeStruct((n, size, width), BF16 if s else F32) for s in range(m)
        ),
        grid_spec=pltpu.PrefetchScalarGridSpec(
            num_scalar_prefetch=1,
            grid=(1,),
            in_specs=[whole(x.shape) for x in left + right],
            out_specs=tuple(whole((n, size, width)) for _ in range(m)),
            scratch_shapes=[pltpu.VMEM((rows, width), F32)],
        ),
        compiler_params=pltpu.CompilerParams(vmem_limit_bytes=32 << 20),
        cost_estimate=cost(
            flops=2 * rows * width * right[0].shape[1] * len(left),
            bytes_accessed=8 * width * right[0].shape[1] + 6 * rows * width,
        ),
        name="row_products",
    )(place, *left, *right)


def heads_side_by_side(ref):
    hd = HEAD_DIM
    return jnp.concatenate([ref[g * hd : (g + 1) * hd, :] for g in range(GROUP)], 1)


def causal(shape, n):
    key = lax.broadcasted_iota(jnp.int32, shape, 0)
    query = lax.rem(lax.broadcasted_iota(jnp.int32, shape, 1), n)
    return key <= query


def attn_fwd_kernel(blocks, c_ref, q_ref, *refs):
    k_refs, v_refs = refs[:blocks], refs[blocks : 2 * blocks]
    o_ref, ob_ref, lse_ref, scores_ref = refs[2 * blocks :]
    c = c_ref[0]
    n = q_ref.shape[1]
    hd = HEAD_DIM
    queries = heads_side_by_side(q_ref)
    for s in range(blocks):
        rows = slice(s * n, (s + 1) * n)

        def fill(s=s, rows=rows):
            scores = mm(k_refs[s][...], queries, 0, 0)
            if s == 0:
                scores = jnp.where(causal(scores.shape, n), scores, NEG_LARGE)
            scores_ref[rows, :] = scores

        def blank(rows=rows):
            scores_ref[rows, :] = jnp.full((n, GROUP * n), NEG_LARGE, F32)

        if s == 0:
            fill()
        else:
            pl.when(c >= s)(fill)
            pl.when(c < s)(blank)
    lse_ref[...] = jnp.zeros_like(lse_ref)
    for g in range(GROUP):
        cols = slice(g * n, (g + 1) * n)
        scores = scores_ref[:, cols]
        top = jnp.max(scores, 0, keepdims=True)
        weights = jnp.exp(scores - top)
        total = jnp.sum(weights, 0, keepdims=True)
        weights = weights.astype(BF16)
        out = jnp.zeros((hd, n), F32)
        for s in range(blocks):
            out = out + mm(v_refs[s][...], weights[s * n : (s + 1) * n], 1, 0)
        out = out / total
        o_ref[g * hd : (g + 1) * hd, :] = out
        ob_ref[g * hd : (g + 1) * hd, :] = out.astype(BF16)
        lse_ref[0, g : g + 1, :] = top + jnp.log(total)


def kv_specs(blocks, n, first=0):
    keys = [pl.BlockSpec((HEAD_DIM, n), lambda h, c: (first + h, 0))] * blocks
    values = [pl.BlockSpec((HEAD_DIM, n), lambda h, c: (first + h + KV_HEADS, 0))] * blocks
    return keys + values


def attention_forward(context_index, query_t, kv_blocks):
    blocks = len(kv_blocks)
    n = query_t.shape[1]
    wide = GROUP * HEAD_DIM
    heads = query_t.shape[0] // wide
    head = pl.BlockSpec((wide, n), lambda h, c: (h, 0))
    return pl.pallas_call(
        functools.partial(attn_fwd_kernel, blocks),
        out_shape=(
            jax.ShapeDtypeStruct(query_t.shape, F32),
            jax.ShapeDtypeStruct(query_t.shape, BF16),
            jax.ShapeDtypeStruct((heads, 8, n), F32),
        ),
        grid_spec=pltpu.PrefetchScalarGridSpec(
            num_scalar_prefetch=1,
            grid=(heads,),
            in_specs=[head] + kv_specs(blocks, n),
            out_specs=(head, head, pl.BlockSpec((1, 8, n), lambda h, c: (h, 0, 0))),
            scratch_shapes=[pltpu.VMEM((blocks * n, GROUP * n), F32)],
        ),
        compiler_params=pltpu.CompilerParams(vmem_limit_bytes=40 << 20),
        cost_estimate=cost(
            flops=heads * GROUP * blocks * n * n * 256 * 4,
            transcendentals=heads * GROUP * blocks * n * n,
            bytes_accessed=16 * query_t.size,
        ),
        name="attn_fwd",
    )(context_index.reshape(1), query_t, *kv_blocks, *kv_blocks)


def attn_bwd_kernel(blocks, c_ref, q_ref, do_ref, o_ref, lse_ref, *refs):
    k_refs, v_refs = refs[:blocks], refs[blocks : 2 * blocks]
    dq_ref, dkv_ref = refs[2 * blocks :]
    c = c_ref[0]
    n = q_ref.shape[1]
    hd = HEAD_DIM
    queries, grads = heads_side_by_side(q_ref), heads_side_by_side(do_ref)
    deltas, lses = [], []
    for g in range(GROUP):
        head = slice(g * hd, (g + 1) * hd)
        both = do_ref[head, :].astype(F32) * o_ref[head, :]
        deltas.append(jnp.sum(both, 0, keepdims=True))
        lses.append(lse_ref[0, g : g + 1, :])
    delta, lse = jnp.concatenate(deltas, 1), jnp.concatenate(lses, 1)
    for s in range(blocks):

        def work(s=s):
            key_t = k_refs[s][...]
            weights = jnp.exp(mm(key_t, queries, 0, 0) - lse)
            if s == 0:
                weights = jnp.where(causal(weights.shape, n), weights, 0.0)
            grad_weights = mm(v_refs[s][...], grads, 0, 0)
            grad_scores = (weights * (grad_weights - delta)).astype(BF16)
            owner = lax.rem(c - s + blocks, blocks)
            dkv_ref[owner, 0] = mm(queries, grad_scores, 1, 1).astype(BF16)
            dkv_ref[owner, 1] = mm(grads, weights.astype(BF16), 1, 1).astype(BF16)
            step = mm(key_t, grad_scores, 1, 0) * (HEAD_DIM**-0.5)
            for g in range(GROUP):
                head, cols = slice(g * hd, (g + 1) * hd), slice(g * n, (g + 1) * n)
                if s == 0:
                    dq_ref[head, :] = step[:, cols]
                else:
                    dq_ref[head, :] += step[:, cols]

        def skip(s=s):
            owner = lax.rem(c - s + blocks, blocks)
            dkv_ref[owner] = jnp.zeros(dkv_ref.shape[1:], BF16)

        if s == 0:
            work()
        else:
            pl.when(c >= s)(work)
            pl.when(c < s)(skip)


def attention_backward(context_index, query_t, grad_t, out_t, lse, kv_blocks, first, heads):
    blocks = len(kv_blocks)
    n = query_t.shape[1]
    wide = GROUP * HEAD_DIM
    head = pl.BlockSpec((wide, n), lambda h, c: (first + h, 0))
    out = pl.BlockSpec((wide, n), lambda h, c: (h, 0))
    return pl.pallas_call(
        functools.partial(attn_bwd_kernel, blocks),
        out_shape=(
            jax.ShapeDtypeStruct((heads * wide, n), F32),
            jax.ShapeDtypeStruct((blocks, 2, heads * HEAD_DIM, n), BF16),
        ),
        grid_spec=pltpu.PrefetchScalarGridSpec(
            num_scalar_prefetch=1,
            grid=(heads,),
            in_specs=[head, head, head, pl.BlockSpec((1, 8, n), lambda h, c: (first + h, 0, 0))]
            + kv_specs(blocks, n, first),
            out_specs=(
                out,
                pl.BlockSpec((blocks, 2, HEAD_DIM, n), lambda h, c: (0, 0, h, 0)),
            ),
        ),
        compiler_params=pltpu.CompilerParams(vmem_limit_bytes=40 << 20),
        cost_estimate=cost(
            flops=heads * GROUP * blocks * n * n * 256 * 10,
            transcendentals=heads * GROUP * blocks * n * n,
            bytes_accessed=20 * query_t.size,
        ),
        name="attn_bwd",
    )(context_index.reshape(1), query_t, grad_t, out_t, lse, *kv_blocks, *kv_blocks)


def rope_tables(positions):
    half_dim = HEAD_DIM // 2
    frequency = ROPE_BASE ** (-2.0 * jnp.arange(half_dim, dtype=F32) / HEAD_DIM)
    angles = frequency[:, None] * positions.astype(F32)[None, :]
    return jnp.cos(angles), jnp.sin(angles)


def rotate_t(values_t, cosine, sine):
    shaped = values_t.reshape(-1, 2, HEAD_DIM // 2, values_t.shape[1])
    low, high = shaped[:, 0], shaped[:, 1]
    turned = jnp.stack([low * cosine - high * sine, high * cosine + low * sine], 1)
    return turned.reshape(values_t.shape)


def prepare_kernel(p_ref, gate_ref, up_ref, down_ref, *outs):
    in_t_ref, gate_out, up_out, down_out, down_t_out = outs
    gate, up, down = gate_ref[0], up_ref[0], down_ref[0]
    in_t_ref[0, 0, 0] = gate.astype(F32).T.astype(BF16)
    in_t_ref[0, 1, 0] = up.astype(F32).T.astype(BF16)
    gate_out[...] = gate
    up_out[...] = up
    down_out[...] = down
    down_t_out[...] = down.astype(F32).T.astype(BF16)


def prepare_weights(parity, w_gate, w_up, w_down, chunk, share):
    experts, width, hidden = w_gate.shape
    chunks = hidden // chunk // share
    units = chunks * chunk

    def column(e, q, p):
        return (e, 0, q * share + p[0])

    def flat(e, q, p):
        return (0, e * chunks + q)

    return pl.pallas_call(
        prepare_kernel,
        out_shape=(
            jax.ShapeDtypeStruct((experts, 2, chunks, chunk, width), BF16),
            jax.ShapeDtypeStruct((width, experts * units), BF16),
            jax.ShapeDtypeStruct((width, experts * units), BF16),
            jax.ShapeDtypeStruct((experts * units, width), BF16),
            jax.ShapeDtypeStruct((width, experts * units), BF16),
        ),
        grid_spec=pltpu.PrefetchScalarGridSpec(
            num_scalar_prefetch=1,
            grid=(experts, chunks),
            in_specs=[
                pl.BlockSpec((1, width, chunk), column),
                pl.BlockSpec((1, width, chunk), column),
                pl.BlockSpec((1, chunk, width), lambda e, q, p: (e, q * share + p[0], 0)),
            ],
            out_specs=(
                pl.BlockSpec((1, 2, 1, chunk, width), lambda e, q, p: (e, 0, q, 0, 0)),
                pl.BlockSpec((width, chunk), flat),
                pl.BlockSpec((width, chunk), flat),
                pl.BlockSpec((chunk, width), lambda e, q, p: (e * chunks + q, 0)),
                pl.BlockSpec((width, chunk), flat),
            ),
        ),
        compiler_params=pltpu.CompilerParams(vmem_limit_bytes=60 << 20),
        cost_estimate=cost(
            flops=0, transcendentals=0, bytes_accessed=18 * experts * width * units
        ),
        name="prepare_weights",
    )(parity.reshape(1), w_gate, w_up, w_down)


def piece_copies(blocks, refs, target_ref, sems):
    out, at = [], 0
    count = refs[0].shape[1]
    for b, pieces in enumerate(blocks):
        copies = []
        for i, (first, ref, row) in enumerate(pieces):
            last = pieces[i + 1][0] if i + 1 < len(pieces) else target_ref.shape[0]
            copies.append(
                pltpu.make_async_copy(
                    refs[ref].at[row : row + last - first],
                    target_ref.at[first:last, b * count : (b + 1) * count],
                    sems.at[at],
                )
            )
            at += 1
        out.append(copies)
    return out


def write_grads(rows_ref, cots_ref, act, dgate, dup, place_ref, outs, down_s, in_s, share):
    owners = len(outs)
    chunks, _, _, units = outs[0].shape
    width = rows_ref.shape[0]
    size = units // chunks // owners
    tiles = width // units

    def place(k, s):
        return lax.rem(place_ref[2] + k, chunks), lax.rem(place_ref[1] + s, owners)

    down_s[...] = mm(act, cots_ref[...], 1, 1).astype(BF16)
    for k in range(chunks):
        for s in range(owners):
            at_k, at_d = place(k, s)
            start = pl.multiple_of((at_k * owners + at_d) * size, size)
            for t in range(tiles):
                outs[s][k, 0, t * size : (t + 1) * size, :] = down_s[
                    pl.ds(start, size), t * units : (t + 1) * units
                ]
    base = tiles * size
    size = width // (chunks * share * owners)
    for grad_act in (dgate, dup):
        in_s[...] = mm(rows_ref[...], grad_act, 1, 1).astype(BF16)
        for k in range(chunks):
            for q in range(share):
                for s in range(owners):
                    at_k, at_d = place(k, s)
                    start = pl.multiple_of(((at_k * share + q) * owners + at_d) * size, size)
                    to = base + q * size
                    outs[s][k, 0, to : to + size, :] = in_s[pl.ds(start, size), :]
        base += share * size


class Experts:
    def __init__(self, rows, cots, width, units, share, chunks, owners):
        self.arrays, self.plans = [], []
        for blocks in (rows, cots):
            arrays, plan = [], []
            for block in blocks:
                pieces = []
                for first, array, row in block:
                    known = [i for i, x in enumerate(arrays) if x is array]
                    if not known:
                        arrays.append(array)
                    pieces.append((first, known[0] if known else len(arrays) - 1, row))
                plan.append(pieces)
            self.arrays.append(arrays)
            self.plans.append(plan)
        self.blocks = len(rows)
        self.width, self.count = width, rows[0][0][1].shape[1]
        self.tokens = self.blocks * self.count
        self.units, self.share, self.chunks, self.owners = units, share, chunks, owners
        self.height = self.width // chunks // owners * 3

    def n_arrays(self):
        return sum(map(len, self.arrays))

    def scratch(self):
        wide = pltpu.VMEM((self.width, self.tokens), BF16)
        sems = [pltpu.SemaphoreType.DMA((sum(map(len, plan)),)) for plan in self.plans]
        return [wide, wide] + sems

    def copies(self, refs, rows_ref, cots_ref, row_sems, cot_sems):
        n = len(self.arrays[0])
        row_copies = piece_copies(self.plans[0], refs[:n], rows_ref, row_sems)
        cot_copies = piece_copies(self.plans[1], refs[n:], cots_ref, cot_sems)
        return [a + b for a, b in zip(row_copies, cot_copies)]

    def grads_structs(self, n):
        shape = (self.chunks, n, self.height, self.units)
        spec = pl.BlockSpec(
            (self.chunks, 1, self.height, self.units), lambda i, *_: (0, i, 0, 0)
        )
        return [jax.ShapeDtypeStruct(shape, BF16)] * self.owners, [spec] * self.owners

    def act_kernel(self, first, n, make_gates, e_ref, *refs):
        n_arrays = self.n_arrays()
        kept_ref, scales_ref, in_t_ref, down_ref = refs[:4]
        piece_refs, outs, scratch = refs[4 : 4 + n_arrays], refs[4 + n_arrays : -6], refs[-6:]
        if make_gates:
            chosen_ref = scales_ref
            gates_ref, scales_ref = outs[:2]
            outs = outs[2:]
        act_ref, dgate_ref, dup_ref, dscale_ref = outs[:4]
        rows_ref, cots_ref = scratch[:2]
        units, count, blocks = self.units, self.count, self.blocks
        copies = self.copies(piece_refs, *scratch[:4])
        step = pl.program_id(0)
        row = e_ref[0] + first + step

        def move(wait, start):
            def run():
                for b in start:
                    for copy in copies[b]:
                        copy.start()
                for copy in copies[wait]:
                    copy.wait()

            if n == 1:
                run()
            else:
                pl.when(step == 0)(run)

        def products(b):
            move(b, range(blocks) if b == 0 else ())
            cols = slice(b * count, (b + 1) * count)
            acts = jnp.dot(in_t_ref[...], rows_ref[:, cols], preferred_element_type=F32)
            grad = jnp.dot(down_ref[...], cots_ref[:, cols], preferred_element_type=F32)
            return acts, grad

        def finish(b, acts, grad):
            cols = slice(b * count, (b + 1) * count)
            gate, up = acts[:units], acts[units : 2 * units]
            if make_gates:
                chosen = chosen_ref[:, cols] > 0
                logits = jnp.where(chosen, acts[2 * units :], NEG_LARGE)
                gates = jnp.exp(logits - jnp.max(logits, 0, keepdims=True))
                gates = jnp.where(chosen, gates, 0.0)
                gates = gates / jnp.sum(gates, 0, keepdims=True)
                gates_ref[:, cols] = gates
                scales_ref[:, cols] = gates * kept_ref[:, cols]
            scale = scales_ref[pl.ds(row, 1), cols]
            keep = kept_ref[pl.ds(row, 1), cols]
            sigmoid = jax.nn.sigmoid(gate)
            silu = gate * sigmoid
            hidden = silu * up
            dscale_ref[0, 0:1, cols] = keep * jnp.sum(hidden * grad, 0, keepdims=True)
            act_ref[:, cols] = (hidden * scale).astype(BF16)
            grad = grad * scale
            dup_ref[:, cols] = (grad * silu).astype(BF16)
            dgate_ref[:, cols] = (grad * up * (sigmoid + silu * (1.0 - sigmoid))).astype(BF16)

        dscale_ref[...] = jnp.zeros_like(dscale_ref)
        for b in range(blocks):
            finish(b, *products(b))
        write_grads(
            rows_ref,
            cots_ref,
            act_ref[...],
            dgate_ref[...],
            dup_ref[...],
            e_ref,
            outs[4:],
            *scratch[4:],
            self.share,
        )

    def act(self, places, first, n, kept, scales, in_t, down, make_gates=False):
        units, width, tokens = self.units, self.width, self.tokens
        lanes = kept.shape[0]
        in_rows = 2 * units + (lanes if make_gates else 0)
        table = pl.BlockSpec((lanes, tokens), lambda i, e: (0, 0))
        one = pl.BlockSpec((units, tokens), lambda i, e: (i, 0))
        outs, specs = [], []
        if make_gates:
            outs += [jax.ShapeDtypeStruct((lanes, tokens), F32)] * 2
            specs += [table] * 2
        outs += [jax.ShapeDtypeStruct((n * units, tokens), BF16)] * 3
        specs += [one] * 3
        outs.append(jax.ShapeDtypeStruct((n, 8, tokens), F32))
        specs.append(pl.BlockSpec((1, 8, tokens), lambda i, e: (i, 0, 0)))
        structs, grad_specs = self.grads_structs(n)
        extra = [pltpu.VMEM((units, width), BF16), pltpu.VMEM((width, units), BF16)]
        return pl.pallas_call(
            functools.partial(self.act_kernel, first, n, make_gates),
            out_shape=tuple(outs + structs),
            grid_spec=pltpu.PrefetchScalarGridSpec(
                num_scalar_prefetch=1,
                grid=(n,),
                in_specs=[
                    table,
                    table,
                    pl.BlockSpec((in_rows, width), lambda i, e: (first + i, 0)),
                    pl.BlockSpec((units, width), lambda i, e: (first + i, 0)),
                ]
                + [pl.BlockSpec(memory_space=pl.ANY)] * self.n_arrays(),
                out_specs=tuple(specs + grad_specs),
                scratch_shapes=self.scratch() + extra,
            ),
            compiler_params=pltpu.CompilerParams(vmem_limit_bytes=60 << 20),
            cost_estimate=cost(
                flops=12 * width * units * tokens * n,
                transcendentals=units * tokens * n,
                bytes_accessed=4 * width * tokens + 6 * n * units * (width + tokens),
            ),
            name="experts_act",
        )(places, kept, scales, in_t, down, *self.arrays[0], *self.arrays[1])

    def out_kernel(self, parts, e_ref, weight_ref, *refs):
        act_refs, dscale_refs = refs[:parts], refs[parts : 2 * parts]
        message_ref, act_s, dscale_s = refs[2 * parts :]
        at = row = 0
        dscale_s[...] = jnp.zeros_like(dscale_s)
        for act_ref, dscale_ref in zip(act_refs, dscale_refs):
            act_s[at : at + act_ref.shape[0], :] = act_ref[...]
            at += act_ref.shape[0]
            for i in range(dscale_ref.shape[0]):
                dscale_s[pl.ds(e_ref[0] + row, 1), :] = dscale_ref[i, 0:1, :]
                row += 1
        width, lanes = self.width, dscale_s.shape[0]
        message_ref[0, :width, :] = jnp.dot(
            weight_ref[...], act_s[...], preferred_element_type=F32
        ).astype(BF16)
        grads = dscale_s[...]
        high = grads.astype(BF16)
        message_ref[0, width : width + lanes, :] = high
        message_ref[0, width + lanes :, :] = (grads - high.astype(F32)).astype(BF16)

    def out(self, places, lanes, weight, acts, dscales, first_block, n_blocks):
        rows = weight.shape[1]
        parts = len(acts)
        width, count = self.width, self.count

        def column(shape):
            return pl.BlockSpec(
                shape, lambda b, e: (0,) * (len(shape) - 1) + (first_block + b,)
            )

        return pl.pallas_call(
            functools.partial(self.out_kernel, parts),
            out_shape=jax.ShapeDtypeStruct((n_blocks, width + 2 * lanes, count), BF16),
            grid_spec=pltpu.PrefetchScalarGridSpec(
                num_scalar_prefetch=1,
                grid=(n_blocks,),
                in_specs=[
                    pl.BlockSpec(
                        (width, rows),
                        lambda b, e: (0, 0),
                        pipeline_mode=pl.Buffered(buffer_count=1),
                    )
                ]
                + [column((a.shape[0], count)) for a in acts]
                + [column((a.shape[0], 8, count)) for a in dscales],
                out_specs=pl.BlockSpec((1, width + 2 * lanes, count), lambda b, e: (b, 0, 0)),
                scratch_shapes=[pltpu.VMEM((rows, count), BF16), pltpu.VMEM((lanes, count), F32)],
            ),
            compiler_params=pltpu.CompilerParams(vmem_limit_bytes=60 << 20),
            cost_estimate=cost(
                flops=2 * width * rows * count * n_blocks,
                transcendentals=0,
                bytes_accessed=2 * width * rows + 4 * width * count * n_blocks,
            ),
            name="experts_out",
        )(places, weight, *acts, *dscales)

    def back_kernel(self, parts, gate_w_ref, up_w_ref, *refs):
        dgate_refs, dup_refs = refs[:parts], refs[parts : 2 * parts]
        back_ref, dgate_s, dup_s = refs[2 * parts :]
        for target, pieces in ((dgate_s, dgate_refs), (dup_s, dup_refs)):
            at = 0
            for piece in pieces:
                target[at : at + piece.shape[0], :] = piece[...]
                at += piece.shape[0]
        back = jnp.dot(gate_w_ref[...], dgate_s[...], preferred_element_type=F32)
        back = back + jnp.dot(up_w_ref[...], dup_s[...], preferred_element_type=F32)
        back_ref[0] = back.astype(BF16)

    def back(self, gate_w, up_w, dgates, dups, first_block, n_blocks):
        width, count = self.width, self.count
        rows = gate_w.shape[1]
        parts = len(dgates)
        whole = pl.BlockSpec(
            (width, rows), lambda b: (0, 0), pipeline_mode=pl.Buffered(buffer_count=1)
        )
        column = [pl.BlockSpec((a.shape[0], count), lambda b: (0, first_block + b)) for a in dgates]
        return pl.pallas_call(
            functools.partial(self.back_kernel, parts),
            out_shape=jax.ShapeDtypeStruct((n_blocks, width, count), BF16),
            grid=(n_blocks,),
            in_specs=[whole, whole] + column * 2,
            out_specs=pl.BlockSpec((1, width, count), lambda b: (b, 0, 0)),
            scratch_shapes=[pltpu.VMEM((rows, count), BF16)] * 2,
            compiler_params=pltpu.CompilerParams(vmem_limit_bytes=60 << 20),
            cost_estimate=cost(
                flops=4 * width * rows * count * n_blocks,
                transcendentals=0,
                bytes_accessed=4 * width * rows + 4 * width * count * n_blocks,
            ),
            name="experts_back",
        )(gate_w, up_w, *dgates, *dups)


def body(
    tokens,
    routes,
    cotangent,
    norm_attn,
    w_query,
    w_key,
    w_value,
    w_out,
    norm_ffn,
    w_router,
    w_gate,
    w_up,
    w_down,
):
    comm = Comm()
    hold = lax.optimization_barrier
    count, width = tokens.shape[1], tokens.shape[2]
    top_k = routes.shape[2]
    n_experts, _, hidden_units = w_gate.shape
    all_experts = n_experts * comm.n_expert
    capacity = (9 * count * top_k + 8 * all_experts - 1) // (8 * all_experts)
    n_context, n_dp, share = comm.n_context, comm.n_dp, comm.share
    expert_index = lax.axis_index("expert")
    context_index = lax.axis_index("context")
    dp_index = lax.axis_index("dp")
    parity = context_index % share
    chunks = n_context // share
    units = hidden_units // share
    lanes = -(-all_experts // 32) * 32
    places = jnp.stack([expert_index * n_experts, dp_index, context_index // share])

    cot_t = cotangent[0].T
    routed = (
        routes[0].T[:, None, :] == jnp.arange(lanes, dtype=jnp.int32)[None, :, None]
    ).astype(F32)
    cot_message = jnp.concatenate([cot_t, routed.sum(0).astype(BF16)])
    tokens, cot_message = hold((tokens, cot_message))
    across = [comm.pair(cot_message)] if share == 2 else []
    cots = [cot_message] + [comm.pull(cot_message, k, 0) for k in range(1, comm.columns)]

    hidden = tokens[0].T.astype(F32)
    gain_attn = norm_attn.astype(F32)[:, None]
    gain_ffn = norm_ffn.astype(F32)[:, None]
    scale_attn = rms_scale(hidden)
    normed_attn = (hidden * scale_attn * gain_attn).astype(BF16)
    positions = context_index * count + jnp.arange(count, dtype=jnp.int32)
    cosine, sine = rope_tables(positions)
    key_t = rotate_t(mm(w_key, normed_attn, 0, 0), cosine, sine).astype(BF16)
    value_t = mm(w_value, normed_attn, 0, 0).astype(BF16)
    kv_width = key_t.shape[0]
    kv_own = jnp.concatenate([key_t, value_t], 0)
    kv_blocks = [kv_own]
    for s in range(1, n_context):
        pairs = [(i, i + s) for i in range(n_context - s)]
        kv_blocks.append(lax.ppermute(kv_own, "context", pairs))
    query_t = rotate_t(mm(w_query, normed_attn, 0, 0), cosine, sine)
    query_t = (query_t * HEAD_DIM**-0.5).astype(BF16)

    weights = prepare_weights(parity, w_gate, w_up, w_down, hidden_units // n_context, share)
    router_t = jnp.zeros((lanes, width), BF16).at[:all_experts].set(w_router.T)
    in_t, gate_w, up_w, down, down_t = weights
    in_t = in_t.reshape(n_experts * 2 * units, width)
    in_first = jnp.concatenate([in_t[: 2 * units], router_t])
    if across:
        across, in_t, in_first = hold((across, in_t, in_first))
        across = across + [comm.pull(across[0], k, 0) for k in range(1, comm.columns)]
        cots, across[0], in_t = hold((cots, across[0], in_t))
    cots, across = [[[(0, x, 0)] for x in part] for part in (cots, across)]
    others = comm.from_core(cots) if comm.cores == 2 else []
    kv_blocks, in_t, in_first, gate_w, up_w, down, down_t = hold(
        (kv_blocks, in_t, in_first, gate_w, up_w, down, down_t)
    )
    out_t, out_low, lse = attention_forward(context_index, query_t, kv_blocks)
    middle = hidden + mm(w_out, out_low, 0, 0)
    scale_ffn = rms_scale(middle)
    normed_ffn = (middle * scale_ffn * gain_ffn).astype(BF16)
    across = [block[0][1] for block in across]
    across, normed_ffn = hold((across, normed_ffn))
    rows, across = comm.gather_group(normed_ffn, across)
    across = [[(0, x, 0)] for x in across]
    if comm.cores == 2 and across:
        others = others + comm.from_core(across)
    cots = cots + across + others

    routed_all = jnp.concatenate(
        [block[0][1][block[0][2] + width : block[0][2] + width + lanes] for block in cots]
    )
    n_blocks = len(cots)
    before = jnp.triu(jnp.ones((count, count), BF16), 1)
    ranking = mm(routed_all, before, 1, 0)
    chosen = routed_all.astype(F32)
    kept = jnp.where(ranking < capacity, chosen, 0.0)

    def side_by_side(array):
        array = array.reshape(n_blocks, lanes, count)
        return jnp.concatenate([array[b] for b in range(n_blocks)], 1)

    chosen, kept = side_by_side(chosen), side_by_side(kept)

    row_count = width // comm.n_expert

    def for_experts(*arrays):
        out = []
        for j in range(comm.cores):
            for k in range(comm.columns):
                column, core = expert_index // comm.cores, expert_index % comm.cores
                column = (column - k) % comm.columns
                target = column * comm.cores + (core + j) % comm.cores
                pieces = [
                    lax.dynamic_slice_in_dim(array, target * row_count, row_count, 0)
                    for array in arrays
                ]
                out.append(jnp.concatenate(pieces))
        return out

    def to_experts(pieces):
        peers = [(j, k) for j in range(comm.cores) for k in range(comm.columns)]
        return pieces[:1] + [comm.pull(x, k, j) for x, (j, k) in zip(pieces[1:], peers[1:])]

    columns_sent = for_experts(normed_attn, out_low)
    chosen, columns_sent = hold((chosen, columns_sent))

    own = Experts(rows, cots, width, units, share, chunks, n_dp)
    groups, at = [], 0
    for n in (1, (n_experts - 1) // 2, n_experts - 1 - (n_experts - 1) // 2):
        if n:
            groups.append((at, n))
            at += n
    acts, dgates, dups, dscales, kept_parts, arrived, crossing = ([] for _ in range(7))
    scales = None

    def pass_on(g, values):
        if g >= len(groups):
            return values
        terms, values = hold((arrived[g], values))
        terms = [kept_parts[g]] + terms

        def part(k):
            return sum(term[k].astype(F32) for term in terms)

        sent = comm.send_context([part(k).astype(BF16) for k in range(1, chunks)], share)
        crossing.append([part(0).astype(BF16)] + sent)
        return values

    for g, (first, n) in enumerate(groups):
        if g == 0:
            gates_all, scales, *done = own.act(
                places, first, n, kept, chosen, in_first, down, make_gates=True
            )
        else:
            done = own.act(places, first, n, kept, scales, in_t, down)
        for target, value in zip((acts, dgates, dups, dscales, kept_parts), done):
            target.append(value)
        arrived.append(comm.send_dp(done[5:]))
        if g == 0:
            scales, columns_sent = hold((scales, columns_sent))
            columns_got = to_experts(columns_sent)
        if g == 1:
            scales = pass_on(0, scales)

    columns_got, acts = hold((columns_got, acts))
    h1_rows = [x[:row_count] for x in columns_got]
    ob_rows = [x[row_count:] for x in columns_got]
    near_count = n_blocks // comm.cores

    def both_cores(call):
        other = None
        if comm.cores == 2:
            other = comm.push(call(near_count, near_count), 0, 1)
        return call(0, near_count), other

    message = both_cores(
        lambda first, n: own.out(places, lanes, down_t, acts, dscales, first, n)
    )
    back_other = None
    if comm.cores == 2:
        back_other = own.back(gate_w, up_w, dgates, dups, near_count, near_count)
        back_other = comm.push(back_other, 0, 1)
    message, dgates = hold((message, dgates))
    dgates, crossing[0] = pass_on(1, (dgates, crossing[0]))
    back_near = own.back(gate_w, up_w, dgates, dups, 0, near_count)
    message = comm.return_hops(*message)
    message, back_near = hold((message, back_near))
    back = comm.return_hops(back_near, back_other)
    returned = comm.return_last(message)
    back = pass_on(2, back)
    grad_normed_ffn = comm.return_last(back)
    result = (middle + returned[:width]).astype(BF16)
    grad_gates = returned[width : width + lanes] + returned[width + lanes :]
    gates_own = gates_all[:, :count]

    upstream = cot_t.astype(F32)
    mean_grad = jnp.sum(gates_own * grad_gates, 0, keepdims=True)
    grad_logits = (gates_own * (grad_gates - mean_grad)).astype(BF16)
    grad_normed_ffn = grad_normed_ffn + mm(router_t, grad_logits, 0, 0)
    grad_gain_ffn = jnp.sum(grad_normed_ffn * middle * scale_ffn, 1)
    grad_middle = upstream + norm_back(grad_normed_ffn, middle, scale_ffn, gain_ffn)
    grad_branch = grad_middle.astype(BF16)

    gain_grid = grad_gain_ffn.reshape(-1, count)
    gain_lines = gain_grid.shape[0]
    gain_high = lax.reduce_precision(gain_grid, 8, 7)
    gain_rows = jnp.concatenate([gain_high, gain_grid - gain_high]).astype(BF16)
    gain_rows = jnp.pad(gain_rows, ((0, -2 * gain_lines % 16), (0, 0)))
    branch_all = comm.gather_columns(jnp.concatenate([grad_branch, grad_logits, gain_rows]))
    grad_attn_t = mm(w_out, grad_branch, 1, 0).astype(BF16)

    def attention_half(first, heads):
        return attention_backward(
            context_index, query_t, grad_attn_t, out_t, lse, kv_blocks, first, heads
        )

    def to_keys(grad_kv):
        return lax.all_to_all(grad_kv, "context", 0, 0, tiled=True)

    size_down = units // chunks // n_dp
    tiles = width // units

    def total_of(terms):
        total = jnp.concatenate([sum(x.astype(F32) for x in group) for group in terms])
        n = total.shape[0]
        part = total[:, : tiles * size_down].reshape(n, tiles, size_down, units)
        down = jnp.swapaxes(part, 1, 2).reshape(n, size_down, width)
        part = total[:, tiles * size_down :]
        return down, part.reshape(n, 2, share, part.shape[1] // 2 // share, units)

    def send_pair(part):
        if share == 1:
            return part[:, :, 0], None
        keep = lax.dynamic_index_in_dim(part, parity, 2, False)
        send = lax.dynamic_index_in_dim(part, 1 - parity, 2, False)
        return keep, comm.pair(send.astype(BF16))

    def both_columns(keep, other):
        if other is None:
            return keep
        other = other.astype(F32)
        first = jnp.where(parity == 0, keep, other)
        second = jnp.where(parity == 0, other, keep)
        chunk = hidden_units // n_context
        pieces = []
        for q in range(chunks):
            pieces += [x[..., q * chunk : (q + 1) * chunk] for x in (first, second)]
        return jnp.concatenate(pieces, -1)

    early = crossing[:-1]
    early, grad_attn_t = hold((early, grad_attn_t))
    totals = [total_of(early)] if early else []
    pairs = [send_pair(part) for _, part in totals]
    half = KV_HEADS // 2
    grad_query_a, grad_kv_a = attention_half(0, half)
    kv_a = to_keys(grad_kv_a)
    branch_all, grad_attn_t = hold((branch_all, grad_attn_t))
    branch_all = comm.gather_cores(branch_all)
    grad_query_b, grad_kv_b = attention_half(half, half)
    kv_a, grad_kv_b, branch_all, crossing[-1] = hold((kv_a, grad_kv_b, branch_all, crossing[-1]))
    kv_b = to_keys(grad_kv_b)

    out_sum = comm.scatter_rows(ob_rows, branch_all, width)
    h2_rows = [
        lax.dynamic_slice_in_dim(array, at + expert_index * row_count, row_count, 0)
        for j in range(comm.cores)
        for ((_, array, at),) in rows[j * near_count : j * near_count + comm.columns]
    ]
    router_rows = sum(mm(a, b[width : width + lanes], 1, 1) for a, b in zip(h2_rows, branch_all))
    gain_total = sum(x[width + lanes :].astype(F32) for x in branch_all)
    gain_total = gain_total[:gain_lines] + gain_total[gain_lines : 2 * gain_lines]
    gain_part = lax.dynamic_slice_in_dim(
        gain_total.reshape(width), expert_index * row_count, row_count, 0
    )
    rest = jnp.zeros((row_count, LANES - lanes - 1), F32)
    extra = jnp.concatenate([router_rows, gain_part[:, None], rest], 1).astype(BF16)
    extra = extra.reshape(n_context * n_dp, -1, LANES)
    extra, kv_b = hold((extra, kv_b))
    extra = lax.all_to_all(extra, ("context", "dp"), 0, 0, tiled=True)
    extra = jnp.sum(extra.astype(F32), 0)

    grad_query_raw = jnp.concatenate(
        [rotate_t(x, cosine, -sine).astype(BF16) for x in (grad_query_a, grad_query_b)]
    )
    query_sum = comm.scatter_rows(h1_rows, comm.gather_expert(grad_query_raw), width)
    late, pairs, kv_b = hold((crossing[-1], pairs, kv_b))
    totals.append(total_of([late]))
    pairs.append(send_pair(totals[-1][1]))
    kv_sums = [jnp.sum(x.astype(F32), 0) for x in (kv_a, kv_b)]
    grad_key_raw = [rotate_t(kv_sum[0], cosine, -sine).astype(BF16) for kv_sum in kv_sums]
    grad_kv_raw = jnp.concatenate(grad_key_raw + [kv_sum[1].astype(BF16) for kv_sum in kv_sums])
    kv_rows = comm.scatter_rows(h1_rows, comm.gather_expert(grad_kv_raw), 2 * kv_width)
    key_sum, value_sum = kv_rows[:, :kv_width], kv_rows[:, kv_width:]

    down_sum = jnp.concatenate([down for down, _ in totals])
    parts = [both_columns(*pair) for pair in pairs]
    gate_sum = jnp.concatenate([part[:, 0] for part in parts])
    up_sum = jnp.concatenate([part[:, 1] for part in parts])

    shard = (expert_index * n_context + context_index) * n_dp + dp_index
    shard_rows = query_sum.shape[0]

    def shard_of(array):
        return lax.dynamic_slice_in_dim(array, shard * shard_rows, shard_rows, 0).astype(F32)

    gain_sum = (
        jnp.sum(shard_of(w_query) * query_sum, 1)
        + jnp.sum(shard_of(w_key) * key_sum, 1)
        + jnp.sum(shard_of(w_value) * value_sum, 1)
    ) / shard_of(norm_attn)

    grad_normed_attn = mm(w_query, grad_query_raw, 1, 0)
    grad_normed_attn = grad_normed_attn + mm(w_key, grad_kv_raw[:kv_width], 1, 0)
    grad_normed_attn = grad_normed_attn + mm(w_value, grad_kv_raw[kv_width:], 1, 0)
    grad_hidden = grad_middle + norm_back(grad_normed_attn, hidden, scale_attn, gain_attn)
    return (
        result.T[None],
        grad_hidden.astype(BF16).T[None],
        gain_sum,
        query_sum,
        key_sum,
        value_sum,
        out_sum,
        extra[:, lanes],
        extra[:, :all_experts],
        gate_sum,
        up_sum,
        down_sum,
    )


def solution(mesh):
    rows = P(("expert", "dp"), "context", None)
    dense = P(("expert", "context", "dp"), None)
    vector = P(("expert", "context", "dp"))
    experts = P("expert", None, None)
    expert_grads = P("expert", ("context", "dp"), None)
    return jax.shard_map(
        body,
        mesh=mesh,
        in_specs=(rows, rows, rows) + (P(),) * 7 + (experts,) * 3,
        out_specs=(rows, rows, vector, dense, dense, dense, dense, vector, dense)
        + (expert_grads,) * 3,
        check_vma=False,
    )
```

```python
import functools

import jax
import jax.numpy as jnp
from jax import lax
from jax.experimental import pallas as pl
from jax.experimental.pallas import tpu as pltpu
from jax.sharding import PartitionSpec as P

HEADS = 24
KV_HEADS = 8
HEAD_DIM = 64
GROUP = HEADS // KV_HEADS


EPS = 1e-05
ROPE_BASE = 10000.0
NEG_LARGE = -1e30
F32 = jnp.float32
BF16 = jnp.bfloat16
LANES = 128


def cost(flops, bytes_accessed, transcendentals=0):
    scale = 64
    return pl.CostEstimate(
        flops=flops // scale,
        bytes_accessed=bytes_accessed // scale,
        transcendentals=transcendentals // scale,
    )


def rms_scale(values):
    return lax.rsqrt(jnp.mean(values * values, 0, keepdims=True) + EPS)


def norm_back(grad_out, values, scale, gain):
    weighted = gain * grad_out
    return scale * weighted - values * scale**3 * jnp.mean(weighted * values, 0, keepdims=True)


def mm(a, b, da, db):
    return lax.dot_general(a, b, (((da,), (db,)), ((), ())), preferred_element_type=F32)


class Comm:
    def __init__(self):
        self.n_expert = lax.axis_size("expert")
        self.n_context = lax.axis_size("context")
        self.n_dp = lax.axis_size("dp")
        self.cores = 2 if self.n_expert % 2 == 0 else 1
        self.columns = self.n_expert // self.cores
        self.share = 2 if self.n_context % 2 == 0 else 1

    def peer(self, i, k, j):
        column, core = divmod(i, self.cores)
        return ((column + k) % self.columns) * self.cores + (core + j) % self.cores

    def pull(self, value, k, j):
        pairs = [(self.peer(i, k, j), i) for i in range(self.n_expert)]
        return lax.ppermute(value, "expert", pairs)

    def push(self, value, k, j):
        pairs = [(i, self.peer(i, k, j)) for i in range(self.n_expert)]
        return lax.ppermute(value, "expert", pairs)

    def pair(self, value):
        return lax.ppermute(value, "context", [(i, i ^ 1) for i in range(self.n_context)])

    def from_core(self, blocks):
        arrays = [array for block in blocks for _, array, _ in block]
        moved = self.pull(jnp.concatenate(arrays) if len(arrays) > 1 else arrays[0], 0, 1)
        out, at = [], 0
        for block in blocks:
            pieces = []
            for row, array, _ in block:
                pieces.append((row, moved, at))
                at += array.shape[0]
            out.append(pieces)
        return out

    def gather_columns(self, value):
        return [value] + [self.pull(value, k, 0) for k in range(1, self.columns)]

    def gather_cores(self, near):
        if self.cores == 2:
            near = near + [self.pull(block, 0, 1) for block in near]
        return near

    def gather_expert(self, value):
        return self.gather_cores(self.gather_columns(value))

    def gather_group(self, value, beside):
        columns = [self.pull(value, k, 0) for k in range(1, self.columns)]
        far = []
        if self.share == 2:
            half = value.shape[0] // 2
            across = self.pair(value)
            columns, across, beside = lax.optimization_barrier((columns, across, beside))
        first = [[(0, value, 0)]] + [[(0, block, 0)] for block in columns]
        if self.share == 2:
            first.append([(0, across, 0)])
            for k in range(1, self.columns):
                top = self.pull(across[:half], k, 0)
                bottom = self.pair(columns[k - 1][half:])
                far.append([(0, top, 0), (half, bottom, 0)])
        blocks = first + far
        if self.cores == 2:
            blocks = blocks + self.from_core(first)
            blocks = blocks + (self.from_core(far) if far else [])
        return blocks, beside

    def return_hops(self, near, other):
        columns = self.columns
        shape = (self.share, columns) + near.shape[1:]
        arrays = [x.reshape(shape) for x in (near, other) if x is not None]

        def part(*at):
            return sum(array[at].astype(F32) for array in arrays)

        if self.share == 1:
            sent = [self.push(part(0, k).astype(BF16), k, 0) for k in range(1, columns)]
            return [part(0, 0)] + sent
        half = near.shape[1] // 2
        low, high = slice(0, half), slice(half, 2 * half)
        every = slice(None)
        by_column = [
            self.push(part(every, k, low).astype(BF16), k, 0) for k in range(1, columns)
        ]
        by_pair = self.pair(part(1, every, high).astype(BF16))
        return [part(every, 0, low)] + by_column + [part(0, every, high), by_pair]

    def return_last(self, terms):
        columns = self.columns
        if self.share == 1:
            return sum(term.astype(F32) for term in terms)
        top = terms[:columns]
        bottom = terms[columns : columns + 2]

        def total(parts, at):
            return sum(part[at].astype(F32) for part in parts)

        top_other = self.pair(total(top, 1).astype(BF16))
        others = [
            self.push(total(bottom, k).astype(BF16), k, 0).astype(F32)
            for k in range(1, columns)
        ]
        return jnp.concatenate(
            [total(top, 0) + top_other.astype(F32), sum(others, total(bottom, 0))]
        )

    def send_dp(self, parts):
        n = self.n_dp
        return [
            lax.ppermute(parts[s - 1], "dp", [(i, (i + s) % n) for i in range(n)])
            for s in range(1, n)
        ]

    def send_context(self, parts, stride):
        n = self.n_context // stride
        out = []
        for s in range(1, n):
            pairs = []
            for i in range(self.n_context):
                k, r = divmod(i, stride)
                pairs.append((i, ((k + s) % n) * stride + r))
            out.append(lax.ppermute(parts[s - 1], "context", pairs))
        return out

    def scatter_rows(self, left, right, width):
        n, m = self.n_context, self.n_dp
        c, d = lax.axis_index("context"), lax.axis_index("dp")
        size = left[0].shape[0] // (n * m)
        if size % 16 == 0:
            mine, *parts = row_products(jnp.stack([c, d]), left, right, width, n, m)
        else:
            local = sum(mm(a, b[:width], 1, 1) for a, b in zip(left, right))
            local = local.reshape(n, m, size, width)
            local = jnp.stack(
                [lax.dynamic_index_in_dim(local, (c + k) % n, 0, False) for k in range(n)]
            )
            mine, *parts = [
                lax.dynamic_index_in_dim(local, (d + s) % m, 1, False) for s in range(m)
            ]
        came = self.send_dp([part.astype(BF16) for part in parts])

        def of_context(k):
            return mine[k].astype(F32) + sum(x[k].astype(F32) for x in came)

        came_far = self.send_context([of_context(k).astype(BF16) for k in range(1, n)], 1)
        return of_context(0) + sum(x.astype(F32) for x in came_far)


def row_products_kernel(count, place_ref, *refs):
    left, right, outs, total_s = refs[:count], refs[count : 2 * count], refs[2 * count : -1], refs[-1]
    width = total_s.shape[1]
    total_s[...] = mm(
        jnp.concatenate([a[...] for a in left], 1),
        jnp.concatenate([b[:width, :] for b in right], 1),
        1,
        1,
    )
    n, size, _ = outs[0].shape
    m = len(outs)
    for k in range(n):
        for s in range(m):
            owner = lax.rem(place_ref[0] + k, n) * m + lax.rem(place_ref[1] + s, m)
            rows = pl.ds(pl.multiple_of(owner * size, size), size)
            outs[s][k] = total_s[rows, :].astype(outs[s].dtype)


def row_products(place, left, right, width, n, m):
    rows = left[0].shape[0]
    size = rows // (n * m)

    def whole(shape):
        return pl.BlockSpec(shape, lambda i, p: (0,) * len(shape))

    return pl.pallas_call(
        functools.partial(row_products_kernel, len(left)),
        out_shape=tuple(
            jax.ShapeDtypeStruct((n, size, width), BF16 if s else F32) for s in range(m)
        ),
        grid_spec=pltpu.PrefetchScalarGridSpec(
            num_scalar_prefetch=1,
            grid=(1,),
            in_specs=[whole(x.shape) for x in left + right],
            out_specs=tuple(whole((n, size, width)) for _ in range(m)),
            scratch_shapes=[pltpu.VMEM((rows, width), F32)],
        ),
        compiler_params=pltpu.CompilerParams(vmem_limit_bytes=32 << 20),
        cost_estimate=cost(
            flops=2 * rows * width * right[0].shape[1] * len(left),
            bytes_accessed=8 * width * right[0].shape[1] + 6 * rows * width,
        ),
        name="row_products",
    )(place, *left, *right)


def heads_side_by_side(ref):
    hd = HEAD_DIM
    return jnp.concatenate([ref[g * hd : (g + 1) * hd, :] for g in range(GROUP)], 1)


def causal(shape, n):
    key = lax.broadcasted_iota(jnp.int32, shape, 0)
    query = lax.rem(lax.broadcasted_iota(jnp.int32, shape, 1), n)
    return key <= query


def attn_fwd_kernel(blocks, c_ref, q_ref, *refs):
    k_refs, v_refs = refs[:blocks], refs[blocks : 2 * blocks]
    o_ref, ob_ref, lse_ref, scores_ref = refs[2 * blocks :]
    c = c_ref[0]
    n = q_ref.shape[1]
    hd = HEAD_DIM
    queries = heads_side_by_side(q_ref)
    for s in range(blocks):
        rows = slice(s * n, (s + 1) * n)

        def fill(s=s, rows=rows):
            scores = mm(k_refs[s][...], queries, 0, 0)
            if s == 0:
                scores = jnp.where(causal(scores.shape, n), scores, NEG_LARGE)
            scores_ref[rows, :] = scores

        def blank(rows=rows):
            scores_ref[rows, :] = jnp.full((n, GROUP * n), NEG_LARGE, F32)

        if s == 0:
            fill()
        else:
            pl.when(c >= s)(fill)
            pl.when(c < s)(blank)
    lse_ref[...] = jnp.zeros_like(lse_ref)
    for g in range(GROUP):
        cols = slice(g * n, (g + 1) * n)
        scores = scores_ref[:, cols]
        top = jnp.max(scores, 0, keepdims=True)
        weights = jnp.exp(scores - top)
        total = jnp.sum(weights, 0, keepdims=True)
        weights = weights.astype(BF16)
        out = jnp.zeros((hd, n), F32)
        for s in range(blocks):
            out = out + mm(v_refs[s][...], weights[s * n : (s + 1) * n], 1, 0)
        out = out / total
        o_ref[g * hd : (g + 1) * hd, :] = out
        ob_ref[g * hd : (g + 1) * hd, :] = out.astype(BF16)
        lse_ref[0, g : g + 1, :] = top + jnp.log(total)


def kv_specs(blocks, n, first=0):
    keys = [pl.BlockSpec((HEAD_DIM, n), lambda h, c: (first + h, 0))] * blocks
    values = [pl.BlockSpec((HEAD_DIM, n), lambda h, c: (first + h + KV_HEADS, 0))] * blocks
    return keys + values


def attention_forward(context_index, query_t, kv_blocks):
    blocks = len(kv_blocks)
    n = query_t.shape[1]
    wide = GROUP * HEAD_DIM
    heads = query_t.shape[0] // wide
    head = pl.BlockSpec((wide, n), lambda h, c: (h, 0))
    return pl.pallas_call(
        functools.partial(attn_fwd_kernel, blocks),
        out_shape=(
            jax.ShapeDtypeStruct(query_t.shape, F32),
            jax.ShapeDtypeStruct(query_t.shape, BF16),
            jax.ShapeDtypeStruct((heads, 8, n), F32),
        ),
        grid_spec=pltpu.PrefetchScalarGridSpec(
            num_scalar_prefetch=1,
            grid=(heads,),
            in_specs=[head] + kv_specs(blocks, n),
            out_specs=(head, head, pl.BlockSpec((1, 8, n), lambda h, c: (h, 0, 0))),
            scratch_shapes=[pltpu.VMEM((blocks * n, GROUP * n), F32)],
        ),
        compiler_params=pltpu.CompilerParams(vmem_limit_bytes=40 << 20),
        cost_estimate=cost(
            flops=heads * GROUP * blocks * n * n * 256 * 4,
            transcendentals=heads * GROUP * blocks * n * n,
            bytes_accessed=16 * query_t.size,
        ),
        name="attn_fwd",
    )(context_index.reshape(1), query_t, *kv_blocks, *kv_blocks)


def attn_bwd_kernel(blocks, c_ref, q_ref, do_ref, o_ref, lse_ref, *refs):
    k_refs, v_refs = refs[:blocks], refs[blocks : 2 * blocks]
    dq_ref, dkv_ref = refs[2 * blocks :]
    c = c_ref[0]
    n = q_ref.shape[1]
    hd = HEAD_DIM
    queries, grads = heads_side_by_side(q_ref), heads_side_by_side(do_ref)
    deltas, lses = [], []
    for g in range(GROUP):
        head = slice(g * hd, (g + 1) * hd)
        both = do_ref[head, :].astype(F32) * o_ref[head, :]
        deltas.append(jnp.sum(both, 0, keepdims=True))
        lses.append(lse_ref[0, g : g + 1, :])
    delta, lse = jnp.concatenate(deltas, 1), jnp.concatenate(lses, 1)
    for s in range(blocks):

        def work(s=s):
            key_t = k_refs[s][...]
            weights = jnp.exp(mm(key_t, queries, 0, 0) - lse)
            if s == 0:
                weights = jnp.where(causal(weights.shape, n), weights, 0.0)
            grad_weights = mm(v_refs[s][...], grads, 0, 0)
            grad_scores = (weights * (grad_weights - delta)).astype(BF16)
            owner = lax.rem(c - s + blocks, blocks)
            dkv_ref[owner, 0] = mm(queries, grad_scores, 1, 1).astype(BF16)
            dkv_ref[owner, 1] = mm(grads, weights.astype(BF16), 1, 1).astype(BF16)
            step = mm(key_t, grad_scores, 1, 0) * (HEAD_DIM**-0.5)
            for g in range(GROUP):
                head, cols = slice(g * hd, (g + 1) * hd), slice(g * n, (g + 1) * n)
                if s == 0:
                    dq_ref[head, :] = step[:, cols]
                else:
                    dq_ref[head, :] += step[:, cols]

        def skip(s=s):
            owner = lax.rem(c - s + blocks, blocks)
            dkv_ref[owner] = jnp.zeros(dkv_ref.shape[1:], BF16)

        if s == 0:
            work()
        else:
            pl.when(c >= s)(work)
            pl.when(c < s)(skip)


def attention_backward(context_index, query_t, grad_t, out_t, lse, kv_blocks, first, heads):
    blocks = len(kv_blocks)
    n = query_t.shape[1]
    wide = GROUP * HEAD_DIM
    head = pl.BlockSpec((wide, n), lambda h, c: (first + h, 0))
    out = pl.BlockSpec((wide, n), lambda h, c: (h, 0))
    return pl.pallas_call(
        functools.partial(attn_bwd_kernel, blocks),
        out_shape=(
            jax.ShapeDtypeStruct((heads * wide, n), F32),
            jax.ShapeDtypeStruct((blocks, 2, heads * HEAD_DIM, n), BF16),
        ),
        grid_spec=pltpu.PrefetchScalarGridSpec(
            num_scalar_prefetch=1,
            grid=(heads,),
            in_specs=[head, head, head, pl.BlockSpec((1, 8, n), lambda h, c: (first + h, 0, 0))]
            + kv_specs(blocks, n, first),
            out_specs=(
                out,
                pl.BlockSpec((blocks, 2, HEAD_DIM, n), lambda h, c: (0, 0, h, 0)),
            ),
        ),
        compiler_params=pltpu.CompilerParams(vmem_limit_bytes=40 << 20),
        cost_estimate=cost(
            flops=heads * GROUP * blocks * n * n * 256 * 10,
            transcendentals=heads * GROUP * blocks * n * n,
            bytes_accessed=20 * query_t.size,
        ),
        name="attn_bwd",
    )(context_index.reshape(1), query_t, grad_t, out_t, lse, *kv_blocks, *kv_blocks)


def rope_tables(positions):
    half_dim = HEAD_DIM // 2
    frequency = ROPE_BASE ** (-2.0 * jnp.arange(half_dim, dtype=F32) / HEAD_DIM)
    angles = frequency[:, None] * positions.astype(F32)[None, :]
    return jnp.cos(angles), jnp.sin(angles)


def rotate_t(values_t, cosine, sine):
    shaped = values_t.reshape(-1, 2, HEAD_DIM // 2, values_t.shape[1])
    low, high = shaped[:, 0], shaped[:, 1]
    turned = jnp.stack([low * cosine - high * sine, high * cosine + low * sine], 1)
    return turned.reshape(values_t.shape)


def prepare_kernel(p_ref, gate_ref, up_ref, down_ref, *outs):
    in_t_ref, gate_out, up_out, down_out, down_t_out = outs
    gate, up, down = gate_ref[0], up_ref[0], down_ref[0]
    in_t_ref[0, 0, 0] = gate.astype(F32).T.astype(BF16)
    in_t_ref[0, 1, 0] = up.astype(F32).T.astype(BF16)
    gate_out[...] = gate
    up_out[...] = up
    down_out[...] = down
    down_t_out[...] = down.astype(F32).T.astype(BF16)


def prepare_weights(parity, w_gate, w_up, w_down, chunk, share):
    experts, width, hidden = w_gate.shape
    chunks = hidden // chunk // share
    units = chunks * chunk

    def column(e, q, p):
        return (e, 0, q * share + p[0])

    def flat(e, q, p):
        return (0, e * chunks + q)

    return pl.pallas_call(
        prepare_kernel,
        out_shape=(
            jax.ShapeDtypeStruct((experts, 2, chunks, chunk, width), BF16),
            jax.ShapeDtypeStruct((width, experts * units), BF16),
            jax.ShapeDtypeStruct((width, experts * units), BF16),
            jax.ShapeDtypeStruct((experts * units, width), BF16),
            jax.ShapeDtypeStruct((width, experts * units), BF16),
        ),
        grid_spec=pltpu.PrefetchScalarGridSpec(
            num_scalar_prefetch=1,
            grid=(experts, chunks),
            in_specs=[
                pl.BlockSpec((1, width, chunk), column),
                pl.BlockSpec((1, width, chunk), column),
                pl.BlockSpec((1, chunk, width), lambda e, q, p: (e, q * share + p[0], 0)),
            ],
            out_specs=(
                pl.BlockSpec((1, 2, 1, chunk, width), lambda e, q, p: (e, 0, q, 0, 0)),
                pl.BlockSpec((width, chunk), flat),
                pl.BlockSpec((width, chunk), flat),
                pl.BlockSpec((chunk, width), lambda e, q, p: (e * chunks + q, 0)),
                pl.BlockSpec((width, chunk), flat),
            ),
        ),
        compiler_params=pltpu.CompilerParams(vmem_limit_bytes=60 << 20),
        cost_estimate=cost(
            flops=0, transcendentals=0, bytes_accessed=18 * experts * width * units
        ),
        name="prepare_weights",
    )(parity.reshape(1), w_gate, w_up, w_down)


def piece_copies(blocks, refs, target_ref, sems):
    out, at = [], 0
    count = refs[0].shape[1]
    for b, pieces in enumerate(blocks):
        copies = []
        for i, (first, ref, row) in enumerate(pieces):
            last = pieces[i + 1][0] if i + 1 < len(pieces) else target_ref.shape[0]
            copies.append(
                pltpu.make_async_copy(
                    refs[ref].at[row : row + last - first],
                    target_ref.at[first:last, b * count : (b + 1) * count],
                    sems.at[at],
                )
            )
            at += 1
        out.append(copies)
    return out


def write_grads(rows_ref, cots_ref, act, dgate, dup, place_ref, outs, down_s, in_s, share):
    owners = len(outs)
    chunks, _, _, units = outs[0].shape
    width = rows_ref.shape[0]
    size = units // chunks // owners
    tiles = width // units

    def place(k, s):
        return lax.rem(place_ref[2] + k, chunks), lax.rem(place_ref[1] + s, owners)

    down_s[...] = mm(act, cots_ref[...], 1, 1).astype(BF16)
    for k in range(chunks):
        for s in range(owners):
            at_k, at_d = place(k, s)
            start = pl.multiple_of((at_k * owners + at_d) * size, size)
            for t in range(tiles):
                outs[s][k, 0, t * size : (t + 1) * size, :] = down_s[
                    pl.ds(start, size), t * units : (t + 1) * units
                ]
    base = tiles * size
    size = width // (chunks * share * owners)
    for grad_act in (dgate, dup):
        in_s[...] = mm(rows_ref[...], grad_act, 1, 1).astype(BF16)
        for k in range(chunks):
            for q in range(share):
                for s in range(owners):
                    at_k, at_d = place(k, s)
                    start = pl.multiple_of(((at_k * share + q) * owners + at_d) * size, size)
                    to = base + q * size
                    outs[s][k, 0, to : to + size, :] = in_s[pl.ds(start, size), :]
        base += share * size


class Experts:
    def __init__(self, rows, cots, width, units, share, chunks, owners):
        self.arrays, self.plans = [], []
        for blocks in (rows, cots):
            arrays, plan = [], []
            for block in blocks:
                pieces = []
                for first, array, row in block:
                    known = [i for i, x in enumerate(arrays) if x is array]
                    if not known:
                        arrays.append(array)
                    pieces.append((first, known[0] if known else len(arrays) - 1, row))
                plan.append(pieces)
            self.arrays.append(arrays)
            self.plans.append(plan)
        self.blocks = len(rows)
        self.width, self.count = width, rows[0][0][1].shape[1]
        self.tokens = self.blocks * self.count
        self.units, self.share, self.chunks, self.owners = units, share, chunks, owners
        self.height = self.width // chunks // owners * 3

    def n_arrays(self):
        return sum(map(len, self.arrays))

    def scratch(self):
        wide = pltpu.VMEM((self.width, self.tokens), BF16)
        sems = [pltpu.SemaphoreType.DMA((sum(map(len, plan)),)) for plan in self.plans]
        return [wide, wide] + sems

    def copies(self, refs, rows_ref, cots_ref, row_sems, cot_sems):
        n = len(self.arrays[0])
        row_copies = piece_copies(self.plans[0], refs[:n], rows_ref, row_sems)
        cot_copies = piece_copies(self.plans[1], refs[n:], cots_ref, cot_sems)
        return [a + b for a, b in zip(row_copies, cot_copies)]

    def grads_structs(self, n):
        shape = (self.chunks, n, self.height, self.units)
        spec = pl.BlockSpec(
            (self.chunks, 1, self.height, self.units), lambda i, *_: (0, i, 0, 0)
        )
        return [jax.ShapeDtypeStruct(shape, BF16)] * self.owners, [spec] * self.owners

    def act_kernel(self, first, n, make_gates, e_ref, *refs):
        n_arrays = self.n_arrays()
        kept_ref, scales_ref, in_t_ref, down_ref = refs[:4]
        piece_refs, outs, scratch = refs[4 : 4 + n_arrays], refs[4 + n_arrays : -6], refs[-6:]
        if make_gates:
            chosen_ref = scales_ref
            gates_ref, scales_ref = outs[:2]
            outs = outs[2:]
        act_ref, dgate_ref, dup_ref, dscale_ref = outs[:4]
        rows_ref, cots_ref = scratch[:2]
        units, count, blocks = self.units, self.count, self.blocks
        copies = self.copies(piece_refs, *scratch[:4])
        step = pl.program_id(0)
        row = e_ref[0] + first + step

        def move(wait, start):
            def run():
                for b in start:
                    for copy in copies[b]:
                        copy.start()
                for copy in copies[wait]:
                    copy.wait()

            if n == 1:
                run()
            else:
                pl.when(step == 0)(run)

        def products(b):
            move(b, range(blocks) if b == 0 else ())
            cols = slice(b * count, (b + 1) * count)
            acts = jnp.dot(in_t_ref[...], rows_ref[:, cols], preferred_element_type=F32)
            grad = jnp.dot(down_ref[...], cots_ref[:, cols], preferred_element_type=F32)
            return acts, grad

        def finish(b, acts, grad):
            cols = slice(b * count, (b + 1) * count)
            gate, up = acts[:units], acts[units : 2 * units]
            if make_gates:
                chosen = chosen_ref[:, cols] > 0
                logits = jnp.where(chosen, acts[2 * units :], NEG_LARGE)
                gates = jnp.exp(logits - jnp.max(logits, 0, keepdims=True))
                gates = jnp.where(chosen, gates, 0.0)
                gates = gates / jnp.sum(gates, 0, keepdims=True)
                gates_ref[:, cols] = gates
                scales_ref[:, cols] = gates * kept_ref[:, cols]
            scale = scales_ref[pl.ds(row, 1), cols]
            keep = kept_ref[pl.ds(row, 1), cols]
            sigmoid = jax.nn.sigmoid(gate)
            silu = gate * sigmoid
            hidden = silu * up
            dscale_ref[0, 0:1, cols] = keep * jnp.sum(hidden * grad, 0, keepdims=True)
            act_ref[:, cols] = (hidden * scale).astype(BF16)
            grad = grad * scale
            dup_ref[:, cols] = (grad * silu).astype(BF16)
            dgate_ref[:, cols] = (grad * up * (sigmoid + silu * (1.0 - sigmoid))).astype(BF16)

        dscale_ref[...] = jnp.zeros_like(dscale_ref)
        for b in range(blocks):
            finish(b, *products(b))
        write_grads(
            rows_ref,
            cots_ref,
            act_ref[...],
            dgate_ref[...],
            dup_ref[...],
            e_ref,
            outs[4:],
            *scratch[4:],
            self.share,
        )

    def act(self, places, first, n, kept, scales, in_t, down, make_gates=False):
        units, width, tokens = self.units, self.width, self.tokens
        lanes = kept.shape[0]
        in_rows = 2 * units + (lanes if make_gates else 0)
        table = pl.BlockSpec((lanes, tokens), lambda i, e: (0, 0))
        one = pl.BlockSpec((units, tokens), lambda i, e: (i, 0))
        outs, specs = [], []
        if make_gates:
            outs += [jax.ShapeDtypeStruct((lanes, tokens), F32)] * 2
            specs += [table] * 2
        outs += [jax.ShapeDtypeStruct((n * units, tokens), BF16)] * 3
        specs += [one] * 3
        outs.append(jax.ShapeDtypeStruct((n, 8, tokens), F32))
        specs.append(pl.BlockSpec((1, 8, tokens), lambda i, e: (i, 0, 0)))
        structs, grad_specs = self.grads_structs(n)
        extra = [pltpu.VMEM((units, width), BF16), pltpu.VMEM((width, units), BF16)]
        return pl.pallas_call(
            functools.partial(self.act_kernel, first, n, make_gates),
            out_shape=tuple(outs + structs),
            grid_spec=pltpu.PrefetchScalarGridSpec(
                num_scalar_prefetch=1,
                grid=(n,),
                in_specs=[
                    table,
                    table,
                    pl.BlockSpec((in_rows, width), lambda i, e: (first + i, 0)),
                    pl.BlockSpec((units, width), lambda i, e: (first + i, 0)),
                ]
                + [pl.BlockSpec(memory_space=pl.ANY)] * self.n_arrays(),
                out_specs=tuple(specs + grad_specs),
                scratch_shapes=self.scratch() + extra,
            ),
            compiler_params=pltpu.CompilerParams(vmem_limit_bytes=60 << 20),
            cost_estimate=cost(
                flops=12 * width * units * tokens * n,
                transcendentals=units * tokens * n,
                bytes_accessed=4 * width * tokens + 6 * n * units * (width + tokens),
            ),
            name="experts_act",
        )(places, kept, scales, in_t, down, *self.arrays[0], *self.arrays[1])

    def out_kernel(self, parts, e_ref, weight_ref, *refs):
        act_refs, dscale_refs = refs[:parts], refs[parts : 2 * parts]
        message_ref, act_s, dscale_s = refs[2 * parts :]
        at = row = 0
        dscale_s[...] = jnp.zeros_like(dscale_s)
        for act_ref, dscale_ref in zip(act_refs, dscale_refs):
            act_s[at : at + act_ref.shape[0], :] = act_ref[...]
            at += act_ref.shape[0]
            for i in range(dscale_ref.shape[0]):
                dscale_s[pl.ds(e_ref[0] + row, 1), :] = dscale_ref[i, 0:1, :]
                row += 1
        width, lanes = self.width, dscale_s.shape[0]
        message_ref[0, :width, :] = jnp.dot(
            weight_ref[...], act_s[...], preferred_element_type=F32
        ).astype(BF16)
        grads = dscale_s[...]
        high = grads.astype(BF16)
        message_ref[0, width : width + lanes, :] = high
        message_ref[0, width + lanes :, :] = (grads - high.astype(F32)).astype(BF16)

    def out(self, places, lanes, weight, acts, dscales, first_block, n_blocks):
        rows = weight.shape[1]
        parts = len(acts)
        width, count = self.width, self.count

        def column(shape):
            return pl.BlockSpec(
                shape, lambda b, e: (0,) * (len(shape) - 1) + (first_block + b,)
            )

        return pl.pallas_call(
            functools.partial(self.out_kernel, parts),
            out_shape=jax.ShapeDtypeStruct((n_blocks, width + 2 * lanes, count), BF16),
            grid_spec=pltpu.PrefetchScalarGridSpec(
                num_scalar_prefetch=1,
                grid=(n_blocks,),
                in_specs=[
                    pl.BlockSpec(
                        (width, rows),
                        lambda b, e: (0, 0),
                        pipeline_mode=pl.Buffered(buffer_count=1),
                    )
                ]
                + [column((a.shape[0], count)) for a in acts]
                + [column((a.shape[0], 8, count)) for a in dscales],
                out_specs=pl.BlockSpec((1, width + 2 * lanes, count), lambda b, e: (b, 0, 0)),
                scratch_shapes=[pltpu.VMEM((rows, count), BF16), pltpu.VMEM((lanes, count), F32)],
            ),
            compiler_params=pltpu.CompilerParams(vmem_limit_bytes=60 << 20),
            cost_estimate=cost(
                flops=2 * width * rows * count * n_blocks,
                transcendentals=0,
                bytes_accessed=2 * width * rows + 4 * width * count * n_blocks,
            ),
            name="experts_out",
        )(places, weight, *acts, *dscales)

    def back_kernel(self, parts, gate_w_ref, up_w_ref, *refs):
        dgate_refs, dup_refs = refs[:parts], refs[parts : 2 * parts]
        back_ref, dgate_s, dup_s = refs[2 * parts :]
        for target, pieces in ((dgate_s, dgate_refs), (dup_s, dup_refs)):
            at = 0
            for piece in pieces:
                target[at : at + piece.shape[0], :] = piece[...]
                at += piece.shape[0]
        back = jnp.dot(gate_w_ref[...], dgate_s[...], preferred_element_type=F32)
        back = back + jnp.dot(up_w_ref[...], dup_s[...], preferred_element_type=F32)
        back_ref[0] = back.astype(BF16)

    def back(self, gate_w, up_w, dgates, dups, first_block, n_blocks):
        width, count = self.width, self.count
        rows = gate_w.shape[1]
        parts = len(dgates)
        whole = pl.BlockSpec(
            (width, rows), lambda b: (0, 0), pipeline_mode=pl.Buffered(buffer_count=1)
        )
        column = [pl.BlockSpec((a.shape[0], count), lambda b: (0, first_block + b)) for a in dgates]
        return pl.pallas_call(
            functools.partial(self.back_kernel, parts),
            out_shape=jax.ShapeDtypeStruct((n_blocks, width, count), BF16),
            grid=(n_blocks,),
            in_specs=[whole, whole] + column * 2,
            out_specs=pl.BlockSpec((1, width, count), lambda b: (b, 0, 0)),
            scratch_shapes=[pltpu.VMEM((rows, count), BF16)] * 2,
            compiler_params=pltpu.CompilerParams(vmem_limit_bytes=60 << 20),
            cost_estimate=cost(
                flops=4 * width * rows * count * n_blocks,
                transcendentals=0,
                bytes_accessed=4 * width * rows + 4 * width * count * n_blocks,
            ),
            name="experts_back",
        )(gate_w, up_w, *dgates, *dups)


def body(
    tokens,
    routes,
    cotangent,
    norm_attn,
    w_query,
    w_key,
    w_value,
    w_out,
    norm_ffn,
    w_router,
    w_gate,
    w_up,
    w_down,
):
    comm = Comm()
    hold = lax.optimization_barrier
    count, width = tokens.shape[1], tokens.shape[2]
    top_k = routes.shape[2]
    n_experts, _, hidden_units = w_gate.shape
    all_experts = n_experts * comm.n_expert
    capacity = (9 * count * top_k + 8 * all_experts - 1) // (8 * all_experts)
    n_context, n_dp, share = comm.n_context, comm.n_dp, comm.share
    expert_index = lax.axis_index("expert")
    context_index = lax.axis_index("context")
    dp_index = lax.axis_index("dp")
    parity = context_index % share
    chunks = n_context // share
    units = hidden_units // share
    lanes = -(-all_experts // 32) * 32
    places = jnp.stack([expert_index * n_experts, dp_index, context_index // share])

    cot_t = cotangent[0].T
    routed = (
        routes[0].T[:, None, :] == jnp.arange(lanes, dtype=jnp.int32)[None, :, None]
    ).astype(F32)
    cot_message = jnp.concatenate([cot_t, routed.sum(0).astype(BF16)])
    tokens, cot_message = hold((tokens, cot_message))
    across = [comm.pair(cot_message)] if share == 2 else []
    cots = [cot_message] + [comm.pull(cot_message, k, 0) for k in range(1, comm.columns)]

    hidden = tokens[0].T.astype(F32)
    gain_attn = norm_attn.astype(F32)[:, None]
    gain_ffn = norm_ffn.astype(F32)[:, None]
    scale_attn = rms_scale(hidden)
    normed_attn = (hidden * scale_attn * gain_attn).astype(BF16)
    positions = context_index * count + jnp.arange(count, dtype=jnp.int32)
    cosine, sine = rope_tables(positions)
    key_t = rotate_t(mm(w_key, normed_attn, 0, 0), cosine, sine).astype(BF16)
    value_t = mm(w_value, normed_attn, 0, 0).astype(BF16)
    kv_width = key_t.shape[0]
    kv_own = jnp.concatenate([key_t, value_t], 0)
    kv_blocks = [kv_own]
    for s in range(1, n_context):
        pairs = [(i, i + s) for i in range(n_context - s)]
        kv_blocks.append(lax.ppermute(kv_own, "context", pairs))
    query_t = rotate_t(mm(w_query, normed_attn, 0, 0), cosine, sine)
    query_t = (query_t * HEAD_DIM**-0.5).astype(BF16)

    weights = prepare_weights(parity, w_gate, w_up, w_down, hidden_units // n_context, share)
    router_t = jnp.zeros((lanes, width), BF16).at[:all_experts].set(w_router.T)
    in_t, gate_w, up_w, down, down_t = weights
    in_t = in_t.reshape(n_experts * 2 * units, width)
    in_first = jnp.concatenate([in_t[: 2 * units], router_t])
    if across:
        across, in_t, in_first = hold((across, in_t, in_first))
        across = across + [comm.pull(across[0], k, 0) for k in range(1, comm.columns)]
        cots, across[0], in_t = hold((cots, across[0], in_t))
    cots, across = [[[(0, x, 0)] for x in part] for part in (cots, across)]
    others = comm.from_core(cots) if comm.cores == 2 else []
    kv_blocks, in_t, in_first, gate_w, up_w, down, down_t = hold(
        (kv_blocks, in_t, in_first, gate_w, up_w, down, down_t)
    )
    out_t, out_low, lse = attention_forward(context_index, query_t, kv_blocks)
    middle = hidden + mm(w_out, out_low, 0, 0)
    scale_ffn = rms_scale(middle)
    normed_ffn = (middle * scale_ffn * gain_ffn).astype(BF16)
    across = [block[0][1] for block in across]
    across, normed_ffn = hold((across, normed_ffn))
    rows, across = comm.gather_group(normed_ffn, across)
    across = [[(0, x, 0)] for x in across]
    if comm.cores == 2 and across:
        others = others + comm.from_core(across)
    cots = cots + across + others

    routed_all = jnp.concatenate(
        [block[0][1][block[0][2] + width : block[0][2] + width + lanes] for block in cots]
    )
    n_blocks = len(cots)
    before = jnp.triu(jnp.ones((count, count), BF16), 1)
    ranking = mm(routed_all, before, 1, 0)
    chosen = routed_all.astype(F32)
    kept = jnp.where(ranking < capacity, chosen, 0.0)

    def side_by_side(array):
        array = array.reshape(n_blocks, lanes, count)
        return jnp.concatenate([array[b] for b in range(n_blocks)], 1)

    chosen, kept = side_by_side(chosen), side_by_side(kept)

    row_count = width // comm.n_expert

    def for_experts(*arrays):
        out = []
        for j in range(comm.cores):
            for k in range(comm.columns):
                column, core = expert_index // comm.cores, expert_index % comm.cores
                column = (column - k) % comm.columns
                target = column * comm.cores + (core + j) % comm.cores
                pieces = [
                    lax.dynamic_slice_in_dim(array, target * row_count, row_count, 0)
                    for array in arrays
                ]
                out.append(jnp.concatenate(pieces))
        return out

    def to_experts(pieces):
        peers = [(j, k) for j in range(comm.cores) for k in range(comm.columns)]
        return pieces[:1] + [comm.pull(x, k, j) for x, (j, k) in zip(pieces[1:], peers[1:])]

    columns_sent = for_experts(normed_attn, out_low)
    chosen, columns_sent = hold((chosen, columns_sent))

    own = Experts(rows, cots, width, units, share, chunks, n_dp)
    groups, at = [], 0
    for n in (1, (n_experts - 1) // 2, n_experts - 1 - (n_experts - 1) // 2):
        if n:
            groups.append((at, n))
            at += n
    acts, dgates, dups, dscales, kept_parts, arrived, crossing = ([] for _ in range(7))
    scales = None

    def pass_on(g, values):
        if g >= len(groups):
            return values
        terms, values = hold((arrived[g], values))
        terms = [kept_parts[g]] + terms

        def part(k):
            return sum(term[k].astype(F32) for term in terms)

        sent = comm.send_context([part(k).astype(BF16) for k in range(1, chunks)], share)
        crossing.append([part(0).astype(BF16)] + sent)
        return values

    for g, (first, n) in enumerate(groups):
        if g == 0:
            gates_all, scales, *done = own.act(
                places, first, n, kept, chosen, in_first, down, make_gates=True
            )
        else:
            done = own.act(places, first, n, kept, scales, in_t, down)
        for target, value in zip((acts, dgates, dups, dscales, kept_parts), done):
            target.append(value)
        arrived.append(comm.send_dp(done[5:]))
        if g == 0:
            scales, columns_sent = hold((scales, columns_sent))
            columns_got = to_experts(columns_sent)
        if g == 1:
            scales = pass_on(0, scales)

    columns_got, acts = hold((columns_got, acts))
    h1_rows = [x[:row_count] for x in columns_got]
    ob_rows = [x[row_count:] for x in columns_got]
    near_count = n_blocks // comm.cores

    def both_cores(call):
        other = None
        if comm.cores == 2:
            other = comm.push(call(near_count, near_count), 0, 1)
        return call(0, near_count), other

    message = both_cores(
        lambda first, n: own.out(places, lanes, down_t, acts, dscales, first, n)
    )
    back_other = None
    if comm.cores == 2:
        back_other = own.back(gate_w, up_w, dgates, dups, near_count, near_count)
        back_other = comm.push(back_other, 0, 1)
    message, dgates = hold((message, dgates))
    dgates, crossing[0] = pass_on(1, (dgates, crossing[0]))
    back_near = own.back(gate_w, up_w, dgates, dups, 0, near_count)
    message = comm.return_hops(*message)
    message, back_near = hold((message, back_near))
    back = comm.return_hops(back_near, back_other)
    returned = comm.return_last(message)
    back = pass_on(2, back)
    grad_normed_ffn = comm.return_last(back)
    result = (middle + returned[:width]).astype(BF16)
    grad_gates = returned[width : width + lanes] + returned[width + lanes :]
    gates_own = gates_all[:, :count]

    upstream = cot_t.astype(F32)
    mean_grad = jnp.sum(gates_own * grad_gates, 0, keepdims=True)
    grad_logits = (gates_own * (grad_gates - mean_grad)).astype(BF16)
    grad_normed_ffn = grad_normed_ffn + mm(router_t, grad_logits, 0, 0)
    grad_gain_ffn = jnp.sum(grad_normed_ffn * middle * scale_ffn, 1)
    grad_middle = upstream + norm_back(grad_normed_ffn, middle, scale_ffn, gain_ffn)
    grad_branch = grad_middle.astype(BF16)

    gain_grid = grad_gain_ffn.reshape(-1, count)
    gain_lines = gain_grid.shape[0]
    gain_high = lax.reduce_precision(gain_grid, 8, 7)
    gain_rows = jnp.concatenate([gain_high, gain_grid - gain_high]).astype(BF16)
    gain_rows = jnp.pad(gain_rows, ((0, -2 * gain_lines % 16), (0, 0)))
    branch_all = comm.gather_columns(jnp.concatenate([grad_branch, grad_logits, gain_rows]))
    grad_attn_t = mm(w_out, grad_branch, 1, 0).astype(BF16)

    def attention_half(first, heads):
        return attention_backward(
            context_index, query_t, grad_attn_t, out_t, lse, kv_blocks, first, heads
        )

    def to_keys(grad_kv):
        return lax.all_to_all(grad_kv, "context", 0, 0, tiled=True)

    size_down = units // chunks // n_dp
    tiles = width // units

    def total_of(terms):
        total = jnp.concatenate([sum(x.astype(F32) for x in group) for group in terms])
        n = total.shape[0]
        part = total[:, : tiles * size_down].reshape(n, tiles, size_down, units)
        down = jnp.swapaxes(part, 1, 2).reshape(n, size_down, width)
        part = total[:, tiles * size_down :]
        return down, part.reshape(n, 2, share, part.shape[1] // 2 // share, units)

    def send_pair(part):
        if share == 1:
            return part[:, :, 0], None
        keep = lax.dynamic_index_in_dim(part, parity, 2, False)
        send = lax.dynamic_index_in_dim(part, 1 - parity, 2, False)
        return keep, comm.pair(send.astype(BF16))

    def both_columns(keep, other):
        if other is None:
            return keep
        other = other.astype(F32)
        first = jnp.where(parity == 0, keep, other)
        second = jnp.where(parity == 0, other, keep)
        chunk = hidden_units // n_context
        pieces = []
        for q in range(chunks):
            pieces += [x[..., q * chunk : (q + 1) * chunk] for x in (first, second)]
        return jnp.concatenate(pieces, -1)

    early = crossing[:-1]
    early, grad_attn_t = hold((early, grad_attn_t))
    totals = [total_of(early)] if early else []
    pairs = [send_pair(part) for _, part in totals]
    half = KV_HEADS // 2
    grad_query_a, grad_kv_a = attention_half(0, half)
    kv_a = to_keys(grad_kv_a)
    branch_all, grad_attn_t = hold((branch_all, grad_attn_t))
    branch_all = comm.gather_cores(branch_all)
    grad_query_b, grad_kv_b = attention_half(half, half)
    kv_a, grad_kv_b, branch_all, crossing[-1] = hold((kv_a, grad_kv_b, branch_all, crossing[-1]))
    kv_b = to_keys(grad_kv_b)

    out_sum = comm.scatter_rows(ob_rows, branch_all, width)
    h2_rows = [
        lax.dynamic_slice_in_dim(array, at + expert_index * row_count, row_count, 0)
        for j in range(comm.cores)
        for ((_, array, at),) in rows[j * near_count : j * near_count + comm.columns]
    ]
    router_rows = sum(mm(a, b[width : width + lanes], 1, 1) for a, b in zip(h2_rows, branch_all))
    gain_total = sum(x[width + lanes :].astype(F32) for x in branch_all)
    gain_total = gain_total[:gain_lines] + gain_total[gain_lines : 2 * gain_lines]
    gain_part = lax.dynamic_slice_in_dim(
        gain_total.reshape(width), expert_index * row_count, row_count, 0
    )
    rest = jnp.zeros((row_count, LANES - lanes - 1), F32)
    extra = jnp.concatenate([router_rows, gain_part[:, None], rest], 1).astype(BF16)
    extra = extra.reshape(n_context * n_dp, -1, LANES)
    extra, kv_b = hold((extra, kv_b))
    extra = lax.all_to_all(extra, ("context", "dp"), 0, 0, tiled=True)
    extra = jnp.sum(extra.astype(F32), 0)

    grad_query_raw = jnp.concatenate(
        [rotate_t(x, cosine, -sine).astype(BF16) for x in (grad_query_a, grad_query_b)]
    )
    query_sum = comm.scatter_rows(h1_rows, comm.gather_expert(grad_query_raw), width)
    late = crossing[-1]
    pairs, kv_b = hold((pairs, kv_b))
    totals.append(total_of([late]))
    pairs.append(send_pair(totals[-1][1]))
    kv_sums = [jnp.sum(x.astype(F32), 0) for x in (kv_a, kv_b)]
    grad_key_raw = [rotate_t(kv_sum[0], cosine, -sine).astype(BF16) for kv_sum in kv_sums]
    grad_kv_raw = jnp.concatenate(grad_key_raw + [kv_sum[1].astype(BF16) for kv_sum in kv_sums])
    kv_rows = comm.scatter_rows(h1_rows, comm.gather_expert(grad_kv_raw), 2 * kv_width)
    key_sum, value_sum = kv_rows[:, :kv_width], kv_rows[:, kv_width:]

    down_sum = jnp.concatenate([down for down, _ in totals])
    parts = [both_columns(*pair) for pair in pairs]
    gate_sum = jnp.concatenate([part[:, 0] for part in parts])
    up_sum = jnp.concatenate([part[:, 1] for part in parts])

    shard = (expert_index * n_context + context_index) * n_dp + dp_index
    shard_rows = query_sum.shape[0]

    def shard_of(array):
        return lax.dynamic_slice_in_dim(array, shard * shard_rows, shard_rows, 0).astype(F32)

    gain_sum = (
        jnp.sum(shard_of(w_query) * query_sum, 1)
        + jnp.sum(shard_of(w_key) * key_sum, 1)
        + jnp.sum(shard_of(w_value) * value_sum, 1)
    ) / shard_of(norm_attn)

    grad_normed_attn = mm(w_query, grad_query_raw, 1, 0)
    grad_normed_attn = grad_normed_attn + mm(w_key, grad_kv_raw[:kv_width], 1, 0)
    grad_normed_attn = grad_normed_attn + mm(w_value, grad_kv_raw[kv_width:], 1, 0)
    grad_hidden = grad_middle + norm_back(grad_normed_attn, hidden, scale_attn, gain_attn)
    return (
        result.T[None],
        grad_hidden.astype(BF16).T[None],
        gain_sum,
        query_sum,
        key_sum,
        value_sum,
        out_sum,
        extra[:, lanes],
        extra[:, :all_experts],
        gate_sum,
        up_sum,
        down_sum,
    )


def solution(mesh):
    rows = P(("expert", "dp"), "context", None)
    dense = P(("expert", "context", "dp"), None)
    vector = P(("expert", "context", "dp"))
    experts = P("expert", None, None)
    expert_grads = P("expert", ("context", "dp"), None)
    return jax.shard_map(
        body,
        mesh=mesh,
        in_specs=(rows, rows, rows) + (P(),) * 7 + (experts,) * 3,
        out_specs=(rows, rows, vector, dense, dense, dense, dense, vector, dense)
        + (expert_grads,) * 3,
        check_vma=False,
    )
```

```python
import functools

import jax
import jax.numpy as jnp
from jax import lax
from jax.experimental import pallas as pl
from jax.experimental.pallas import tpu as pltpu
from jax.sharding import PartitionSpec as P

HEADS = 24
KV_HEADS = 8
HEAD_DIM = 64
GROUP = HEADS // KV_HEADS


EPS = 1e-05
ROPE_BASE = 10000.0
NEG_LARGE = -1e30
F32 = jnp.float32
BF16 = jnp.bfloat16
LANES = 128


def cost(flops, bytes_accessed, transcendentals=0):
    scale = 64
    return pl.CostEstimate(
        flops=flops // scale,
        bytes_accessed=bytes_accessed // scale,
        transcendentals=transcendentals // scale,
    )


def rms_scale(values):
    return lax.rsqrt(jnp.mean(values * values, 0, keepdims=True) + EPS)


def norm_back(grad_out, values, scale, gain):
    weighted = gain * grad_out
    return scale * weighted - values * scale**3 * jnp.mean(weighted * values, 0, keepdims=True)


def mm(a, b, da, db):
    return lax.dot_general(a, b, (((da,), (db,)), ((), ())), preferred_element_type=F32)


class Comm:
    def __init__(self):
        self.n_expert = lax.axis_size("expert")
        self.n_context = lax.axis_size("context")
        self.n_dp = lax.axis_size("dp")
        self.cores = 2 if self.n_expert % 2 == 0 else 1
        self.columns = self.n_expert // self.cores
        self.share = 2 if self.n_context % 2 == 0 else 1

    def peer(self, i, k, j):
        column, core = divmod(i, self.cores)
        return ((column + k) % self.columns) * self.cores + (core + j) % self.cores

    def pull(self, value, k, j):
        pairs = [(self.peer(i, k, j), i) for i in range(self.n_expert)]
        return lax.ppermute(value, "expert", pairs)

    def push(self, value, k, j):
        pairs = [(i, self.peer(i, k, j)) for i in range(self.n_expert)]
        return lax.ppermute(value, "expert", pairs)

    def pair(self, value):
        return lax.ppermute(value, "context", [(i, i ^ 1) for i in range(self.n_context)])

    def from_core(self, blocks):
        arrays = [array for block in blocks for _, array, _ in block]
        moved = self.pull(jnp.concatenate(arrays) if len(arrays) > 1 else arrays[0], 0, 1)
        out, at = [], 0
        for block in blocks:
            pieces = []
            for row, array, _ in block:
                pieces.append((row, moved, at))
                at += array.shape[0]
            out.append(pieces)
        return out

    def gather_columns(self, value):
        return [value] + [self.pull(value, k, 0) for k in range(1, self.columns)]

    def gather_cores(self, near):
        if self.cores == 2:
            near = near + [self.pull(block, 0, 1) for block in near]
        return near

    def gather_expert(self, value):
        return self.gather_cores(self.gather_columns(value))

    def gather_group(self, value, beside):
        columns = [self.pull(value, k, 0) for k in range(1, self.columns)]
        far = []
        if self.share == 2:
            half = value.shape[0] // 2
            across = self.pair(value)
            columns, across, beside = lax.optimization_barrier((columns, across, beside))
        first = [[(0, value, 0)]] + [[(0, block, 0)] for block in columns]
        if self.share == 2:
            first.append([(0, across, 0)])
            for k in range(1, self.columns):
                top = self.pull(across[:half], k, 0)
                bottom = self.pair(columns[k - 1][half:])
                far.append([(0, top, 0), (half, bottom, 0)])
        blocks = first + far
        if self.cores == 2:
            blocks = blocks + self.from_core(first)
            blocks = blocks + (self.from_core(far) if far else [])
        return blocks, beside

    def return_hops(self, near, other):
        columns = self.columns
        shape = (self.share, columns) + near.shape[1:]
        arrays = [x.reshape(shape) for x in (near, other) if x is not None]

        def part(*at):
            return sum(array[at].astype(F32) for array in arrays)

        if self.share == 1:
            sent = [self.push(part(0, k).astype(BF16), k, 0) for k in range(1, columns)]
            return [part(0, 0)] + sent
        half = near.shape[1] // 2
        low, high = slice(0, half), slice(half, 2 * half)
        every = slice(None)
        by_column = [
            self.push(part(every, k, low).astype(BF16), k, 0) for k in range(1, columns)
        ]
        by_pair = self.pair(part(1, every, high).astype(BF16))
        return [part(every, 0, low)] + by_column + [part(0, every, high), by_pair]

    def return_last(self, terms):
        columns = self.columns
        if self.share == 1:
            return sum(term.astype(F32) for term in terms)
        top = terms[:columns]
        bottom = terms[columns : columns + 2]

        def total(parts, at):
            return sum(part[at].astype(F32) for part in parts)

        top_other = self.pair(total(top, 1).astype(BF16))
        others = [
            self.push(total(bottom, k).astype(BF16), k, 0).astype(F32)
            for k in range(1, columns)
        ]
        return jnp.concatenate(
            [total(top, 0) + top_other.astype(F32), sum(others, total(bottom, 0))]
        )

    def send_dp(self, parts):
        n = self.n_dp
        return [
            lax.ppermute(parts[s - 1], "dp", [(i, (i + s) % n) for i in range(n)])
            for s in range(1, n)
        ]

    def send_context(self, parts, stride):
        n = self.n_context // stride
        out = []
        for s in range(1, n):
            pairs = []
            for i in range(self.n_context):
                k, r = divmod(i, stride)
                pairs.append((i, ((k + s) % n) * stride + r))
            out.append(lax.ppermute(parts[s - 1], "context", pairs))
        return out

    def scatter_rows(self, left, right, width):
        n, m = self.n_context, self.n_dp
        c, d = lax.axis_index("context"), lax.axis_index("dp")
        size = left[0].shape[0] // (n * m)
        if size % 16 == 0:
            mine, *parts = row_products(jnp.stack([c, d]), left, right, width, n, m)
        else:
            local = sum(mm(a, b[:width], 1, 1) for a, b in zip(left, right))
            local = local.reshape(n, m, size, width)
            local = jnp.stack(
                [lax.dynamic_index_in_dim(local, (c + k) % n, 0, False) for k in range(n)]
            )
            mine, *parts = [
                lax.dynamic_index_in_dim(local, (d + s) % m, 1, False) for s in range(m)
            ]
        return [mine] + self.send_dp([part.astype(BF16) for part in parts])

    def scatter_rest(self, terms):
        n = self.n_context

        def of_context(k):
            return sum(x[k].astype(F32) for x in terms)

        came_far = self.send_context([of_context(k).astype(BF16) for k in range(1, n)], 1)
        return of_context(0) + sum(x.astype(F32) for x in came_far)


def row_products_kernel(count, place_ref, *refs):
    left, right, outs, total_s = refs[:count], refs[count : 2 * count], refs[2 * count : -1], refs[-1]
    width = total_s.shape[1]
    total_s[...] = mm(
        jnp.concatenate([a[...] for a in left], 1),
        jnp.concatenate([b[:width, :] for b in right], 1),
        1,
        1,
    )
    n, size, _ = outs[0].shape
    m = len(outs)
    for k in range(n):
        for s in range(m):
            owner = lax.rem(place_ref[0] + k, n) * m + lax.rem(place_ref[1] + s, m)
            rows = pl.ds(pl.multiple_of(owner * size, size), size)
            outs[s][k] = total_s[rows, :].astype(outs[s].dtype)


def row_products(place, left, right, width, n, m):
    rows = left[0].shape[0]
    size = rows // (n * m)

    def whole(shape):
        return pl.BlockSpec(shape, lambda i, p: (0,) * len(shape))

    return pl.pallas_call(
        functools.partial(row_products_kernel, len(left)),
        out_shape=tuple(
            jax.ShapeDtypeStruct((n, size, width), BF16 if s else F32) for s in range(m)
        ),
        grid_spec=pltpu.PrefetchScalarGridSpec(
            num_scalar_prefetch=1,
            grid=(1,),
            in_specs=[whole(x.shape) for x in left + right],
            out_specs=tuple(whole((n, size, width)) for _ in range(m)),
            scratch_shapes=[pltpu.VMEM((rows, width), F32)],
        ),
        compiler_params=pltpu.CompilerParams(vmem_limit_bytes=32 << 20),
        cost_estimate=cost(
            flops=2 * rows * width * right[0].shape[1] * len(left),
            bytes_accessed=8 * width * right[0].shape[1] + 6 * rows * width,
        ),
        name="row_products",
    )(place, *left, *right)


def heads_side_by_side(ref):
    hd = HEAD_DIM
    return jnp.concatenate([ref[g * hd : (g + 1) * hd, :] for g in range(GROUP)], 1)


def causal(shape, n):
    key = lax.broadcasted_iota(jnp.int32, shape, 0)
    query = lax.rem(lax.broadcasted_iota(jnp.int32, shape, 1), n)
    return key <= query


def attn_fwd_kernel(blocks, c_ref, q_ref, *refs):
    k_refs, v_refs = refs[:blocks], refs[blocks : 2 * blocks]
    o_ref, ob_ref, lse_ref, scores_ref = refs[2 * blocks :]
    c = c_ref[0]
    n = q_ref.shape[1]
    hd = HEAD_DIM
    queries = heads_side_by_side(q_ref)
    for s in range(blocks):
        rows = slice(s * n, (s + 1) * n)

        def fill(s=s, rows=rows):
            scores = mm(k_refs[s][...], queries, 0, 0)
            if s == 0:
                scores = jnp.where(causal(scores.shape, n), scores, NEG_LARGE)
            scores_ref[rows, :] = scores

        def blank(rows=rows):
            scores_ref[rows, :] = jnp.full((n, GROUP * n), NEG_LARGE, F32)

        if s == 0:
            fill()
        else:
            pl.when(c >= s)(fill)
            pl.when(c < s)(blank)
    lse_ref[...] = jnp.zeros_like(lse_ref)
    for g in range(GROUP):
        cols = slice(g * n, (g + 1) * n)
        scores = scores_ref[:, cols]
        top = jnp.max(scores, 0, keepdims=True)
        weights = jnp.exp(scores - top)
        total = jnp.sum(weights, 0, keepdims=True)
        weights = weights.astype(BF16)
        out = jnp.zeros((hd, n), F32)
        for s in range(blocks):
            out = out + mm(v_refs[s][...], weights[s * n : (s + 1) * n], 1, 0)
        out = out / total
        o_ref[g * hd : (g + 1) * hd, :] = out
        ob_ref[g * hd : (g + 1) * hd, :] = out.astype(BF16)
        lse_ref[0, g : g + 1, :] = top + jnp.log(total)


def kv_specs(blocks, n, first=0):
    keys = [pl.BlockSpec((HEAD_DIM, n), lambda h, c: (first + h, 0))] * blocks
    values = [pl.BlockSpec((HEAD_DIM, n), lambda h, c: (first + h + KV_HEADS, 0))] * blocks
    return keys + values


def attention_forward(context_index, query_t, kv_blocks):
    blocks = len(kv_blocks)
    n = query_t.shape[1]
    wide = GROUP * HEAD_DIM
    heads = query_t.shape[0] // wide
    head = pl.BlockSpec((wide, n), lambda h, c: (h, 0))
    return pl.pallas_call(
        functools.partial(attn_fwd_kernel, blocks),
        out_shape=(
            jax.ShapeDtypeStruct(query_t.shape, F32),
            jax.ShapeDtypeStruct(query_t.shape, BF16),
            jax.ShapeDtypeStruct((heads, 8, n), F32),
        ),
        grid_spec=pltpu.PrefetchScalarGridSpec(
            num_scalar_prefetch=1,
            grid=(heads,),
            in_specs=[head] + kv_specs(blocks, n),
            out_specs=(head, head, pl.BlockSpec((1, 8, n), lambda h, c: (h, 0, 0))),
            scratch_shapes=[pltpu.VMEM((blocks * n, GROUP * n), F32)],
        ),
        compiler_params=pltpu.CompilerParams(vmem_limit_bytes=40 << 20),
        cost_estimate=cost(
            flops=heads * GROUP * blocks * n * n * 256 * 4,
            transcendentals=heads * GROUP * blocks * n * n,
            bytes_accessed=16 * query_t.size,
        ),
        name="attn_fwd",
    )(context_index.reshape(1), query_t, *kv_blocks, *kv_blocks)


def attn_bwd_kernel(blocks, c_ref, q_ref, do_ref, o_ref, lse_ref, *refs):
    k_refs, v_refs = refs[:blocks], refs[blocks : 2 * blocks]
    dq_ref, dkv_ref = refs[2 * blocks :]
    c = c_ref[0]
    n = q_ref.shape[1]
    hd = HEAD_DIM
    queries, grads = heads_side_by_side(q_ref), heads_side_by_side(do_ref)
    deltas, lses = [], []
    for g in range(GROUP):
        head = slice(g * hd, (g + 1) * hd)
        both = do_ref[head, :].astype(F32) * o_ref[head, :]
        deltas.append(jnp.sum(both, 0, keepdims=True))
        lses.append(lse_ref[0, g : g + 1, :])
    delta, lse = jnp.concatenate(deltas, 1), jnp.concatenate(lses, 1)
    for s in range(blocks):

        def work(s=s):
            key_t = k_refs[s][...]
            weights = jnp.exp(mm(key_t, queries, 0, 0) - lse)
            if s == 0:
                weights = jnp.where(causal(weights.shape, n), weights, 0.0)
            grad_weights = mm(v_refs[s][...], grads, 0, 0)
            grad_scores = (weights * (grad_weights - delta)).astype(BF16)
            owner = lax.rem(c - s + blocks, blocks)
            dkv_ref[owner, 0] = mm(queries, grad_scores, 1, 1).astype(BF16)
            dkv_ref[owner, 1] = mm(grads, weights.astype(BF16), 1, 1).astype(BF16)
            step = mm(key_t, grad_scores, 1, 0) * (HEAD_DIM**-0.5)
            for g in range(GROUP):
                head, cols = slice(g * hd, (g + 1) * hd), slice(g * n, (g + 1) * n)
                if s == 0:
                    dq_ref[head, :] = step[:, cols]
                else:
                    dq_ref[head, :] += step[:, cols]

        def skip(s=s):
            owner = lax.rem(c - s + blocks, blocks)
            dkv_ref[owner] = jnp.zeros(dkv_ref.shape[1:], BF16)

        if s == 0:
            work()
        else:
            pl.when(c >= s)(work)
            pl.when(c < s)(skip)


def attention_backward(context_index, query_t, grad_t, out_t, lse, kv_blocks, first, heads):
    blocks = len(kv_blocks)
    n = query_t.shape[1]
    wide = GROUP * HEAD_DIM
    head = pl.BlockSpec((wide, n), lambda h, c: (first + h, 0))
    out = pl.BlockSpec((wide, n), lambda h, c: (h, 0))
    return pl.pallas_call(
        functools.partial(attn_bwd_kernel, blocks),
        out_shape=(
            jax.ShapeDtypeStruct((heads * wide, n), F32),
            jax.ShapeDtypeStruct((blocks, 2, heads * HEAD_DIM, n), BF16),
        ),
        grid_spec=pltpu.PrefetchScalarGridSpec(
            num_scalar_prefetch=1,
            grid=(heads,),
            in_specs=[head, head, head, pl.BlockSpec((1, 8, n), lambda h, c: (first + h, 0, 0))]
            + kv_specs(blocks, n, first),
            out_specs=(
                out,
                pl.BlockSpec((blocks, 2, HEAD_DIM, n), lambda h, c: (0, 0, h, 0)),
            ),
        ),
        compiler_params=pltpu.CompilerParams(vmem_limit_bytes=40 << 20),
        cost_estimate=cost(
            flops=heads * GROUP * blocks * n * n * 256 * 10,
            transcendentals=heads * GROUP * blocks * n * n,
            bytes_accessed=20 * query_t.size,
        ),
        name="attn_bwd",
    )(context_index.reshape(1), query_t, grad_t, out_t, lse, *kv_blocks, *kv_blocks)


def rope_tables(positions):
    half_dim = HEAD_DIM // 2
    frequency = ROPE_BASE ** (-2.0 * jnp.arange(half_dim, dtype=F32) / HEAD_DIM)
    angles = frequency[:, None] * positions.astype(F32)[None, :]
    return jnp.cos(angles), jnp.sin(angles)


def rotate_t(values_t, cosine, sine):
    shaped = values_t.reshape(-1, 2, HEAD_DIM // 2, values_t.shape[1])
    low, high = shaped[:, 0], shaped[:, 1]
    turned = jnp.stack([low * cosine - high * sine, high * cosine + low * sine], 1)
    return turned.reshape(values_t.shape)


def prepare_kernel(p_ref, gate_ref, up_ref, down_ref, *outs):
    in_t_ref, gate_out, up_out, down_out, down_t_out = outs
    gate, up, down = gate_ref[0], up_ref[0], down_ref[0]
    in_t_ref[0, 0, 0] = gate.astype(F32).T.astype(BF16)
    in_t_ref[0, 1, 0] = up.astype(F32).T.astype(BF16)
    gate_out[...] = gate
    up_out[...] = up
    down_out[...] = down
    down_t_out[...] = down.astype(F32).T.astype(BF16)


def prepare_weights(parity, w_gate, w_up, w_down, chunk, share):
    experts, width, hidden = w_gate.shape
    chunks = hidden // chunk // share
    units = chunks * chunk

    def column(e, q, p):
        return (e, 0, q * share + p[0])

    def flat(e, q, p):
        return (0, e * chunks + q)

    return pl.pallas_call(
        prepare_kernel,
        out_shape=(
            jax.ShapeDtypeStruct((experts, 2, chunks, chunk, width), BF16),
            jax.ShapeDtypeStruct((width, experts * units), BF16),
            jax.ShapeDtypeStruct((width, experts * units), BF16),
            jax.ShapeDtypeStruct((experts * units, width), BF16),
            jax.ShapeDtypeStruct((width, experts * units), BF16),
        ),
        grid_spec=pltpu.PrefetchScalarGridSpec(
            num_scalar_prefetch=1,
            grid=(experts, chunks),
            in_specs=[
                pl.BlockSpec((1, width, chunk), column),
                pl.BlockSpec((1, width, chunk), column),
                pl.BlockSpec((1, chunk, width), lambda e, q, p: (e, q * share + p[0], 0)),
            ],
            out_specs=(
                pl.BlockSpec((1, 2, 1, chunk, width), lambda e, q, p: (e, 0, q, 0, 0)),
                pl.BlockSpec((width, chunk), flat),
                pl.BlockSpec((width, chunk), flat),
                pl.BlockSpec((chunk, width), lambda e, q, p: (e * chunks + q, 0)),
                pl.BlockSpec((width, chunk), flat),
            ),
        ),
        compiler_params=pltpu.CompilerParams(vmem_limit_bytes=60 << 20),
        cost_estimate=cost(
            flops=0, transcendentals=0, bytes_accessed=18 * experts * width * units
        ),
        name="prepare_weights",
    )(parity.reshape(1), w_gate, w_up, w_down)


def piece_copies(blocks, refs, target_ref, sems):
    out, at = [], 0
    count = refs[0].shape[1]
    for b, pieces in enumerate(blocks):
        copies = []
        for i, (first, ref, row) in enumerate(pieces):
            last = pieces[i + 1][0] if i + 1 < len(pieces) else target_ref.shape[0]
            copies.append(
                pltpu.make_async_copy(
                    refs[ref].at[row : row + last - first],
                    target_ref.at[first:last, b * count : (b + 1) * count],
                    sems.at[at],
                )
            )
            at += 1
        out.append(copies)
    return out


def write_grads(rows_ref, cots_ref, act, dgate, dup, place_ref, outs, down_s, in_s, share):
    owners = len(outs)
    chunks, _, _, units = outs[0].shape
    width = rows_ref.shape[0]
    size = units // chunks // owners
    tiles = width // units

    def place(k, s):
        return lax.rem(place_ref[2] + k, chunks), lax.rem(place_ref[1] + s, owners)

    down_s[...] = mm(act, cots_ref[...], 1, 1).astype(BF16)
    for k in range(chunks):
        for s in range(owners):
            at_k, at_d = place(k, s)
            start = pl.multiple_of((at_k * owners + at_d) * size, size)
            for t in range(tiles):
                outs[s][k, 0, t * size : (t + 1) * size, :] = down_s[
                    pl.ds(start, size), t * units : (t + 1) * units
                ]
    base = tiles * size
    size = width // (chunks * share * owners)
    for grad_act in (dgate, dup):
        in_s[...] = mm(rows_ref[...], grad_act, 1, 1).astype(BF16)
        for k in range(chunks):
            for q in range(share):
                for s in range(owners):
                    at_k, at_d = place(k, s)
                    start = pl.multiple_of(((at_k * share + q) * owners + at_d) * size, size)
                    to = base + q * size
                    outs[s][k, 0, to : to + size, :] = in_s[pl.ds(start, size), :]
        base += share * size


class Experts:
    def __init__(self, rows, cots, width, units, share, chunks, owners):
        self.arrays, self.plans = [], []
        for blocks in (rows, cots):
            arrays, plan = [], []
            for block in blocks:
                pieces = []
                for first, array, row in block:
                    known = [i for i, x in enumerate(arrays) if x is array]
                    if not known:
                        arrays.append(array)
                    pieces.append((first, known[0] if known else len(arrays) - 1, row))
                plan.append(pieces)
            self.arrays.append(arrays)
            self.plans.append(plan)
        self.blocks = len(rows)
        self.width, self.count = width, rows[0][0][1].shape[1]
        self.tokens = self.blocks * self.count
        self.units, self.share, self.chunks, self.owners = units, share, chunks, owners
        self.height = self.width // chunks // owners * 3

    def n_arrays(self):
        return sum(map(len, self.arrays))

    def scratch(self):
        wide = pltpu.VMEM((self.width, self.tokens), BF16)
        sems = [pltpu.SemaphoreType.DMA((sum(map(len, plan)),)) for plan in self.plans]
        return [wide, wide] + sems

    def copies(self, refs, rows_ref, cots_ref, row_sems, cot_sems):
        n = len(self.arrays[0])
        row_copies = piece_copies(self.plans[0], refs[:n], rows_ref, row_sems)
        cot_copies = piece_copies(self.plans[1], refs[n:], cots_ref, cot_sems)
        return [a + b for a, b in zip(row_copies, cot_copies)]

    def grads_structs(self, n):
        shape = (self.chunks, n, self.height, self.units)
        spec = pl.BlockSpec(
            (self.chunks, 1, self.height, self.units), lambda i, *_: (0, i, 0, 0)
        )
        return [jax.ShapeDtypeStruct(shape, BF16)] * self.owners, [spec] * self.owners

    def act_kernel(self, first, n, make_gates, e_ref, *refs):
        n_arrays = self.n_arrays()
        kept_ref, scales_ref, in_t_ref, down_ref = refs[:4]
        piece_refs, outs, scratch = refs[4 : 4 + n_arrays], refs[4 + n_arrays : -6], refs[-6:]
        if make_gates:
            chosen_ref = scales_ref
            gates_ref, scales_ref = outs[:2]
            outs = outs[2:]
        act_ref, dgate_ref, dup_ref, dscale_ref = outs[:4]
        rows_ref, cots_ref = scratch[:2]
        units, count, blocks = self.units, self.count, self.blocks
        copies = self.copies(piece_refs, *scratch[:4])
        step = pl.program_id(0)
        row = e_ref[0] + first + step

        def move(wait, start):
            def run():
                for b in start:
                    for copy in copies[b]:
                        copy.start()
                for copy in copies[wait]:
                    copy.wait()

            if n == 1:
                run()
            else:
                pl.when(step == 0)(run)

        def products(b):
            move(b, range(blocks) if b == 0 else ())
            cols = slice(b * count, (b + 1) * count)
            acts = jnp.dot(in_t_ref[...], rows_ref[:, cols], preferred_element_type=F32)
            grad = jnp.dot(down_ref[...], cots_ref[:, cols], preferred_element_type=F32)
            return acts, grad

        def finish(b, acts, grad):
            cols = slice(b * count, (b + 1) * count)
            gate, up = acts[:units], acts[units : 2 * units]
            if make_gates:
                chosen = chosen_ref[:, cols] > 0
                logits = jnp.where(chosen, acts[2 * units :], NEG_LARGE)
                gates = jnp.exp(logits - jnp.max(logits, 0, keepdims=True))
                gates = jnp.where(chosen, gates, 0.0)
                gates = gates / jnp.sum(gates, 0, keepdims=True)
                gates_ref[:, cols] = gates
                scales_ref[:, cols] = gates * kept_ref[:, cols]
            scale = scales_ref[pl.ds(row, 1), cols]
            keep = kept_ref[pl.ds(row, 1), cols]
            sigmoid = jax.nn.sigmoid(gate)
            silu = gate * sigmoid
            hidden = silu * up
            dscale_ref[0, 0:1, cols] = keep * jnp.sum(hidden * grad, 0, keepdims=True)
            act_ref[:, cols] = (hidden * scale).astype(BF16)
            grad = grad * scale
            dup_ref[:, cols] = (grad * silu).astype(BF16)
            dgate_ref[:, cols] = (grad * up * (sigmoid + silu * (1.0 - sigmoid))).astype(BF16)

        dscale_ref[...] = jnp.zeros_like(dscale_ref)
        for b in range(blocks):
            finish(b, *products(b))
        write_grads(
            rows_ref,
            cots_ref,
            act_ref[...],
            dgate_ref[...],
            dup_ref[...],
            e_ref,
            outs[4:],
            *scratch[4:],
            self.share,
        )

    def act(self, places, first, n, kept, scales, in_t, down, make_gates=False):
        units, width, tokens = self.units, self.width, self.tokens
        lanes = kept.shape[0]
        in_rows = 2 * units + (lanes if make_gates else 0)
        table = pl.BlockSpec((lanes, tokens), lambda i, e: (0, 0))
        one = pl.BlockSpec((units, tokens), lambda i, e: (i, 0))
        outs, specs = [], []
        if make_gates:
            outs += [jax.ShapeDtypeStruct((lanes, tokens), F32)] * 2
            specs += [table] * 2
        outs += [jax.ShapeDtypeStruct((n * units, tokens), BF16)] * 3
        specs += [one] * 3
        outs.append(jax.ShapeDtypeStruct((n, 8, tokens), F32))
        specs.append(pl.BlockSpec((1, 8, tokens), lambda i, e: (i, 0, 0)))
        structs, grad_specs = self.grads_structs(n)
        extra = [pltpu.VMEM((units, width), BF16), pltpu.VMEM((width, units), BF16)]
        return pl.pallas_call(
            functools.partial(self.act_kernel, first, n, make_gates),
            out_shape=tuple(outs + structs),
            grid_spec=pltpu.PrefetchScalarGridSpec(
                num_scalar_prefetch=1,
                grid=(n,),
                in_specs=[
                    table,
                    table,
                    pl.BlockSpec((in_rows, width), lambda i, e: (first + i, 0)),
                    pl.BlockSpec((units, width), lambda i, e: (first + i, 0)),
                ]
                + [pl.BlockSpec(memory_space=pl.ANY)] * self.n_arrays(),
                out_specs=tuple(specs + grad_specs),
                scratch_shapes=self.scratch() + extra,
            ),
            compiler_params=pltpu.CompilerParams(vmem_limit_bytes=60 << 20),
            cost_estimate=cost(
                flops=12 * width * units * tokens * n,
                transcendentals=units * tokens * n,
                bytes_accessed=4 * width * tokens + 6 * n * units * (width + tokens),
            ),
            name="experts_act",
        )(places, kept, scales, in_t, down, *self.arrays[0], *self.arrays[1])

    def out_kernel(self, parts, e_ref, weight_ref, *refs):
        act_refs, dscale_refs = refs[:parts], refs[parts : 2 * parts]
        message_ref, act_s, dscale_s = refs[2 * parts :]
        at = row = 0
        dscale_s[...] = jnp.zeros_like(dscale_s)
        for act_ref, dscale_ref in zip(act_refs, dscale_refs):
            act_s[at : at + act_ref.shape[0], :] = act_ref[...]
            at += act_ref.shape[0]
            for i in range(dscale_ref.shape[0]):
                dscale_s[pl.ds(e_ref[0] + row, 1), :] = dscale_ref[i, 0:1, :]
                row += 1
        width, lanes = self.width, dscale_s.shape[0]
        message_ref[0, :width, :] = jnp.dot(
            weight_ref[...], act_s[...], preferred_element_type=F32
        ).astype(BF16)
        grads = dscale_s[...]
        high = grads.astype(BF16)
        message_ref[0, width : width + lanes, :] = high
        message_ref[0, width + lanes :, :] = (grads - high.astype(F32)).astype(BF16)

    def out(self, places, lanes, weight, acts, dscales, first_block, n_blocks):
        rows = weight.shape[1]
        parts = len(acts)
        width, count = self.width, self.count

        def column(shape):
            return pl.BlockSpec(
                shape, lambda b, e: (0,) * (len(shape) - 1) + (first_block + b,)
            )

        return pl.pallas_call(
            functools.partial(self.out_kernel, parts),
            out_shape=jax.ShapeDtypeStruct((n_blocks, width + 2 * lanes, count), BF16),
            grid_spec=pltpu.PrefetchScalarGridSpec(
                num_scalar_prefetch=1,
                grid=(n_blocks,),
                in_specs=[
                    pl.BlockSpec(
                        (width, rows),
                        lambda b, e: (0, 0),
                        pipeline_mode=pl.Buffered(buffer_count=1),
                    )
                ]
                + [column((a.shape[0], count)) for a in acts]
                + [column((a.shape[0], 8, count)) for a in dscales],
                out_specs=pl.BlockSpec((1, width + 2 * lanes, count), lambda b, e: (b, 0, 0)),
                scratch_shapes=[pltpu.VMEM((rows, count), BF16), pltpu.VMEM((lanes, count), F32)],
            ),
            compiler_params=pltpu.CompilerParams(vmem_limit_bytes=60 << 20),
            cost_estimate=cost(
                flops=2 * width * rows * count * n_blocks,
                transcendentals=0,
                bytes_accessed=2 * width * rows + 4 * width * count * n_blocks,
            ),
            name="experts_out",
        )(places, weight, *acts, *dscales)

    def back_kernel(self, parts, gate_w_ref, up_w_ref, *refs):
        dgate_refs, dup_refs = refs[:parts], refs[parts : 2 * parts]
        back_ref, dgate_s, dup_s = refs[2 * parts :]
        for target, pieces in ((dgate_s, dgate_refs), (dup_s, dup_refs)):
            at = 0
            for piece in pieces:
                target[at : at + piece.shape[0], :] = piece[...]
                at += piece.shape[0]
        back = jnp.dot(gate_w_ref[...], dgate_s[...], preferred_element_type=F32)
        back = back + jnp.dot(up_w_ref[...], dup_s[...], preferred_element_type=F32)
        back_ref[0] = back.astype(BF16)

    def back(self, gate_w, up_w, dgates, dups, first_block, n_blocks):
        width, count = self.width, self.count
        rows = gate_w.shape[1]
        parts = len(dgates)
        whole = pl.BlockSpec(
            (width, rows), lambda b: (0, 0), pipeline_mode=pl.Buffered(buffer_count=1)
        )
        column = [pl.BlockSpec((a.shape[0], count), lambda b: (0, first_block + b)) for a in dgates]
        return pl.pallas_call(
            functools.partial(self.back_kernel, parts),
            out_shape=jax.ShapeDtypeStruct((n_blocks, width, count), BF16),
            grid=(n_blocks,),
            in_specs=[whole, whole] + column * 2,
            out_specs=pl.BlockSpec((1, width, count), lambda b: (b, 0, 0)),
            scratch_shapes=[pltpu.VMEM((rows, count), BF16)] * 2,
            compiler_params=pltpu.CompilerParams(vmem_limit_bytes=60 << 20),
            cost_estimate=cost(
                flops=4 * width * rows * count * n_blocks,
                transcendentals=0,
                bytes_accessed=4 * width * rows + 4 * width * count * n_blocks,
            ),
            name="experts_back",
        )(gate_w, up_w, *dgates, *dups)


def body(
    tokens,
    routes,
    cotangent,
    norm_attn,
    w_query,
    w_key,
    w_value,
    w_out,
    norm_ffn,
    w_router,
    w_gate,
    w_up,
    w_down,
):
    comm = Comm()
    hold = lax.optimization_barrier
    count, width = tokens.shape[1], tokens.shape[2]
    top_k = routes.shape[2]
    n_experts, _, hidden_units = w_gate.shape
    all_experts = n_experts * comm.n_expert
    capacity = (9 * count * top_k + 8 * all_experts - 1) // (8 * all_experts)
    n_context, n_dp, share = comm.n_context, comm.n_dp, comm.share
    expert_index = lax.axis_index("expert")
    context_index = lax.axis_index("context")
    dp_index = lax.axis_index("dp")
    parity = context_index % share
    chunks = n_context // share
    units = hidden_units // share
    lanes = -(-all_experts // 32) * 32
    places = jnp.stack([expert_index * n_experts, dp_index, context_index // share])

    cot_t = cotangent[0].T
    routed = (
        routes[0].T[:, None, :] == jnp.arange(lanes, dtype=jnp.int32)[None, :, None]
    ).astype(F32)
    cot_message = jnp.concatenate([cot_t, routed.sum(0).astype(BF16)])
    tokens, cot_message = hold((tokens, cot_message))
    across = [comm.pair(cot_message)] if share == 2 else []
    cots = [cot_message] + [comm.pull(cot_message, k, 0) for k in range(1, comm.columns)]

    hidden = tokens[0].T.astype(F32)
    gain_attn = norm_attn.astype(F32)[:, None]
    gain_ffn = norm_ffn.astype(F32)[:, None]
    scale_attn = rms_scale(hidden)
    normed_attn = (hidden * scale_attn * gain_attn).astype(BF16)
    positions = context_index * count + jnp.arange(count, dtype=jnp.int32)
    cosine, sine = rope_tables(positions)
    key_t = rotate_t(mm(w_key, normed_attn, 0, 0), cosine, sine).astype(BF16)
    value_t = mm(w_value, normed_attn, 0, 0).astype(BF16)
    kv_width = key_t.shape[0]
    kv_own = jnp.concatenate([key_t, value_t], 0)
    kv_blocks = [kv_own]
    for s in range(1, n_context):
        pairs = [(i, i + s) for i in range(n_context - s)]
        kv_blocks.append(lax.ppermute(kv_own, "context", pairs))
    query_t = rotate_t(mm(w_query, normed_attn, 0, 0), cosine, sine)
    query_t = (query_t * HEAD_DIM**-0.5).astype(BF16)

    weights = prepare_weights(parity, w_gate, w_up, w_down, hidden_units // n_context, share)
    router_t = jnp.zeros((lanes, width), BF16).at[:all_experts].set(w_router.T)
    in_t, gate_w, up_w, down, down_t = weights
    in_t = in_t.reshape(n_experts * 2 * units, width)
    in_first = jnp.concatenate([in_t[: 2 * units], router_t])
    if across:
        across, in_t, in_first = hold((across, in_t, in_first))
        across = across + [comm.pull(across[0], k, 0) for k in range(1, comm.columns)]
        cots, across[0], in_t = hold((cots, across[0], in_t))
    cots, across = [[[(0, x, 0)] for x in part] for part in (cots, across)]
    others = comm.from_core(cots) if comm.cores == 2 else []
    kv_blocks, in_t, in_first, gate_w, up_w, down, down_t = hold(
        (kv_blocks, in_t, in_first, gate_w, up_w, down, down_t)
    )
    out_t, out_low, lse = attention_forward(context_index, query_t, kv_blocks)
    middle = hidden + mm(w_out, out_low, 0, 0)
    scale_ffn = rms_scale(middle)
    normed_ffn = (middle * scale_ffn * gain_ffn).astype(BF16)
    across = [block[0][1] for block in across]
    across, normed_ffn = hold((across, normed_ffn))
    rows, across = comm.gather_group(normed_ffn, across)
    across = [[(0, x, 0)] for x in across]
    if comm.cores == 2 and across:
        others = others + comm.from_core(across)
    cots = cots + across + others

    routed_all = jnp.concatenate(
        [block[0][1][block[0][2] + width : block[0][2] + width + lanes] for block in cots]
    )
    n_blocks = len(cots)
    before = jnp.triu(jnp.ones((count, count), BF16), 1)
    ranking = mm(routed_all, before, 1, 0)
    chosen = routed_all.astype(F32)
    kept = jnp.where(ranking < capacity, chosen, 0.0)

    def side_by_side(array):
        array = array.reshape(n_blocks, lanes, count)
        return jnp.concatenate([array[b] for b in range(n_blocks)], 1)

    chosen, kept = side_by_side(chosen), side_by_side(kept)

    row_count = width // comm.n_expert

    def for_experts(*arrays):
        out = []
        for j in range(comm.cores):
            for k in range(comm.columns):
                column, core = expert_index // comm.cores, expert_index % comm.cores
                column = (column - k) % comm.columns
                target = column * comm.cores + (core + j) % comm.cores
                pieces = [
                    lax.dynamic_slice_in_dim(array, target * row_count, row_count, 0)
                    for array in arrays
                ]
                out.append(jnp.concatenate(pieces))
        return out

    def to_experts(pieces):
        peers = [(j, k) for j in range(comm.cores) for k in range(comm.columns)]
        return pieces[:1] + [comm.pull(x, k, j) for x, (j, k) in zip(pieces[1:], peers[1:])]

    columns_sent = for_experts(normed_attn, out_low)
    chosen, columns_sent = hold((chosen, columns_sent))

    own = Experts(rows, cots, width, units, share, chunks, n_dp)
    groups, at = [], 0
    for n in (1, (n_experts - 1) // 2, n_experts - 1 - (n_experts - 1) // 2):
        if n:
            groups.append((at, n))
            at += n
    acts, dgates, dups, dscales, kept_parts, arrived, crossing = ([] for _ in range(7))
    scales = None

    def pass_on(g, values):
        if g >= len(groups):
            return values
        terms, values = hold((arrived[g], values))
        terms = [kept_parts[g]] + terms

        def part(k):
            return sum(term[k].astype(F32) for term in terms)

        sent = comm.send_context([part(k).astype(BF16) for k in range(1, chunks)], share)
        crossing.append([part(0).astype(BF16)] + sent)
        return values

    for g, (first, n) in enumerate(groups):
        if g == 0:
            gates_all, scales, *done = own.act(
                places, first, n, kept, chosen, in_first, down, make_gates=True
            )
        else:
            done = own.act(places, first, n, kept, scales, in_t, down)
        for target, value in zip((acts, dgates, dups, dscales, kept_parts), done):
            target.append(value)
        arrived.append(comm.send_dp(done[5:]))
        if g == 0:
            scales, columns_sent = hold((scales, columns_sent))
            columns_got = to_experts(columns_sent)
        if g == 1:
            scales = pass_on(0, scales)

    columns_got, acts = hold((columns_got, acts))
    h1_rows = [x[:row_count] for x in columns_got]
    ob_rows = [x[row_count:] for x in columns_got]
    near_count = n_blocks // comm.cores

    def both_cores(call):
        other = None
        if comm.cores == 2:
            other = comm.push(call(near_count, near_count), 0, 1)
        return call(0, near_count), other

    message = both_cores(
        lambda first, n: own.out(places, lanes, down_t, acts, dscales, first, n)
    )
    back_other = None
    if comm.cores == 2:
        back_other = own.back(gate_w, up_w, dgates, dups, near_count, near_count)
        back_other = comm.push(back_other, 0, 1)
    message, dgates = hold((message, dgates))
    dgates, crossing[0] = pass_on(1, (dgates, crossing[0]))
    back_near = own.back(gate_w, up_w, dgates, dups, 0, near_count)
    message = comm.return_hops(*message)
    message, back_near = hold((message, back_near))
    back = comm.return_hops(back_near, back_other)
    returned = comm.return_last(message)
    back = pass_on(2, back)
    grad_normed_ffn = comm.return_last(back)
    result = (middle + returned[:width]).astype(BF16)
    grad_gates = returned[width : width + lanes] + returned[width + lanes :]
    gates_own = gates_all[:, :count]

    upstream = cot_t.astype(F32)
    mean_grad = jnp.sum(gates_own * grad_gates, 0, keepdims=True)
    grad_logits = (gates_own * (grad_gates - mean_grad)).astype(BF16)
    grad_normed_ffn = grad_normed_ffn + mm(router_t, grad_logits, 0, 0)
    grad_gain_ffn = jnp.sum(grad_normed_ffn * middle * scale_ffn, 1)
    grad_middle = upstream + norm_back(grad_normed_ffn, middle, scale_ffn, gain_ffn)
    grad_branch = grad_middle.astype(BF16)

    gain_grid = grad_gain_ffn.reshape(-1, count)
    gain_lines = gain_grid.shape[0]
    gain_high = lax.reduce_precision(gain_grid, 8, 7)
    gain_rows = jnp.concatenate([gain_high, gain_grid - gain_high]).astype(BF16)
    gain_rows = jnp.pad(gain_rows, ((0, -2 * gain_lines % 16), (0, 0)))
    branch_all = comm.gather_columns(jnp.concatenate([grad_branch, grad_logits, gain_rows]))
    grad_attn_t = mm(w_out, grad_branch, 1, 0).astype(BF16)

    def attention_half(first, heads):
        return attention_backward(
            context_index, query_t, grad_attn_t, out_t, lse, kv_blocks, first, heads
        )

    def to_keys(grad_kv):
        return lax.all_to_all(grad_kv, "context", 0, 0, tiled=True)

    size_down = units // chunks // n_dp
    tiles = width // units

    def total_of(terms):
        total = jnp.concatenate([sum(x.astype(F32) for x in group) for group in terms])
        n = total.shape[0]
        part = total[:, : tiles * size_down].reshape(n, tiles, size_down, units)
        down = jnp.swapaxes(part, 1, 2).reshape(n, size_down, width)
        part = total[:, tiles * size_down :]
        return down, part.reshape(n, 2, share, part.shape[1] // 2 // share, units)

    def send_pair(part):
        if share == 1:
            return part[:, :, 0], None
        keep = lax.dynamic_index_in_dim(part, parity, 2, False)
        send = lax.dynamic_index_in_dim(part, 1 - parity, 2, False)
        return keep, comm.pair(send.astype(BF16))

    def both_columns(keep, other):
        if other is None:
            return keep
        other = other.astype(F32)
        first = jnp.where(parity == 0, keep, other)
        second = jnp.where(parity == 0, other, keep)
        chunk = hidden_units // n_context
        pieces = []
        for q in range(chunks):
            pieces += [x[..., q * chunk : (q + 1) * chunk] for x in (first, second)]
        return jnp.concatenate(pieces, -1)

    early = crossing[:-1]
    early, grad_attn_t = hold((early, grad_attn_t))
    totals = [total_of(early)] if early else []
    pairs = [send_pair(part) for _, part in totals]
    half = KV_HEADS // 2
    grad_query_a, grad_kv_a = attention_half(0, half)
    kv_a = to_keys(grad_kv_a)
    branch_all, grad_attn_t = hold((branch_all, grad_attn_t))
    branch_all = comm.gather_cores(branch_all)
    grad_query_b, grad_kv_b = attention_half(half, half)
    kv_a, grad_kv_b, branch_all, crossing[-1] = hold((kv_a, grad_kv_b, branch_all, crossing[-1]))
    kv_b = to_keys(grad_kv_b)

    out_terms = comm.scatter_rows(ob_rows, branch_all, width)
    h2_rows = [
        lax.dynamic_slice_in_dim(array, at + expert_index * row_count, row_count, 0)
        for j in range(comm.cores)
        for ((_, array, at),) in rows[j * near_count : j * near_count + comm.columns]
    ]
    router_rows = sum(mm(a, b[width : width + lanes], 1, 1) for a, b in zip(h2_rows, branch_all))
    gain_total = sum(x[width + lanes :].astype(F32) for x in branch_all)
    gain_total = gain_total[:gain_lines] + gain_total[gain_lines : 2 * gain_lines]
    gain_part = lax.dynamic_slice_in_dim(
        gain_total.reshape(width), expert_index * row_count, row_count, 0
    )
    rest = jnp.zeros((row_count, LANES - lanes - 1), F32)
    extra = jnp.concatenate([router_rows, gain_part[:, None], rest], 1).astype(BF16)
    extra = extra.reshape(n_context * n_dp, -1, LANES)
    extra, kv_b = hold((extra, kv_b))
    extra = lax.all_to_all(extra, ("context", "dp"), 0, 0, tiled=True)
    extra = jnp.sum(extra.astype(F32), 0)

    grad_query_raw = jnp.concatenate(
        [rotate_t(x, cosine, -sine).astype(BF16) for x in (grad_query_a, grad_query_b)]
    )
    query_terms = comm.scatter_rows(h1_rows, comm.gather_expert(grad_query_raw), width)
    late = crossing[-1]
    pairs, kv_b = hold((pairs, kv_b))
    totals.append(total_of([late]))
    pairs.append(send_pair(totals[-1][1]))
    kv_sums = [jnp.sum(x.astype(F32), 0) for x in (kv_a, kv_b)]
    grad_key_raw = [rotate_t(kv_sum[0], cosine, -sine).astype(BF16) for kv_sum in kv_sums]
    grad_kv_raw = jnp.concatenate(grad_key_raw + [kv_sum[1].astype(BF16) for kv_sum in kv_sums])
    near_kv = comm.gather_columns(grad_kv_raw)
    near_kv, out_terms, query_terms = hold((near_kv, out_terms, query_terms))
    out_sum, query_sum = comm.scatter_rest(out_terms), comm.scatter_rest(query_terms)
    kv_terms = comm.scatter_rows(h1_rows, comm.gather_cores(near_kv), 2 * kv_width)
    kv_rows = comm.scatter_rest(kv_terms)
    key_sum, value_sum = kv_rows[:, :kv_width], kv_rows[:, kv_width:]

    down_sum = jnp.concatenate([down for down, _ in totals])
    parts = [both_columns(*pair) for pair in pairs]
    gate_sum = jnp.concatenate([part[:, 0] for part in parts])
    up_sum = jnp.concatenate([part[:, 1] for part in parts])

    shard = (expert_index * n_context + context_index) * n_dp + dp_index
    shard_rows = query_sum.shape[0]

    def shard_of(array):
        return lax.dynamic_slice_in_dim(array, shard * shard_rows, shard_rows, 0).astype(F32)

    gain_sum = (
        jnp.sum(shard_of(w_query) * query_sum, 1)
        + jnp.sum(shard_of(w_key) * key_sum, 1)
        + jnp.sum(shard_of(w_value) * value_sum, 1)
    ) / shard_of(norm_attn)

    grad_normed_attn = mm(w_query, grad_query_raw, 1, 0)
    grad_normed_attn = grad_normed_attn + mm(w_key, grad_kv_raw[:kv_width], 1, 0)
    grad_normed_attn = grad_normed_attn + mm(w_value, grad_kv_raw[kv_width:], 1, 0)
    grad_hidden = grad_middle + norm_back(grad_normed_attn, hidden, scale_attn, gain_attn)
    return (
        result.T[None],
        grad_hidden.astype(BF16).T[None],
        gain_sum,
        query_sum,
        key_sum,
        value_sum,
        out_sum,
        extra[:, lanes],
        extra[:, :all_experts],
        gate_sum,
        up_sum,
        down_sum,
    )


def solution(mesh):
    rows = P(("expert", "dp"), "context", None)
    dense = P(("expert", "context", "dp"), None)
    vector = P(("expert", "context", "dp"))
    experts = P("expert", None, None)
    expert_grads = P("expert", ("context", "dp"), None)
    return jax.shard_map(
        body,
        mesh=mesh,
        in_specs=(rows, rows, rows) + (P(),) * 7 + (experts,) * 3,
        out_specs=(rows, rows, vector, dense, dense, dense, dense, vector, dense)
        + (expert_grads,) * 3,
        check_vma=False,
    )
```

```python
import functools

import jax
import jax.numpy as jnp
from jax import lax
from jax.experimental import pallas as pl
from jax.experimental.pallas import tpu as pltpu
from jax.sharding import PartitionSpec as P

HEADS = 24
KV_HEADS = 8
HEAD_DIM = 64
GROUP = HEADS // KV_HEADS


EPS = 1e-05
ROPE_BASE = 10000.0
NEG_LARGE = -1e30
F32 = jnp.float32
BF16 = jnp.bfloat16
LANES = 128


def cost(flops, bytes_accessed, transcendentals=0):
    scale = 64
    return pl.CostEstimate(
        flops=flops // scale,
        bytes_accessed=bytes_accessed // scale,
        transcendentals=transcendentals // scale,
    )


def rms_scale(values):
    return lax.rsqrt(jnp.mean(values * values, 0, keepdims=True) + EPS)


def norm_back(grad_out, values, scale, gain):
    weighted = gain * grad_out
    return scale * weighted - values * scale**3 * jnp.mean(weighted * values, 0, keepdims=True)


def mm(a, b, da, db):
    return lax.dot_general(a, b, (((da,), (db,)), ((), ())), preferred_element_type=F32)


class Comm:
    def __init__(self):
        self.n_expert = lax.axis_size("expert")
        self.n_context = lax.axis_size("context")
        self.n_dp = lax.axis_size("dp")
        self.cores = 2 if self.n_expert % 2 == 0 else 1
        self.columns = self.n_expert // self.cores
        self.share = 2 if self.n_context % 2 == 0 else 1

    def peer(self, i, k, j):
        column, core = divmod(i, self.cores)
        return ((column + k) % self.columns) * self.cores + (core + j) % self.cores

    def pull(self, value, k, j):
        pairs = [(self.peer(i, k, j), i) for i in range(self.n_expert)]
        return lax.ppermute(value, "expert", pairs)

    def push(self, value, k, j):
        pairs = [(i, self.peer(i, k, j)) for i in range(self.n_expert)]
        return lax.ppermute(value, "expert", pairs)

    def pair(self, value):
        return lax.ppermute(value, "context", [(i, i ^ 1) for i in range(self.n_context)])

    def from_core(self, blocks):
        arrays = [array for block in blocks for _, array, _ in block]
        moved = self.pull(jnp.concatenate(arrays) if len(arrays) > 1 else arrays[0], 0, 1)
        out, at = [], 0
        for block in blocks:
            pieces = []
            for row, array, _ in block:
                pieces.append((row, moved, at))
                at += array.shape[0]
            out.append(pieces)
        return out

    def gather_columns(self, value):
        return [value] + [self.pull(value, k, 0) for k in range(1, self.columns)]

    def gather_cores(self, near):
        if self.cores == 2:
            near = near + [self.pull(block, 0, 1) for block in near]
        return near

    def gather_expert(self, value):
        return self.gather_cores(self.gather_columns(value))

    def gather_group(self, value, beside):
        columns = [self.pull(value, k, 0) for k in range(1, self.columns)]
        far = []
        if self.share == 2:
            half = value.shape[0] // 2
            across = self.pair(value)
            columns, across, beside = lax.optimization_barrier((columns, across, beside))
        first = [[(0, value, 0)]] + [[(0, block, 0)] for block in columns]
        if self.share == 2:
            first.append([(0, across, 0)])
            for k in range(1, self.columns):
                top = self.pull(across[:half], k, 0)
                bottom = self.pair(columns[k - 1][half:])
                far.append([(0, top, 0), (half, bottom, 0)])
        blocks = first + far
        if self.cores == 2:
            blocks = blocks + self.from_core(first)
            blocks = blocks + (self.from_core(far) if far else [])
        return blocks, beside

    def return_hops(self, near, other):
        columns = self.columns
        shape = (self.share, columns) + near.shape[1:]
        arrays = [x.reshape(shape) for x in (near, other) if x is not None]

        def part(*at):
            return sum(array[at].astype(F32) for array in arrays)

        if self.share == 1:
            sent = [self.push(part(0, k).astype(BF16), k, 0) for k in range(1, columns)]
            return [part(0, 0)] + sent
        half = near.shape[1] // 2
        low, high = slice(0, half), slice(half, 2 * half)
        every = slice(None)
        by_column = [
            self.push(part(every, k, low).astype(BF16), k, 0) for k in range(1, columns)
        ]
        by_pair = self.pair(part(1, every, high).astype(BF16))
        return [part(every, 0, low)] + by_column + [part(0, every, high), by_pair]

    def return_last(self, terms):
        columns = self.columns
        if self.share == 1:
            return sum(term.astype(F32) for term in terms)
        top = terms[:columns]
        bottom = terms[columns : columns + 2]

        def total(parts, at):
            return sum(part[at].astype(F32) for part in parts)

        top_other = self.pair(total(top, 1).astype(BF16))
        others = [
            self.push(total(bottom, k).astype(BF16), k, 0).astype(F32)
            for k in range(1, columns)
        ]
        return jnp.concatenate(
            [total(top, 0) + top_other.astype(F32), sum(others, total(bottom, 0))]
        )

    def send_dp(self, parts):
        n = self.n_dp
        return [
            lax.ppermute(parts[s - 1], "dp", [(i, (i + s) % n) for i in range(n)])
            for s in range(1, n)
        ]

    def send_context(self, parts, stride):
        n = self.n_context // stride
        out = []
        for s in range(1, n):
            pairs = []
            for i in range(self.n_context):
                k, r = divmod(i, stride)
                pairs.append((i, ((k + s) % n) * stride + r))
            out.append(lax.ppermute(parts[s - 1], "context", pairs))
        return out

    def scatter_rows(self, left, right, width):
        n, m = self.n_context, self.n_dp
        c, d = lax.axis_index("context"), lax.axis_index("dp")
        size = left[0].shape[0] // (n * m)
        if size % 16 == 0:
            mine, *parts = row_products(jnp.stack([c, d]), left, right, width, n, m)
        else:
            local = sum(mm(a, b[:width], 1, 1) for a, b in zip(left, right))
            local = local.reshape(n, m, size, width)
            local = jnp.stack(
                [lax.dynamic_index_in_dim(local, (c + k) % n, 0, False) for k in range(n)]
            )
            mine, *parts = [
                lax.dynamic_index_in_dim(local, (d + s) % m, 1, False) for s in range(m)
            ]
        return [mine] + self.send_dp([part.astype(BF16) for part in parts])

    def scatter_rest(self, terms):
        n = self.n_context

        def of_context(k):
            return sum(x[k].astype(F32) for x in terms)

        came_far = self.send_context([of_context(k).astype(BF16) for k in range(1, n)], 1)
        return of_context(0) + sum(x.astype(F32) for x in came_far)


def row_products_kernel(count, place_ref, *refs):
    left, right, outs, total_s = refs[:count], refs[count : 2 * count], refs[2 * count : -1], refs[-1]
    width = total_s.shape[1]
    total_s[...] = mm(
        jnp.concatenate([a[...] for a in left], 1),
        jnp.concatenate([b[:width, :] for b in right], 1),
        1,
        1,
    )
    n, size, _ = outs[0].shape
    m = len(outs)
    for k in range(n):
        for s in range(m):
            owner = lax.rem(place_ref[0] + k, n) * m + lax.rem(place_ref[1] + s, m)
            rows = pl.ds(pl.multiple_of(owner * size, size), size)
            outs[s][k] = total_s[rows, :].astype(outs[s].dtype)


def row_products(place, left, right, width, n, m):
    rows = left[0].shape[0]
    size = rows // (n * m)

    def whole(shape):
        return pl.BlockSpec(shape, lambda i, p: (0,) * len(shape))

    return pl.pallas_call(
        functools.partial(row_products_kernel, len(left)),
        out_shape=tuple(
            jax.ShapeDtypeStruct((n, size, width), BF16 if s else F32) for s in range(m)
        ),
        grid_spec=pltpu.PrefetchScalarGridSpec(
            num_scalar_prefetch=1,
            grid=(1,),
            in_specs=[whole(x.shape) for x in left + right],
            out_specs=tuple(whole((n, size, width)) for _ in range(m)),
            scratch_shapes=[pltpu.VMEM((rows, width), F32)],
        ),
        compiler_params=pltpu.CompilerParams(vmem_limit_bytes=32 << 20),
        cost_estimate=cost(
            flops=2 * rows * width * right[0].shape[1] * len(left),
            bytes_accessed=8 * width * right[0].shape[1] + 6 * rows * width,
        ),
        name="row_products",
    )(place, *left, *right)


def heads_side_by_side(ref):
    hd = HEAD_DIM
    return jnp.concatenate([ref[g * hd : (g + 1) * hd, :] for g in range(GROUP)], 1)


def causal(shape, n):
    key = lax.broadcasted_iota(jnp.int32, shape, 0)
    query = lax.rem(lax.broadcasted_iota(jnp.int32, shape, 1), n)
    return key <= query


def attn_fwd_kernel(blocks, c_ref, q_ref, *refs):
    k_refs, v_refs = refs[:blocks], refs[blocks : 2 * blocks]
    o_ref, ob_ref, lse_ref, scores_ref = refs[2 * blocks :]
    c = c_ref[0]
    n = q_ref.shape[1]
    hd = HEAD_DIM
    queries = heads_side_by_side(q_ref)
    for s in range(blocks):
        rows = slice(s * n, (s + 1) * n)

        def fill(s=s, rows=rows):
            scores = mm(k_refs[s][...], queries, 0, 0)
            if s == 0:
                scores = jnp.where(causal(scores.shape, n), scores, NEG_LARGE)
            scores_ref[rows, :] = scores

        def blank(rows=rows):
            scores_ref[rows, :] = jnp.full((n, GROUP * n), NEG_LARGE, F32)

        if s == 0:
            fill()
        else:
            pl.when(c >= s)(fill)
            pl.when(c < s)(blank)
    lse_ref[...] = jnp.zeros_like(lse_ref)
    for g in range(GROUP):
        cols = slice(g * n, (g + 1) * n)
        scores = scores_ref[:, cols]
        top = jnp.max(scores, 0, keepdims=True)
        weights = jnp.exp(scores - top)
        total = jnp.sum(weights, 0, keepdims=True)
        weights = weights.astype(BF16)
        out = jnp.zeros((hd, n), F32)
        for s in range(blocks):
            out = out + mm(v_refs[s][...], weights[s * n : (s + 1) * n], 1, 0)
        out = out / total
        o_ref[g * hd : (g + 1) * hd, :] = out
        ob_ref[g * hd : (g + 1) * hd, :] = out.astype(BF16)
        lse_ref[0, g : g + 1, :] = top + jnp.log(total)


def kv_specs(blocks, n, first=0):
    keys = [pl.BlockSpec((HEAD_DIM, n), lambda h, c: (first + h, 0))] * blocks
    values = [pl.BlockSpec((HEAD_DIM, n), lambda h, c: (first + h + KV_HEADS, 0))] * blocks
    return keys + values


def attention_forward(context_index, query_t, kv_blocks):
    blocks = len(kv_blocks)
    n = query_t.shape[1]
    wide = GROUP * HEAD_DIM
    heads = query_t.shape[0] // wide
    head = pl.BlockSpec((wide, n), lambda h, c: (h, 0))
    return pl.pallas_call(
        functools.partial(attn_fwd_kernel, blocks),
        out_shape=(
            jax.ShapeDtypeStruct(query_t.shape, F32),
            jax.ShapeDtypeStruct(query_t.shape, BF16),
            jax.ShapeDtypeStruct((heads, 8, n), F32),
        ),
        grid_spec=pltpu.PrefetchScalarGridSpec(
            num_scalar_prefetch=1,
            grid=(heads,),
            in_specs=[head] + kv_specs(blocks, n),
            out_specs=(head, head, pl.BlockSpec((1, 8, n), lambda h, c: (h, 0, 0))),
            scratch_shapes=[pltpu.VMEM((blocks * n, GROUP * n), F32)],
        ),
        compiler_params=pltpu.CompilerParams(vmem_limit_bytes=40 << 20),
        cost_estimate=cost(
            flops=heads * GROUP * blocks * n * n * 256 * 4,
            transcendentals=heads * GROUP * blocks * n * n,
            bytes_accessed=16 * query_t.size,
        ),
        name="attn_fwd",
    )(context_index.reshape(1), query_t, *kv_blocks, *kv_blocks)


def attn_bwd_kernel(blocks, c_ref, q_ref, do_ref, o_ref, lse_ref, *refs):
    k_refs, v_refs = refs[:blocks], refs[blocks : 2 * blocks]
    dq_ref, dkv_ref = refs[2 * blocks :]
    c = c_ref[0]
    n = q_ref.shape[1]
    hd = HEAD_DIM
    queries, grads = heads_side_by_side(q_ref), heads_side_by_side(do_ref)
    deltas, lses = [], []
    for g in range(GROUP):
        head = slice(g * hd, (g + 1) * hd)
        both = do_ref[head, :].astype(F32) * o_ref[head, :]
        deltas.append(jnp.sum(both, 0, keepdims=True))
        lses.append(lse_ref[0, g : g + 1, :])
    delta, lse = jnp.concatenate(deltas, 1), jnp.concatenate(lses, 1)
    for s in range(blocks):

        def work(s=s):
            key_t = k_refs[s][...]
            weights = jnp.exp(mm(key_t, queries, 0, 0) - lse)
            if s == 0:
                weights = jnp.where(causal(weights.shape, n), weights, 0.0)
            grad_weights = mm(v_refs[s][...], grads, 0, 0)
            grad_scores = (weights * (grad_weights - delta)).astype(BF16)
            owner = lax.rem(c - s + blocks, blocks)
            dkv_ref[owner, 0] = mm(queries, grad_scores, 1, 1).astype(BF16)
            dkv_ref[owner, 1] = mm(grads, weights.astype(BF16), 1, 1).astype(BF16)
            step = mm(key_t, grad_scores, 1, 0) * (HEAD_DIM**-0.5)
            for g in range(GROUP):
                head, cols = slice(g * hd, (g + 1) * hd), slice(g * n, (g + 1) * n)
                if s == 0:
                    dq_ref[head, :] = step[:, cols]
                else:
                    dq_ref[head, :] += step[:, cols]

        def skip(s=s):
            owner = lax.rem(c - s + blocks, blocks)
            dkv_ref[owner] = jnp.zeros(dkv_ref.shape[1:], BF16)

        if s == 0:
            work()
        else:
            pl.when(c >= s)(work)
            pl.when(c < s)(skip)


def attention_backward(context_index, query_t, grad_t, out_t, lse, kv_blocks, first, heads):
    blocks = len(kv_blocks)
    n = query_t.shape[1]
    wide = GROUP * HEAD_DIM
    head = pl.BlockSpec((wide, n), lambda h, c: (first + h, 0))
    out = pl.BlockSpec((wide, n), lambda h, c: (h, 0))
    return pl.pallas_call(
        functools.partial(attn_bwd_kernel, blocks),
        out_shape=(
            jax.ShapeDtypeStruct((heads * wide, n), F32),
            jax.ShapeDtypeStruct((blocks, 2, heads * HEAD_DIM, n), BF16),
        ),
        grid_spec=pltpu.PrefetchScalarGridSpec(
            num_scalar_prefetch=1,
            grid=(heads,),
            in_specs=[head, head, head, pl.BlockSpec((1, 8, n), lambda h, c: (first + h, 0, 0))]
            + kv_specs(blocks, n, first),
            out_specs=(
                out,
                pl.BlockSpec((blocks, 2, HEAD_DIM, n), lambda h, c: (0, 0, h, 0)),
            ),
        ),
        compiler_params=pltpu.CompilerParams(vmem_limit_bytes=40 << 20),
        cost_estimate=cost(
            flops=heads * GROUP * blocks * n * n * 256 * 10,
            transcendentals=heads * GROUP * blocks * n * n,
            bytes_accessed=20 * query_t.size,
        ),
        name="attn_bwd",
    )(context_index.reshape(1), query_t, grad_t, out_t, lse, *kv_blocks, *kv_blocks)


def rope_tables(positions):
    half_dim = HEAD_DIM // 2
    frequency = ROPE_BASE ** (-2.0 * jnp.arange(half_dim, dtype=F32) / HEAD_DIM)
    angles = frequency[:, None] * positions.astype(F32)[None, :]
    return jnp.cos(angles), jnp.sin(angles)


def rotate_t(values_t, cosine, sine):
    shaped = values_t.reshape(-1, 2, HEAD_DIM // 2, values_t.shape[1])
    low, high = shaped[:, 0], shaped[:, 1]
    turned = jnp.stack([low * cosine - high * sine, high * cosine + low * sine], 1)
    return turned.reshape(values_t.shape)


def prepare_kernel(p_ref, gate_ref, up_ref, down_ref, *outs):
    in_t_ref, gate_out, up_out, down_out, down_t_out = outs
    gate, up, down = gate_ref[0], up_ref[0], down_ref[0]
    in_t_ref[0, 0, 0] = gate.astype(F32).T.astype(BF16)
    in_t_ref[0, 1, 0] = up.astype(F32).T.astype(BF16)
    gate_out[...] = gate
    up_out[...] = up
    down_out[...] = down
    down_t_out[...] = down.astype(F32).T.astype(BF16)


def prepare_weights(parity, w_gate, w_up, w_down, chunk, share):
    experts, width, hidden = w_gate.shape
    chunks = hidden // chunk // share
    units = chunks * chunk

    def column(e, q, p):
        return (e, 0, q * share + p[0])

    def flat(e, q, p):
        return (0, e * chunks + q)

    return pl.pallas_call(
        prepare_kernel,
        out_shape=(
            jax.ShapeDtypeStruct((experts, 2, chunks, chunk, width), BF16),
            jax.ShapeDtypeStruct((width, experts * units), BF16),
            jax.ShapeDtypeStruct((width, experts * units), BF16),
            jax.ShapeDtypeStruct((experts * units, width), BF16),
            jax.ShapeDtypeStruct((width, experts * units), BF16),
        ),
        grid_spec=pltpu.PrefetchScalarGridSpec(
            num_scalar_prefetch=1,
            grid=(experts, chunks),
            in_specs=[
                pl.BlockSpec((1, width, chunk), column),
                pl.BlockSpec((1, width, chunk), column),
                pl.BlockSpec((1, chunk, width), lambda e, q, p: (e, q * share + p[0], 0)),
            ],
            out_specs=(
                pl.BlockSpec((1, 2, 1, chunk, width), lambda e, q, p: (e, 0, q, 0, 0)),
                pl.BlockSpec((width, chunk), flat),
                pl.BlockSpec((width, chunk), flat),
                pl.BlockSpec((chunk, width), lambda e, q, p: (e * chunks + q, 0)),
                pl.BlockSpec((width, chunk), flat),
            ),
        ),
        compiler_params=pltpu.CompilerParams(vmem_limit_bytes=60 << 20),
        cost_estimate=cost(
            flops=0, transcendentals=0, bytes_accessed=18 * experts * width * units
        ),
        name="prepare_weights",
    )(parity.reshape(1), w_gate, w_up, w_down)


def piece_copies(blocks, refs, target_ref, sems):
    out, at = [], 0
    count = refs[0].shape[1]
    for b, pieces in enumerate(blocks):
        copies = []
        for i, (first, ref, row) in enumerate(pieces):
            last = pieces[i + 1][0] if i + 1 < len(pieces) else target_ref.shape[0]
            copies.append(
                pltpu.make_async_copy(
                    refs[ref].at[row : row + last - first],
                    target_ref.at[first:last, b * count : (b + 1) * count],
                    sems.at[at],
                )
            )
            at += 1
        out.append(copies)
    return out


def write_grads(rows_ref, cots_ref, act, dgate, dup, place_ref, outs, down_s, in_s, share):
    owners = len(outs)
    chunks, _, _, units = outs[0].shape
    width = rows_ref.shape[0]
    size = units // chunks // owners
    tiles = width // units

    def place(k, s):
        return lax.rem(place_ref[2] + k, chunks), lax.rem(place_ref[1] + s, owners)

    down_s[...] = mm(act, cots_ref[...], 1, 1).astype(BF16)
    for k in range(chunks):
        for s in range(owners):
            at_k, at_d = place(k, s)
            start = pl.multiple_of((at_k * owners + at_d) * size, size)
            for t in range(tiles):
                outs[s][k, 0, t * size : (t + 1) * size, :] = down_s[
                    pl.ds(start, size), t * units : (t + 1) * units
                ]
    base = tiles * size
    size = width // (chunks * share * owners)
    for grad_act in (dgate, dup):
        in_s[...] = mm(rows_ref[...], grad_act, 1, 1).astype(BF16)
        for k in range(chunks):
            for q in range(share):
                for s in range(owners):
                    at_k, at_d = place(k, s)
                    start = pl.multiple_of(((at_k * share + q) * owners + at_d) * size, size)
                    to = base + q * size
                    outs[s][k, 0, to : to + size, :] = in_s[pl.ds(start, size), :]
        base += share * size


class Experts:
    def __init__(self, rows, cots, width, units, share, chunks, owners):
        self.arrays, self.plans = [], []
        for blocks in (rows, cots):
            arrays, plan = [], []
            for block in blocks:
                pieces = []
                for first, array, row in block:
                    known = [i for i, x in enumerate(arrays) if x is array]
                    if not known:
                        arrays.append(array)
                    pieces.append((first, known[0] if known else len(arrays) - 1, row))
                plan.append(pieces)
            self.arrays.append(arrays)
            self.plans.append(plan)
        self.blocks = len(rows)
        self.width, self.count = width, rows[0][0][1].shape[1]
        self.tokens = self.blocks * self.count
        self.units, self.share, self.chunks, self.owners = units, share, chunks, owners
        self.height = self.width // chunks // owners * 3

    def n_arrays(self):
        return sum(map(len, self.arrays))

    def scratch(self):
        wide = pltpu.VMEM((self.width, self.tokens), BF16)
        sems = [pltpu.SemaphoreType.DMA((sum(map(len, plan)),)) for plan in self.plans]
        return [wide, wide] + sems

    def copies(self, refs, rows_ref, cots_ref, row_sems, cot_sems):
        n = len(self.arrays[0])
        row_copies = piece_copies(self.plans[0], refs[:n], rows_ref, row_sems)
        cot_copies = piece_copies(self.plans[1], refs[n:], cots_ref, cot_sems)
        return [a + b for a, b in zip(row_copies, cot_copies)]

    def grads_structs(self, n):
        shape = (self.chunks, n, self.height, self.units)
        spec = pl.BlockSpec(
            (self.chunks, 1, self.height, self.units), lambda i, *_: (0, i, 0, 0)
        )
        return [jax.ShapeDtypeStruct(shape, BF16)] * self.owners, [spec] * self.owners

    def act_kernel(self, first, n, make_gates, e_ref, *refs):
        n_arrays = self.n_arrays()
        kept_ref, scales_ref, in_t_ref, down_ref = refs[:4]
        piece_refs, outs, scratch = refs[4 : 4 + n_arrays], refs[4 + n_arrays : -6], refs[-6:]
        if make_gates:
            chosen_ref = scales_ref
            gates_ref, scales_ref = outs[:2]
            outs = outs[2:]
        act_ref, dgate_ref, dup_ref, dscale_ref = outs[:4]
        rows_ref, cots_ref = scratch[:2]
        units, count, blocks = self.units, self.count, self.blocks
        copies = self.copies(piece_refs, *scratch[:4])
        step = pl.program_id(0)
        row = e_ref[0] + first + step

        def move(wait, start):
            def run():
                for b in start:
                    for copy in copies[b]:
                        copy.start()
                for copy in copies[wait]:
                    copy.wait()

            if n == 1:
                run()
            else:
                pl.when(step == 0)(run)

        def products(b):
            move(b, range(blocks) if b == 0 else ())
            cols = slice(b * count, (b + 1) * count)
            acts = jnp.dot(in_t_ref[...], rows_ref[:, cols], preferred_element_type=F32)
            grad = jnp.dot(down_ref[...], cots_ref[:, cols], preferred_element_type=F32)
            return acts, grad

        def finish(b, acts, grad):
            cols = slice(b * count, (b + 1) * count)
            gate, up = acts[:units], acts[units : 2 * units]
            if make_gates:
                chosen = chosen_ref[:, cols] > 0
                logits = jnp.where(chosen, acts[2 * units :], NEG_LARGE)
                gates = jnp.exp(logits - jnp.max(logits, 0, keepdims=True))
                gates = jnp.where(chosen, gates, 0.0)
                gates = gates / jnp.sum(gates, 0, keepdims=True)
                gates_ref[:, cols] = gates
                scales_ref[:, cols] = gates * kept_ref[:, cols]
            scale = scales_ref[pl.ds(row, 1), cols]
            keep = kept_ref[pl.ds(row, 1), cols]
            sigmoid = jax.nn.sigmoid(gate)
            silu = gate * sigmoid
            hidden = silu * up
            dscale_ref[0, 0:1, cols] = keep * jnp.sum(hidden * grad, 0, keepdims=True)
            act_ref[:, cols] = (hidden * scale).astype(BF16)
            grad = grad * scale
            dup_ref[:, cols] = (grad * silu).astype(BF16)
            dgate_ref[:, cols] = (grad * up * (sigmoid + silu * (1.0 - sigmoid))).astype(BF16)

        dscale_ref[...] = jnp.zeros_like(dscale_ref)
        for b in range(blocks):
            finish(b, *products(b))
        write_grads(
            rows_ref,
            cots_ref,
            act_ref[...],
            dgate_ref[...],
            dup_ref[...],
            e_ref,
            outs[4:],
            *scratch[4:],
            self.share,
        )

    def act(self, places, first, n, kept, scales, in_t, down, make_gates=False):
        units, width, tokens = self.units, self.width, self.tokens
        lanes = kept.shape[0]
        in_rows = 2 * units + (lanes if make_gates else 0)
        table = pl.BlockSpec((lanes, tokens), lambda i, e: (0, 0))
        one = pl.BlockSpec((units, tokens), lambda i, e: (i, 0))
        outs, specs = [], []
        if make_gates:
            outs += [jax.ShapeDtypeStruct((lanes, tokens), F32)] * 2
            specs += [table] * 2
        outs += [jax.ShapeDtypeStruct((n * units, tokens), BF16)] * 3
        specs += [one] * 3
        outs.append(jax.ShapeDtypeStruct((n, 8, tokens), F32))
        specs.append(pl.BlockSpec((1, 8, tokens), lambda i, e: (i, 0, 0)))
        structs, grad_specs = self.grads_structs(n)
        extra = [pltpu.VMEM((units, width), BF16), pltpu.VMEM((width, units), BF16)]
        return pl.pallas_call(
            functools.partial(self.act_kernel, first, n, make_gates),
            out_shape=tuple(outs + structs),
            grid_spec=pltpu.PrefetchScalarGridSpec(
                num_scalar_prefetch=1,
                grid=(n,),
                in_specs=[
                    table,
                    table,
                    pl.BlockSpec((in_rows, width), lambda i, e: (first + i, 0)),
                    pl.BlockSpec((units, width), lambda i, e: (first + i, 0)),
                ]
                + [pl.BlockSpec(memory_space=pl.ANY)] * self.n_arrays(),
                out_specs=tuple(specs + grad_specs),
                scratch_shapes=self.scratch() + extra,
            ),
            compiler_params=pltpu.CompilerParams(vmem_limit_bytes=60 << 20),
            cost_estimate=cost(
                flops=12 * width * units * tokens * n,
                transcendentals=units * tokens * n,
                bytes_accessed=4 * width * tokens + 6 * n * units * (width + tokens),
            ),
            name="experts_act",
        )(places, kept, scales, in_t, down, *self.arrays[0], *self.arrays[1])

    def out_kernel(self, parts, e_ref, weight_ref, *refs):
        act_refs, dscale_refs = refs[:parts], refs[parts : 2 * parts]
        message_ref, act_s, dscale_s = refs[2 * parts :]
        at = row = 0
        dscale_s[...] = jnp.zeros_like(dscale_s)
        for act_ref, dscale_ref in zip(act_refs, dscale_refs):
            act_s[at : at + act_ref.shape[0], :] = act_ref[...]
            at += act_ref.shape[0]
            for i in range(dscale_ref.shape[0]):
                dscale_s[pl.ds(e_ref[0] + row, 1), :] = dscale_ref[i, 0:1, :]
                row += 1
        width, lanes = self.width, dscale_s.shape[0]
        message_ref[0, :width, :] = jnp.dot(
            weight_ref[...], act_s[...], preferred_element_type=F32
        ).astype(BF16)
        grads = dscale_s[...]
        high = grads.astype(BF16)
        message_ref[0, width : width + lanes, :] = high
        message_ref[0, width + lanes :, :] = (grads - high.astype(F32)).astype(BF16)

    def out(self, places, lanes, weight, acts, dscales, first_block, n_blocks):
        rows = weight.shape[1]
        parts = len(acts)
        width, count = self.width, self.count

        def column(shape):
            return pl.BlockSpec(
                shape, lambda b, e: (0,) * (len(shape) - 1) + (first_block + b,)
            )

        return pl.pallas_call(
            functools.partial(self.out_kernel, parts),
            out_shape=jax.ShapeDtypeStruct((n_blocks, width + 2 * lanes, count), BF16),
            grid_spec=pltpu.PrefetchScalarGridSpec(
                num_scalar_prefetch=1,
                grid=(n_blocks,),
                in_specs=[
                    pl.BlockSpec(
                        (width, rows),
                        lambda b, e: (0, 0),
                        pipeline_mode=pl.Buffered(buffer_count=1),
                    )
                ]
                + [column((a.shape[0], count)) for a in acts]
                + [column((a.shape[0], 8, count)) for a in dscales],
                out_specs=pl.BlockSpec((1, width + 2 * lanes, count), lambda b, e: (b, 0, 0)),
                scratch_shapes=[pltpu.VMEM((rows, count), BF16), pltpu.VMEM((lanes, count), F32)],
            ),
            compiler_params=pltpu.CompilerParams(vmem_limit_bytes=60 << 20),
            cost_estimate=cost(
                flops=2 * width * rows * count * n_blocks,
                transcendentals=0,
                bytes_accessed=2 * width * rows + 4 * width * count * n_blocks,
            ),
            name="experts_out",
        )(places, weight, *acts, *dscales)

    def back_kernel(self, parts, gate_w_ref, up_w_ref, *refs):
        dgate_refs, dup_refs = refs[:parts], refs[parts : 2 * parts]
        back_ref, dgate_s, dup_s = refs[2 * parts :]
        for target, pieces in ((dgate_s, dgate_refs), (dup_s, dup_refs)):
            at = 0
            for piece in pieces:
                target[at : at + piece.shape[0], :] = piece[...]
                at += piece.shape[0]
        back = jnp.dot(gate_w_ref[...], dgate_s[...], preferred_element_type=F32)
        back = back + jnp.dot(up_w_ref[...], dup_s[...], preferred_element_type=F32)
        back_ref[0] = back.astype(BF16)

    def back(self, gate_w, up_w, dgates, dups, first_block, n_blocks):
        width, count = self.width, self.count
        rows = gate_w.shape[1]
        parts = len(dgates)
        whole = pl.BlockSpec(
            (width, rows), lambda b: (0, 0), pipeline_mode=pl.Buffered(buffer_count=1)
        )
        column = [pl.BlockSpec((a.shape[0], count), lambda b: (0, first_block + b)) for a in dgates]
        return pl.pallas_call(
            functools.partial(self.back_kernel, parts),
            out_shape=jax.ShapeDtypeStruct((n_blocks, width, count), BF16),
            grid=(n_blocks,),
            in_specs=[whole, whole] + column * 2,
            out_specs=pl.BlockSpec((1, width, count), lambda b: (b, 0, 0)),
            scratch_shapes=[pltpu.VMEM((rows, count), BF16)] * 2,
            compiler_params=pltpu.CompilerParams(vmem_limit_bytes=60 << 20),
            cost_estimate=cost(
                flops=4 * width * rows * count * n_blocks,
                transcendentals=0,
                bytes_accessed=4 * width * rows + 4 * width * count * n_blocks,
            ),
            name="experts_back",
        )(gate_w, up_w, *dgates, *dups)


def body(
    tokens,
    routes,
    cotangent,
    norm_attn,
    w_query,
    w_key,
    w_value,
    w_out,
    norm_ffn,
    w_router,
    w_gate,
    w_up,
    w_down,
):
    comm = Comm()
    hold = lax.optimization_barrier
    count, width = tokens.shape[1], tokens.shape[2]
    top_k = routes.shape[2]
    n_experts, _, hidden_units = w_gate.shape
    all_experts = n_experts * comm.n_expert
    capacity = (9 * count * top_k + 8 * all_experts - 1) // (8 * all_experts)
    n_context, n_dp, share = comm.n_context, comm.n_dp, comm.share
    expert_index = lax.axis_index("expert")
    context_index = lax.axis_index("context")
    dp_index = lax.axis_index("dp")
    parity = context_index % share
    chunks = n_context // share
    units = hidden_units // share
    lanes = -(-all_experts // 32) * 32
    places = jnp.stack([expert_index * n_experts, dp_index, context_index // share])

    cot_t = cotangent[0].T
    routed = (
        routes[0].T[:, None, :] == jnp.arange(lanes, dtype=jnp.int32)[None, :, None]
    ).astype(F32)
    cot_message = jnp.concatenate([cot_t, routed.sum(0).astype(BF16)])
    tokens, cot_message = hold((tokens, cot_message))
    across = [comm.pair(cot_message)] if share == 2 else []
    cots = [cot_message] + [comm.pull(cot_message, k, 0) for k in range(1, comm.columns)]

    hidden = tokens[0].T.astype(F32)
    gain_attn = norm_attn.astype(F32)[:, None]
    gain_ffn = norm_ffn.astype(F32)[:, None]
    scale_attn = rms_scale(hidden)
    normed_attn = (hidden * scale_attn * gain_attn).astype(BF16)
    positions = context_index * count + jnp.arange(count, dtype=jnp.int32)
    cosine, sine = rope_tables(positions)
    key_t = rotate_t(mm(w_key, normed_attn, 0, 0), cosine, sine).astype(BF16)
    value_t = mm(w_value, normed_attn, 0, 0).astype(BF16)
    kv_width = key_t.shape[0]
    kv_own = jnp.concatenate([key_t, value_t], 0)
    kv_blocks = [kv_own]
    for s in range(1, n_context):
        pairs = [(i, i + s) for i in range(n_context - s)]
        kv_blocks.append(lax.ppermute(kv_own, "context", pairs))
    query_t = rotate_t(mm(w_query, normed_attn, 0, 0), cosine, sine)
    query_t = (query_t * HEAD_DIM**-0.5).astype(BF16)

    weights = prepare_weights(parity, w_gate, w_up, w_down, hidden_units // n_context, share)
    router_t = jnp.zeros((lanes, width), BF16).at[:all_experts].set(w_router.T)
    in_t, gate_w, up_w, down, down_t = weights
    in_t = in_t.reshape(n_experts * 2 * units, width)
    in_first = jnp.concatenate([in_t[: 2 * units], router_t])
    if across:
        across, in_t, in_first = hold((across, in_t, in_first))
        across = across + [comm.pull(across[0], k, 0) for k in range(1, comm.columns)]
        cots, across[0], in_t = hold((cots, across[0], in_t))
    cots, across = [[[(0, x, 0)] for x in part] for part in (cots, across)]
    others = comm.from_core(cots) if comm.cores == 2 else []
    kv_blocks, in_t, in_first, gate_w, up_w, down, down_t = hold(
        (kv_blocks, in_t, in_first, gate_w, up_w, down, down_t)
    )
    out_t, out_low, lse = attention_forward(context_index, query_t, kv_blocks)
    middle = hidden + mm(w_out, out_low, 0, 0)
    scale_ffn = rms_scale(middle)
    normed_ffn = (middle * scale_ffn * gain_ffn).astype(BF16)
    across = [block[0][1] for block in across]
    across, normed_ffn = hold((across, normed_ffn))
    rows, across = comm.gather_group(normed_ffn, across)
    across = [[(0, x, 0)] for x in across]
    if comm.cores == 2 and across:
        others = others + comm.from_core(across)
    cots = cots + across + others

    routed_all = jnp.concatenate(
        [block[0][1][block[0][2] + width : block[0][2] + width + lanes] for block in cots]
    )
    n_blocks = len(cots)
    before = jnp.triu(jnp.ones((count, count), BF16), 1)
    ranking = mm(routed_all, before, 1, 0)
    chosen = routed_all.astype(F32)
    kept = jnp.where(ranking < capacity, chosen, 0.0)

    def side_by_side(array):
        array = array.reshape(n_blocks, lanes, count)
        return jnp.concatenate([array[b] for b in range(n_blocks)], 1)

    chosen, kept = side_by_side(chosen), side_by_side(kept)

    row_count = width // comm.n_expert

    def for_experts(*arrays):
        out = []
        for j in range(comm.cores):
            for k in range(comm.columns):
                column, core = expert_index // comm.cores, expert_index % comm.cores
                column = (column - k) % comm.columns
                target = column * comm.cores + (core + j) % comm.cores
                pieces = [
                    lax.dynamic_slice_in_dim(array, target * row_count, row_count, 0)
                    for array in arrays
                ]
                out.append(jnp.concatenate(pieces))
        return out

    def to_experts(pieces):
        peers = [(j, k) for j in range(comm.cores) for k in range(comm.columns)]
        return pieces[:1] + [comm.pull(x, k, j) for x, (j, k) in zip(pieces[1:], peers[1:])]

    columns_sent = for_experts(normed_attn, out_low)
    chosen, columns_sent = hold((chosen, columns_sent))

    own = Experts(rows, cots, width, units, share, chunks, n_dp)
    groups, at = [], 0
    for n in (1, (n_experts - 1) // 2, n_experts - 1 - (n_experts - 1) // 2):
        if n:
            groups.append((at, n))
            at += n
    acts, dgates, dups, dscales, kept_parts, arrived, crossing = ([] for _ in range(7))
    scales = None

    def pass_on(g, values):
        if g >= len(groups):
            return values
        terms, values = hold((arrived[g], values))
        terms = [kept_parts[g]] + terms

        def part(k):
            return sum(term[k].astype(F32) for term in terms)

        sent = comm.send_context([part(k).astype(BF16) for k in range(1, chunks)], share)
        crossing.append([part(0).astype(BF16)] + sent)
        return values

    for g, (first, n) in enumerate(groups):
        if g == 0:
            gates_all, scales, *done = own.act(
                places, first, n, kept, chosen, in_first, down, make_gates=True
            )
        else:
            done = own.act(places, first, n, kept, scales, in_t, down)
        for target, value in zip((acts, dgates, dups, dscales, kept_parts), done):
            target.append(value)
        arrived.append(comm.send_dp(done[5:]))
        if g == 0:
            scales, columns_sent = hold((scales, columns_sent))
            columns_got = to_experts(columns_sent)
        if g == 1:
            scales = pass_on(0, scales)

    columns_got, acts = hold((columns_got, acts))
    h1_rows = [x[:row_count] for x in columns_got]
    ob_rows = [x[row_count:] for x in columns_got]
    near_count = n_blocks // comm.cores

    def both_cores(call):
        other = None
        if comm.cores == 2:
            other = comm.push(call(near_count, near_count), 0, 1)
        return call(0, near_count), other

    message = both_cores(
        lambda first, n: own.out(places, lanes, down_t, acts, dscales, first, n)
    )
    back_other = None
    if comm.cores == 2:
        back_other = own.back(gate_w, up_w, dgates, dups, near_count, near_count)
        back_other = comm.push(back_other, 0, 1)
    message, dgates = hold((message, dgates))
    dgates, crossing[0] = pass_on(1, (dgates, crossing[0]))
    back_near = own.back(gate_w, up_w, dgates, dups, 0, near_count)
    message = comm.return_hops(*message)
    message, back_near = hold((message, back_near))
    back = comm.return_hops(back_near, back_other)
    returned = comm.return_last(message)
    back = pass_on(2, back)
    grad_normed_ffn = comm.return_last(back)
    result = (middle + returned[:width]).astype(BF16)
    grad_gates = returned[width : width + lanes] + returned[width + lanes :]
    gates_own = gates_all[:, :count]

    upstream = cot_t.astype(F32)
    mean_grad = jnp.sum(gates_own * grad_gates, 0, keepdims=True)
    grad_logits = (gates_own * (grad_gates - mean_grad)).astype(BF16)
    grad_normed_ffn = grad_normed_ffn + mm(router_t, grad_logits, 0, 0)
    grad_gain_ffn = jnp.sum(grad_normed_ffn * middle * scale_ffn, 1)
    grad_middle = upstream + norm_back(grad_normed_ffn, middle, scale_ffn, gain_ffn)
    grad_branch = grad_middle.astype(BF16)

    gain_grid = grad_gain_ffn.reshape(-1, count)
    gain_lines = gain_grid.shape[0]
    gain_high = lax.reduce_precision(gain_grid, 8, 7)
    gain_rows = jnp.concatenate([gain_high, gain_grid - gain_high]).astype(BF16)
    gain_rows = jnp.pad(gain_rows, ((0, -2 * gain_lines % 16), (0, 0)))
    branch_all = comm.gather_columns(jnp.concatenate([grad_branch, grad_logits, gain_rows]))
    grad_attn_t = mm(w_out, grad_branch, 1, 0).astype(BF16)

    def attention_half(first, heads):
        return attention_backward(
            context_index, query_t, grad_attn_t, out_t, lse, kv_blocks, first, heads
        )

    def to_keys(grad_kv):
        return lax.all_to_all(grad_kv, "context", 0, 0, tiled=True)

    size_down = units // chunks // n_dp
    tiles = width // units

    def total_of(terms):
        total = jnp.concatenate([sum(x.astype(F32) for x in group) for group in terms])
        n = total.shape[0]
        part = total[:, : tiles * size_down].reshape(n, tiles, size_down, units)
        down = jnp.swapaxes(part, 1, 2).reshape(n, size_down, width)
        part = total[:, tiles * size_down :]
        return down, part.reshape(n, 2, share, part.shape[1] // 2 // share, units)

    def send_pair(part):
        if share == 1:
            return part[:, :, 0], None
        keep = lax.dynamic_index_in_dim(part, parity, 2, False)
        send = lax.dynamic_index_in_dim(part, 1 - parity, 2, False)
        return keep, comm.pair(send.astype(BF16))

    def both_columns(keep, other):
        if other is None:
            return keep
        other = other.astype(F32)
        first = jnp.where(parity == 0, keep, other)
        second = jnp.where(parity == 0, other, keep)
        chunk = hidden_units // n_context
        pieces = []
        for q in range(chunks):
            pieces += [x[..., q * chunk : (q + 1) * chunk] for x in (first, second)]
        return jnp.concatenate(pieces, -1)

    early = crossing[:-1]
    early, grad_attn_t = hold((early, grad_attn_t))
    totals = [total_of(early)] if early else []
    pairs = [send_pair(part) for _, part in totals]
    half = KV_HEADS // 2
    grad_query_a, grad_kv_a = attention_half(0, half)
    kv_a = to_keys(grad_kv_a)
    branch_all, grad_attn_t = hold((branch_all, grad_attn_t))
    branch_all = comm.gather_cores(branch_all)
    grad_query_b, grad_kv_b = attention_half(half, half)
    kv_a, grad_kv_b, branch_all, crossing[-1] = hold((kv_a, grad_kv_b, branch_all, crossing[-1]))
    kv_b = to_keys(grad_kv_b)

    out_terms = comm.scatter_rows(ob_rows, branch_all, width)
    h2_rows = [
        lax.dynamic_slice_in_dim(array, at + expert_index * row_count, row_count, 0)
        for j in range(comm.cores)
        for ((_, array, at),) in rows[j * near_count : j * near_count + comm.columns]
    ]
    router_rows = sum(mm(a, b[width : width + lanes], 1, 1) for a, b in zip(h2_rows, branch_all))
    gain_total = sum(x[width + lanes :].astype(F32) for x in branch_all)
    gain_total = gain_total[:gain_lines] + gain_total[gain_lines : 2 * gain_lines]
    gain_part = lax.dynamic_slice_in_dim(
        gain_total.reshape(width), expert_index * row_count, row_count, 0
    )
    rest = jnp.zeros((row_count, LANES - lanes - 1), F32)
    extra = jnp.concatenate([router_rows, gain_part[:, None], rest], 1).astype(BF16)
    extra = extra.reshape(n_context * n_dp, -1, LANES)

    grad_query_raw = jnp.concatenate(
        [rotate_t(x, cosine, -sine).astype(BF16) for x in (grad_query_a, grad_query_b)]
    )
    query_terms = comm.scatter_rows(h1_rows, comm.gather_expert(grad_query_raw), width)
    late = crossing[-1]
    pairs, kv_b = hold((pairs, kv_b))
    totals.append(total_of([late]))
    pairs.append(send_pair(totals[-1][1]))
    kv_sums = [jnp.sum(x.astype(F32), 0) for x in (kv_a, kv_b)]
    grad_key_raw = [rotate_t(kv_sum[0], cosine, -sine).astype(BF16) for kv_sum in kv_sums]
    grad_kv_raw = jnp.concatenate(grad_key_raw + [kv_sum[1].astype(BF16) for kv_sum in kv_sums])
    near_kv = comm.gather_columns(grad_kv_raw)
    near_kv, out_terms, query_terms = hold((near_kv, out_terms, query_terms))
    out_sum, query_sum = comm.scatter_rest(out_terms), comm.scatter_rest(query_terms)
    kv_terms = comm.scatter_rows(h1_rows, comm.gather_cores(near_kv), 2 * kv_width)
    extra, kv_terms[0] = hold((extra, kv_terms[0]))
    extra = lax.all_to_all(extra, ("context", "dp"), 0, 0, tiled=True)
    extra = jnp.sum(extra.astype(F32), 0)
    kv_rows = comm.scatter_rest(kv_terms)
    key_sum, value_sum = kv_rows[:, :kv_width], kv_rows[:, kv_width:]

    down_sum = jnp.concatenate([down for down, _ in totals])
    parts = [both_columns(*pair) for pair in pairs]
    gate_sum = jnp.concatenate([part[:, 0] for part in parts])
    up_sum = jnp.concatenate([part[:, 1] for part in parts])

    shard = (expert_index * n_context + context_index) * n_dp + dp_index
    shard_rows = query_sum.shape[0]

    def shard_of(array):
        return lax.dynamic_slice_in_dim(array, shard * shard_rows, shard_rows, 0).astype(F32)

    gain_sum = (
        jnp.sum(shard_of(w_query) * query_sum, 1)
        + jnp.sum(shard_of(w_key) * key_sum, 1)
        + jnp.sum(shard_of(w_value) * value_sum, 1)
    ) / shard_of(norm_attn)

    grad_normed_attn = mm(w_query, grad_query_raw, 1, 0)
    grad_normed_attn = grad_normed_attn + mm(w_key, grad_kv_raw[:kv_width], 1, 0)
    grad_normed_attn = grad_normed_attn + mm(w_value, grad_kv_raw[kv_width:], 1, 0)
    grad_hidden = grad_middle + norm_back(grad_normed_attn, hidden, scale_attn, gain_attn)
    return (
        result.T[None],
        grad_hidden.astype(BF16).T[None],
        gain_sum,
        query_sum,
        key_sum,
        value_sum,
        out_sum,
        extra[:, lanes],
        extra[:, :all_experts],
        gate_sum,
        up_sum,
        down_sum,
    )


def solution(mesh):
    rows = P(("expert", "dp"), "context", None)
    dense = P(("expert", "context", "dp"), None)
    vector = P(("expert", "context", "dp"))
    experts = P("expert", None, None)
    expert_grads = P("expert", ("context", "dp"), None)
    return jax.shard_map(
        body,
        mesh=mesh,
        in_specs=(rows, rows, rows) + (P(),) * 7 + (experts,) * 3,
        out_specs=(rows, rows, vector, dense, dense, dense, dense, vector, dense)
        + (expert_grads,) * 3,
        check_vma=False,
    )
```

```python
import functools

import jax
import jax.numpy as jnp
from jax import lax
from jax.experimental import pallas as pl
from jax.experimental.pallas import tpu as pltpu
from jax.sharding import PartitionSpec as P

HEADS = 24
KV_HEADS = 8
HEAD_DIM = 64
GROUP = HEADS // KV_HEADS


EPS = 1e-05
ROPE_BASE = 10000.0
NEG_LARGE = -1e30
F32 = jnp.float32
BF16 = jnp.bfloat16
LANES = 128


def cost(flops, bytes_accessed, transcendentals=0):
    scale = 64
    return pl.CostEstimate(
        flops=flops // scale,
        bytes_accessed=bytes_accessed // scale,
        transcendentals=transcendentals // scale,
    )


def rms_scale(values):
    return lax.rsqrt(jnp.mean(values * values, 0, keepdims=True) + EPS)


def norm_back(grad_out, values, scale, gain):
    weighted = gain * grad_out
    return scale * weighted - values * scale**3 * jnp.mean(weighted * values, 0, keepdims=True)


def mm(a, b, da, db):
    return lax.dot_general(a, b, (((da,), (db,)), ((), ())), preferred_element_type=F32)


class Comm:
    def __init__(self):
        self.n_expert = lax.axis_size("expert")
        self.n_context = lax.axis_size("context")
        self.n_dp = lax.axis_size("dp")
        self.cores = 2 if self.n_expert % 2 == 0 else 1
        self.columns = self.n_expert // self.cores
        self.share = 2 if self.n_context % 2 == 0 else 1

    def peer(self, i, k, j):
        column, core = divmod(i, self.cores)
        return ((column + k) % self.columns) * self.cores + (core + j) % self.cores

    def pull(self, value, k, j):
        pairs = [(self.peer(i, k, j), i) for i in range(self.n_expert)]
        return lax.ppermute(value, "expert", pairs)

    def push(self, value, k, j):
        pairs = [(i, self.peer(i, k, j)) for i in range(self.n_expert)]
        return lax.ppermute(value, "expert", pairs)

    def pair(self, value):
        return lax.ppermute(value, "context", [(i, i ^ 1) for i in range(self.n_context)])

    def from_core(self, blocks):
        arrays = [array for block in blocks for _, array, _ in block]
        moved = self.pull(jnp.concatenate(arrays) if len(arrays) > 1 else arrays[0], 0, 1)
        out, at = [], 0
        for block in blocks:
            pieces = []
            for row, array, _ in block:
                pieces.append((row, moved, at))
                at += array.shape[0]
            out.append(pieces)
        return out

    def gather_columns(self, value):
        return [value] + [self.pull(value, k, 0) for k in range(1, self.columns)]

    def gather_cores(self, near):
        if self.cores == 2:
            near = near + [self.pull(block, 0, 1) for block in near]
        return near

    def gather_expert(self, value):
        return self.gather_cores(self.gather_columns(value))

    def gather_group(self, value, beside):
        columns = [self.pull(value, k, 0) for k in range(1, self.columns)]
        far = []
        if self.share == 2:
            half = value.shape[0] // 2
            across = self.pair(value)
            columns, across, beside = lax.optimization_barrier((columns, across, beside))
        first = [[(0, value, 0)]] + [[(0, block, 0)] for block in columns]
        if self.share == 2:
            first.append([(0, across, 0)])
            for k in range(1, self.columns):
                top = self.pull(across[:half], k, 0)
                bottom = self.pair(columns[k - 1][half:])
                far.append([(0, top, 0), (half, bottom, 0)])
        blocks = first + far
        if self.cores == 2:
            blocks = blocks + self.from_core(first)
            blocks = blocks + (self.from_core(far) if far else [])
        return blocks, beside

    def return_hops(self, near, other):
        columns = self.columns
        shape = (self.share, columns) + near.shape[1:]
        arrays = [x.reshape(shape) for x in (near, other) if x is not None]

        def part(*at):
            return sum(array[at].astype(F32) for array in arrays)

        if self.share == 1:
            sent = [self.push(part(0, k).astype(BF16), k, 0) for k in range(1, columns)]
            return [part(0, 0)] + sent
        half = near.shape[1] // 2
        low, high = slice(0, half), slice(half, 2 * half)
        every = slice(None)
        by_column = [
            self.push(part(every, k, low).astype(BF16), k, 0) for k in range(1, columns)
        ]
        by_pair = self.pair(part(1, every, high).astype(BF16))
        return [part(every, 0, low)] + by_column + [part(0, every, high), by_pair]

    def return_last(self, terms):
        columns = self.columns
        if self.share == 1:
            return sum(term.astype(F32) for term in terms)
        top = terms[:columns]
        bottom = terms[columns : columns + 2]

        def total(parts, at):
            return sum(part[at].astype(F32) for part in parts)

        top_other = self.pair(total(top, 1).astype(BF16))
        others = [
            self.push(total(bottom, k).astype(BF16), k, 0).astype(F32)
            for k in range(1, columns)
        ]
        return jnp.concatenate(
            [total(top, 0) + top_other.astype(F32), sum(others, total(bottom, 0))]
        )

    def send_dp(self, parts):
        n = self.n_dp
        return [
            lax.ppermute(parts[s - 1], "dp", [(i, (i + s) % n) for i in range(n)])
            for s in range(1, n)
        ]

    def send_context(self, parts, stride):
        n = self.n_context // stride
        out = []
        for s in range(1, n):
            pairs = []
            for i in range(self.n_context):
                k, r = divmod(i, stride)
                pairs.append((i, ((k + s) % n) * stride + r))
            out.append(lax.ppermute(parts[s - 1], "context", pairs))
        return out

    def scatter_rows(self, left, right, width):
        n, m = self.n_context, self.n_dp
        c, d = lax.axis_index("context"), lax.axis_index("dp")
        size = left[0].shape[0] // (n * m)
        if size % 16 == 0:
            mine, *parts = row_products(jnp.stack([c, d]), left, right, width, n, m)
        else:
            local = sum(mm(a, b[:width], 1, 1) for a, b in zip(left, right))
            local = local.reshape(n, m, size, width)
            local = jnp.stack(
                [lax.dynamic_index_in_dim(local, (c + k) % n, 0, False) for k in range(n)]
            )
            mine, *parts = [
                lax.dynamic_index_in_dim(local, (d + s) % m, 1, False) for s in range(m)
            ]
        return [mine] + self.send_dp([part.astype(BF16) for part in parts])

    def scatter_rest(self, terms):
        n = self.n_context

        def of_context(k):
            return sum(x[k].astype(F32) for x in terms)

        came_far = self.send_context([of_context(k).astype(BF16) for k in range(1, n)], 1)
        return of_context(0) + sum(x.astype(F32) for x in came_far)


def row_products_kernel(count, place_ref, *refs):
    left, right, outs, total_s = refs[:count], refs[count : 2 * count], refs[2 * count : -1], refs[-1]
    width = total_s.shape[1]
    total_s[...] = mm(
        jnp.concatenate([a[...] for a in left], 1),
        jnp.concatenate([b[:width, :] for b in right], 1),
        1,
        1,
    )
    n, size, _ = outs[0].shape
    m = len(outs)
    for k in range(n):
        for s in range(m):
            owner = lax.rem(place_ref[0] + k, n) * m + lax.rem(place_ref[1] + s, m)
            rows = pl.ds(pl.multiple_of(owner * size, size), size)
            outs[s][k] = total_s[rows, :].astype(outs[s].dtype)


def row_products(place, left, right, width, n, m):
    rows = left[0].shape[0]
    size = rows // (n * m)

    def whole(shape):
        return pl.BlockSpec(shape, lambda i, p: (0,) * len(shape))

    return pl.pallas_call(
        functools.partial(row_products_kernel, len(left)),
        out_shape=tuple(
            jax.ShapeDtypeStruct((n, size, width), BF16 if s else F32) for s in range(m)
        ),
        grid_spec=pltpu.PrefetchScalarGridSpec(
            num_scalar_prefetch=1,
            grid=(1,),
            in_specs=[whole(x.shape) for x in left + right],
            out_specs=tuple(whole((n, size, width)) for _ in range(m)),
            scratch_shapes=[pltpu.VMEM((rows, width), F32)],
        ),
        compiler_params=pltpu.CompilerParams(vmem_limit_bytes=32 << 20),
        cost_estimate=cost(
            flops=2 * rows * width * right[0].shape[1] * len(left),
            bytes_accessed=8 * width * right[0].shape[1] + 6 * rows * width,
        ),
        name="row_products",
    )(place, *left, *right)


def heads_side_by_side(ref):
    hd = HEAD_DIM
    return jnp.concatenate([ref[g * hd : (g + 1) * hd, :] for g in range(GROUP)], 1)


def causal(shape, n):
    key = lax.broadcasted_iota(jnp.int32, shape, 0)
    query = lax.rem(lax.broadcasted_iota(jnp.int32, shape, 1), n)
    return key <= query


def attn_fwd_kernel(blocks, c_ref, q_ref, *refs):
    k_refs, v_refs = refs[:blocks], refs[blocks : 2 * blocks]
    o_ref, ob_ref, lse_ref, scores_ref = refs[2 * blocks :]
    c = c_ref[0]
    n = q_ref.shape[1]
    hd = HEAD_DIM
    queries = heads_side_by_side(q_ref)
    for s in range(blocks):
        rows = slice(s * n, (s + 1) * n)

        def fill(s=s, rows=rows):
            scores = mm(k_refs[s][...], queries, 0, 0)
            if s == 0:
                scores = jnp.where(causal(scores.shape, n), scores, NEG_LARGE)
            scores_ref[rows, :] = scores

        def blank(rows=rows):
            scores_ref[rows, :] = jnp.full((n, GROUP * n), NEG_LARGE, F32)

        if s == 0:
            fill()
        else:
            pl.when(c >= s)(fill)
            pl.when(c < s)(blank)
    lse_ref[...] = jnp.zeros_like(lse_ref)
    for g in range(GROUP):
        cols = slice(g * n, (g + 1) * n)
        scores = scores_ref[:, cols]
        top = jnp.max(scores, 0, keepdims=True)
        weights = jnp.exp(scores - top)
        total = jnp.sum(weights, 0, keepdims=True)
        weights = weights.astype(BF16)
        out = jnp.zeros((hd, n), F32)
        for s in range(blocks):
            out = out + mm(v_refs[s][...], weights[s * n : (s + 1) * n], 1, 0)
        out = out / total
        o_ref[g * hd : (g + 1) * hd, :] = out
        ob_ref[g * hd : (g + 1) * hd, :] = out.astype(BF16)
        lse_ref[0, g : g + 1, :] = top + jnp.log(total)


def kv_specs(blocks, n, first=0):
    keys = [pl.BlockSpec((HEAD_DIM, n), lambda h, c: (first + h, 0))] * blocks
    values = [pl.BlockSpec((HEAD_DIM, n), lambda h, c: (first + h + KV_HEADS, 0))] * blocks
    return keys + values


def attention_forward(context_index, query_t, kv_blocks):
    blocks = len(kv_blocks)
    n = query_t.shape[1]
    wide = GROUP * HEAD_DIM
    heads = query_t.shape[0] // wide
    head = pl.BlockSpec((wide, n), lambda h, c: (h, 0))
    return pl.pallas_call(
        functools.partial(attn_fwd_kernel, blocks),
        out_shape=(
            jax.ShapeDtypeStruct(query_t.shape, F32),
            jax.ShapeDtypeStruct(query_t.shape, BF16),
            jax.ShapeDtypeStruct((heads, 8, n), F32),
        ),
        grid_spec=pltpu.PrefetchScalarGridSpec(
            num_scalar_prefetch=1,
            grid=(heads,),
            in_specs=[head] + kv_specs(blocks, n),
            out_specs=(head, head, pl.BlockSpec((1, 8, n), lambda h, c: (h, 0, 0))),
            scratch_shapes=[pltpu.VMEM((blocks * n, GROUP * n), F32)],
        ),
        compiler_params=pltpu.CompilerParams(vmem_limit_bytes=40 << 20),
        cost_estimate=cost(
            flops=heads * GROUP * blocks * n * n * 256 * 4,
            transcendentals=heads * GROUP * blocks * n * n,
            bytes_accessed=16 * query_t.size,
        ),
        name="attn_fwd",
    )(context_index.reshape(1), query_t, *kv_blocks, *kv_blocks)


def attn_bwd_kernel(blocks, c_ref, q_ref, do_ref, o_ref, lse_ref, *refs):
    k_refs, v_refs = refs[:blocks], refs[blocks : 2 * blocks]
    dq_ref, dkv_ref = refs[2 * blocks :]
    c = c_ref[0]
    n = q_ref.shape[1]
    hd = HEAD_DIM
    queries, grads = heads_side_by_side(q_ref), heads_side_by_side(do_ref)
    deltas, lses = [], []
    for g in range(GROUP):
        head = slice(g * hd, (g + 1) * hd)
        both = do_ref[head, :].astype(F32) * o_ref[head, :]
        deltas.append(jnp.sum(both, 0, keepdims=True))
        lses.append(lse_ref[0, g : g + 1, :])
    delta, lse = jnp.concatenate(deltas, 1), jnp.concatenate(lses, 1)
    for s in range(blocks):

        def work(s=s):
            key_t = k_refs[s][...]
            weights = jnp.exp(mm(key_t, queries, 0, 0) - lse)
            if s == 0:
                weights = jnp.where(causal(weights.shape, n), weights, 0.0)
            grad_weights = mm(v_refs[s][...], grads, 0, 0)
            grad_scores = (weights * (grad_weights - delta)).astype(BF16)
            owner = lax.rem(c - s + blocks, blocks)
            dkv_ref[owner, 0] = mm(queries, grad_scores, 1, 1).astype(BF16)
            dkv_ref[owner, 1] = mm(grads, weights.astype(BF16), 1, 1).astype(BF16)
            step = mm(key_t, grad_scores, 1, 0) * (HEAD_DIM**-0.5)
            for g in range(GROUP):
                head, cols = slice(g * hd, (g + 1) * hd), slice(g * n, (g + 1) * n)
                if s == 0:
                    dq_ref[head, :] = step[:, cols]
                else:
                    dq_ref[head, :] += step[:, cols]

        def skip(s=s):
            owner = lax.rem(c - s + blocks, blocks)
            dkv_ref[owner] = jnp.zeros(dkv_ref.shape[1:], BF16)

        if s == 0:
            work()
        else:
            pl.when(c >= s)(work)
            pl.when(c < s)(skip)


def attention_backward(context_index, query_t, grad_t, out_t, lse, kv_blocks, first, heads):
    blocks = len(kv_blocks)
    n = query_t.shape[1]
    wide = GROUP * HEAD_DIM
    head = pl.BlockSpec((wide, n), lambda h, c: (first + h, 0))
    out = pl.BlockSpec((wide, n), lambda h, c: (h, 0))
    return pl.pallas_call(
        functools.partial(attn_bwd_kernel, blocks),
        out_shape=(
            jax.ShapeDtypeStruct((heads * wide, n), F32),
            jax.ShapeDtypeStruct((blocks, 2, heads * HEAD_DIM, n), BF16),
        ),
        grid_spec=pltpu.PrefetchScalarGridSpec(
            num_scalar_prefetch=1,
            grid=(heads,),
            in_specs=[head, head, head, pl.BlockSpec((1, 8, n), lambda h, c: (first + h, 0, 0))]
            + kv_specs(blocks, n, first),
            out_specs=(
                out,
                pl.BlockSpec((blocks, 2, HEAD_DIM, n), lambda h, c: (0, 0, h, 0)),
            ),
        ),
        compiler_params=pltpu.CompilerParams(vmem_limit_bytes=40 << 20),
        cost_estimate=cost(
            flops=heads * GROUP * blocks * n * n * 256 * 10,
            transcendentals=heads * GROUP * blocks * n * n,
            bytes_accessed=20 * query_t.size,
        ),
        name="attn_bwd",
    )(context_index.reshape(1), query_t, grad_t, out_t, lse, *kv_blocks, *kv_blocks)


def rope_tables(positions):
    half_dim = HEAD_DIM // 2
    frequency = ROPE_BASE ** (-2.0 * jnp.arange(half_dim, dtype=F32) / HEAD_DIM)
    angles = frequency[:, None] * positions.astype(F32)[None, :]
    return jnp.cos(angles), jnp.sin(angles)


def rotate_t(values_t, cosine, sine):
    shaped = values_t.reshape(-1, 2, HEAD_DIM // 2, values_t.shape[1])
    low, high = shaped[:, 0], shaped[:, 1]
    turned = jnp.stack([low * cosine - high * sine, high * cosine + low * sine], 1)
    return turned.reshape(values_t.shape)


def prepare_kernel(p_ref, gate_ref, up_ref, down_ref, *outs):
    in_t_ref, gate_out, up_out, down_out, down_t_out = outs
    gate, up, down = gate_ref[0], up_ref[0], down_ref[0]
    in_t_ref[0, 0, 0] = gate.astype(F32).T.astype(BF16)
    in_t_ref[0, 1, 0] = up.astype(F32).T.astype(BF16)
    gate_out[...] = gate
    up_out[...] = up
    down_out[...] = down
    down_t_out[...] = down.astype(F32).T.astype(BF16)


def prepare_weights(parity, w_gate, w_up, w_down, chunk, share):
    experts, width, hidden = w_gate.shape
    chunks = hidden // chunk // share
    units = chunks * chunk

    def column(e, q, p):
        return (e, 0, q * share + p[0])

    def flat(e, q, p):
        return (0, e * chunks + q)

    return pl.pallas_call(
        prepare_kernel,
        out_shape=(
            jax.ShapeDtypeStruct((experts, 2, chunks, chunk, width), BF16),
            jax.ShapeDtypeStruct((width, experts * units), BF16),
            jax.ShapeDtypeStruct((width, experts * units), BF16),
            jax.ShapeDtypeStruct((experts * units, width), BF16),
            jax.ShapeDtypeStruct((width, experts * units), BF16),
        ),
        grid_spec=pltpu.PrefetchScalarGridSpec(
            num_scalar_prefetch=1,
            grid=(experts, chunks),
            in_specs=[
                pl.BlockSpec((1, width, chunk), column),
                pl.BlockSpec((1, width, chunk), column),
                pl.BlockSpec((1, chunk, width), lambda e, q, p: (e, q * share + p[0], 0)),
            ],
            out_specs=(
                pl.BlockSpec((1, 2, 1, chunk, width), lambda e, q, p: (e, 0, q, 0, 0)),
                pl.BlockSpec((width, chunk), flat),
                pl.BlockSpec((width, chunk), flat),
                pl.BlockSpec((chunk, width), lambda e, q, p: (e * chunks + q, 0)),
                pl.BlockSpec((width, chunk), flat),
            ),
        ),
        compiler_params=pltpu.CompilerParams(vmem_limit_bytes=60 << 20),
        cost_estimate=cost(
            flops=0, transcendentals=0, bytes_accessed=18 * experts * width * units
        ),
        name="prepare_weights",
    )(parity.reshape(1), w_gate, w_up, w_down)


def piece_copies(blocks, refs, target_ref, sems):
    out = []
    count = refs[0].shape[1]
    for b, pieces in enumerate(blocks):
        copies = []
        for i, (first, ref, row) in enumerate(pieces):
            last = pieces[i + 1][0] if i + 1 < len(pieces) else target_ref.shape[0]
            copies.append(
                pltpu.make_async_copy(
                    refs[ref].at[row : row + last - first],
                    target_ref.at[first:last, b * count : (b + 1) * count],
                    sems.at[b],
                )
            )
        out.append(copies)
    return out


def write_grads(rows_ref, cots_ref, act, dgate, dup, place_ref, outs, down_s, in_s, share):
    owners = len(outs)
    chunks, _, _, units = outs[0].shape
    width = rows_ref.shape[0]
    size = units // chunks // owners
    tiles = width // units

    def place(k, s):
        return lax.rem(place_ref[2] + k, chunks), lax.rem(place_ref[1] + s, owners)

    down_s[...] = mm(act, cots_ref[...], 1, 1).astype(BF16)
    for k in range(chunks):
        for s in range(owners):
            at_k, at_d = place(k, s)
            start = pl.multiple_of((at_k * owners + at_d) * size, size)
            for t in range(tiles):
                outs[s][k, 0, t * size : (t + 1) * size, :] = down_s[
                    pl.ds(start, size), t * units : (t + 1) * units
                ]
    base = tiles * size
    size = width // (chunks * share * owners)
    for grad_act in (dgate, dup):
        in_s[...] = mm(rows_ref[...], grad_act, 1, 1).astype(BF16)
        for k in range(chunks):
            for q in range(share):
                for s in range(owners):
                    at_k, at_d = place(k, s)
                    start = pl.multiple_of(((at_k * share + q) * owners + at_d) * size, size)
                    to = base + q * size
                    outs[s][k, 0, to : to + size, :] = in_s[pl.ds(start, size), :]
        base += share * size


class Experts:
    def __init__(self, rows, cots, width, units, share, chunks, owners):
        self.arrays, self.plans = [], []
        for blocks in (rows, cots):
            arrays, plan = [], []
            for block in blocks:
                pieces = []
                for first, array, row in block:
                    known = [i for i, x in enumerate(arrays) if x is array]
                    if not known:
                        arrays.append(array)
                    pieces.append((first, known[0] if known else len(arrays) - 1, row))
                plan.append(pieces)
            self.arrays.append(arrays)
            self.plans.append(plan)
        self.blocks = len(rows)
        self.width, self.count = width, rows[0][0][1].shape[1]
        self.tokens = self.blocks * self.count
        self.units, self.share, self.chunks, self.owners = units, share, chunks, owners
        self.height = self.width // chunks // owners * 3

    def n_arrays(self):
        return sum(map(len, self.arrays))

    def scratch(self):
        wide = pltpu.VMEM((self.width, self.tokens), BF16)
        sems = [pltpu.SemaphoreType.DMA((self.blocks,))] * 2
        return [wide, wide] + sems

    def copies(self, refs, rows_ref, cots_ref, row_sems, cot_sems):
        n = len(self.arrays[0])
        row_copies = piece_copies(self.plans[0], refs[:n], rows_ref, row_sems)
        cot_copies = piece_copies(self.plans[1], refs[n:], cots_ref, cot_sems)
        return [a + b for a, b in zip(row_copies, cot_copies)]

    def grads_structs(self, n):
        shape = (self.chunks, n, self.height, self.units)
        spec = pl.BlockSpec(
            (self.chunks, 1, self.height, self.units), lambda i, *_: (0, i, 0, 0)
        )
        return [jax.ShapeDtypeStruct(shape, BF16)] * self.owners, [spec] * self.owners

    def act_kernel(self, first, n, make_gates, e_ref, *refs):
        n_arrays = self.n_arrays()
        kept_ref, scales_ref, in_t_ref, down_ref = refs[:4]
        piece_refs, outs, scratch = refs[4 : 4 + n_arrays], refs[4 + n_arrays : -6], refs[-6:]
        if make_gates:
            chosen_ref = scales_ref
            gates_ref, scales_ref = outs[:2]
            outs = outs[2:]
        act_ref, dgate_ref, dup_ref, dscale_ref = outs[:4]
        rows_ref, cots_ref = scratch[:2]
        units, count, blocks = self.units, self.count, self.blocks
        copies = self.copies(piece_refs, *scratch[:4])
        step = pl.program_id(0)
        row = e_ref[0] + first + step

        def start():
            for block in copies:
                for copy in block:
                    copy.start()

        pl.when(step == 0)(start)

        def columns(b):
            return pl.ds(pl.multiple_of(b * count, count), count)

        def arrive(b):
            whole = piece_refs[0].at[0 : self.width]
            for target, sems in zip(scratch[:2], scratch[2:4]):
                pltpu.make_async_copy(whole, target.at[:, columns(b)], sems.at[b]).wait()

        def products(b):
            pl.when(step == 0)(lambda: arrive(b))
            cols = columns(b)
            acts = jnp.dot(in_t_ref[...], rows_ref[:, cols], preferred_element_type=F32)
            grad = jnp.dot(down_ref[...], cots_ref[:, cols], preferred_element_type=F32)
            return acts, grad

        def finish(b, acts, grad):
            cols = columns(b)
            gate, up = acts[:units], acts[units : 2 * units]
            if make_gates:
                chosen = chosen_ref[:, cols] > 0
                logits = jnp.where(chosen, acts[2 * units :], NEG_LARGE)
                gates = jnp.exp(logits - jnp.max(logits, 0, keepdims=True))
                gates = jnp.where(chosen, gates, 0.0)
                gates = gates / jnp.sum(gates, 0, keepdims=True)
                gates_ref[:, cols] = gates
                scales_ref[:, cols] = gates * kept_ref[:, cols]
            scale = scales_ref[pl.ds(row, 1), cols]
            keep = kept_ref[pl.ds(row, 1), cols]
            sigmoid = jax.nn.sigmoid(gate)
            silu = gate * sigmoid
            hidden = silu * up
            dscale_ref[0, 0:1, cols] = keep * jnp.sum(hidden * grad, 0, keepdims=True)
            act_ref[:, cols] = (hidden * scale).astype(BF16)
            grad = grad * scale
            dup_ref[:, cols] = (grad * silu).astype(BF16)
            dgate_ref[:, cols] = (grad * up * (sigmoid + silu * (1.0 - sigmoid))).astype(BF16)

        dscale_ref[...] = jnp.zeros_like(dscale_ref)

        unroll = 4 if blocks % 4 == 0 else 1

        def some(i, carry):
            for u in range(unroll):
                finish(i * unroll + u, *products(i * unroll + u))
            return carry

        lax.fori_loop(0, blocks // unroll, some, 0)
        write_grads(
            rows_ref,
            cots_ref,
            act_ref[...],
            dgate_ref[...],
            dup_ref[...],
            e_ref,
            outs[4:],
            *scratch[4:],
            self.share,
        )

    def act(self, places, first, n, kept, scales, in_t, down, make_gates=False):
        units, width, tokens = self.units, self.width, self.tokens
        lanes = kept.shape[0]
        in_rows = 2 * units + (lanes if make_gates else 0)
        table = pl.BlockSpec((lanes, tokens), lambda i, e: (0, 0))
        one = pl.BlockSpec((units, tokens), lambda i, e: (i, 0))
        outs, specs = [], []
        if make_gates:
            outs += [jax.ShapeDtypeStruct((lanes, tokens), F32)] * 2
            specs += [table] * 2
        outs += [jax.ShapeDtypeStruct((n * units, tokens), BF16)] * 3
        specs += [one] * 3
        outs.append(jax.ShapeDtypeStruct((n, 8, tokens), F32))
        specs.append(pl.BlockSpec((1, 8, tokens), lambda i, e: (i, 0, 0)))
        structs, grad_specs = self.grads_structs(n)
        extra = [pltpu.VMEM((units, width), BF16), pltpu.VMEM((width, units), BF16)]
        return pl.pallas_call(
            functools.partial(self.act_kernel, first, n, make_gates),
            out_shape=tuple(outs + structs),
            grid_spec=pltpu.PrefetchScalarGridSpec(
                num_scalar_prefetch=1,
                grid=(n,),
                in_specs=[
                    table,
                    table,
                    pl.BlockSpec((in_rows, width), lambda i, e: (first + i, 0)),
                    pl.BlockSpec((units, width), lambda i, e: (first + i, 0)),
                ]
                + [pl.BlockSpec(memory_space=pl.ANY)] * self.n_arrays(),
                out_specs=tuple(specs + grad_specs),
                scratch_shapes=self.scratch() + extra,
            ),
            compiler_params=pltpu.CompilerParams(vmem_limit_bytes=60 << 20),
            cost_estimate=cost(
                flops=12 * width * units * tokens * n,
                transcendentals=units * tokens * n,
                bytes_accessed=4 * width * tokens + 6 * n * units * (width + tokens),
            ),
            name="experts_act",
        )(places, kept, scales, in_t, down, *self.arrays[0], *self.arrays[1])

    def out_kernel(self, parts, e_ref, weight_ref, *refs):
        act_refs, dscale_refs = refs[:parts], refs[parts : 2 * parts]
        message_ref, act_s, dscale_s = refs[2 * parts :]
        at = row = 0
        dscale_s[...] = jnp.zeros_like(dscale_s)
        for act_ref, dscale_ref in zip(act_refs, dscale_refs):
            act_s[at : at + act_ref.shape[0], :] = act_ref[...]
            at += act_ref.shape[0]
            for i in range(dscale_ref.shape[0]):
                dscale_s[pl.ds(e_ref[0] + row, 1), :] = dscale_ref[i, 0:1, :]
                row += 1
        width, lanes = self.width, dscale_s.shape[0]
        message_ref[0, :width, :] = jnp.dot(
            weight_ref[...], act_s[...], preferred_element_type=F32
        ).astype(BF16)
        grads = dscale_s[...]
        high = grads.astype(BF16)
        message_ref[0, width : width + lanes, :] = high
        message_ref[0, width + lanes :, :] = (grads - high.astype(F32)).astype(BF16)

    def out(self, places, lanes, weight, acts, dscales, first_block, n_blocks):
        rows = weight.shape[1]
        parts = len(acts)
        width, count = self.width, self.count

        def column(shape):
            return pl.BlockSpec(
                shape, lambda b, e: (0,) * (len(shape) - 1) + (first_block + b,)
            )

        return pl.pallas_call(
            functools.partial(self.out_kernel, parts),
            out_shape=jax.ShapeDtypeStruct((n_blocks, width + 2 * lanes, count), BF16),
            grid_spec=pltpu.PrefetchScalarGridSpec(
                num_scalar_prefetch=1,
                grid=(n_blocks,),
                in_specs=[
                    pl.BlockSpec(
                        (width, rows),
                        lambda b, e: (0, 0),
                        pipeline_mode=pl.Buffered(buffer_count=1),
                    )
                ]
                + [column((a.shape[0], count)) for a in acts]
                + [column((a.shape[0], 8, count)) for a in dscales],
                out_specs=pl.BlockSpec((1, width + 2 * lanes, count), lambda b, e: (b, 0, 0)),
                scratch_shapes=[pltpu.VMEM((rows, count), BF16), pltpu.VMEM((lanes, count), F32)],
            ),
            compiler_params=pltpu.CompilerParams(vmem_limit_bytes=60 << 20),
            cost_estimate=cost(
                flops=2 * width * rows * count * n_blocks,
                transcendentals=0,
                bytes_accessed=2 * width * rows + 4 * width * count * n_blocks,
            ),
            name="experts_out",
        )(places, weight, *acts, *dscales)

    def back_kernel(self, parts, gate_w_ref, up_w_ref, *refs):
        dgate_refs, dup_refs = refs[:parts], refs[parts : 2 * parts]
        back_ref, dgate_s, dup_s = refs[2 * parts :]
        for target, pieces in ((dgate_s, dgate_refs), (dup_s, dup_refs)):
            at = 0
            for piece in pieces:
                target[at : at + piece.shape[0], :] = piece[...]
                at += piece.shape[0]
        back = jnp.dot(gate_w_ref[...], dgate_s[...], preferred_element_type=F32)
        back = back + jnp.dot(up_w_ref[...], dup_s[...], preferred_element_type=F32)
        back_ref[0] = back.astype(BF16)

    def back(self, gate_w, up_w, dgates, dups, first_block, n_blocks):
        width, count = self.width, self.count
        rows = gate_w.shape[1]
        parts = len(dgates)
        whole = pl.BlockSpec(
            (width, rows), lambda b: (0, 0), pipeline_mode=pl.Buffered(buffer_count=1)
        )
        column = [pl.BlockSpec((a.shape[0], count), lambda b: (0, first_block + b)) for a in dgates]
        return pl.pallas_call(
            functools.partial(self.back_kernel, parts),
            out_shape=jax.ShapeDtypeStruct((n_blocks, width, count), BF16),
            grid=(n_blocks,),
            in_specs=[whole, whole] + column * 2,
            out_specs=pl.BlockSpec((1, width, count), lambda b: (b, 0, 0)),
            scratch_shapes=[pltpu.VMEM((rows, count), BF16)] * 2,
            compiler_params=pltpu.CompilerParams(vmem_limit_bytes=60 << 20),
            cost_estimate=cost(
                flops=4 * width * rows * count * n_blocks,
                transcendentals=0,
                bytes_accessed=4 * width * rows + 4 * width * count * n_blocks,
            ),
            name="experts_back",
        )(gate_w, up_w, *dgates, *dups)


def body(
    tokens,
    routes,
    cotangent,
    norm_attn,
    w_query,
    w_key,
    w_value,
    w_out,
    norm_ffn,
    w_router,
    w_gate,
    w_up,
    w_down,
):
    comm = Comm()
    hold = lax.optimization_barrier
    count, width = tokens.shape[1], tokens.shape[2]
    top_k = routes.shape[2]
    n_experts, _, hidden_units = w_gate.shape
    all_experts = n_experts * comm.n_expert
    capacity = (9 * count * top_k + 8 * all_experts - 1) // (8 * all_experts)
    n_context, n_dp, share = comm.n_context, comm.n_dp, comm.share
    expert_index = lax.axis_index("expert")
    context_index = lax.axis_index("context")
    dp_index = lax.axis_index("dp")
    parity = context_index % share
    chunks = n_context // share
    units = hidden_units // share
    lanes = -(-all_experts // 32) * 32
    places = jnp.stack([expert_index * n_experts, dp_index, context_index // share])

    cot_t = cotangent[0].T
    routed = (
        routes[0].T[:, None, :] == jnp.arange(lanes, dtype=jnp.int32)[None, :, None]
    ).astype(F32)
    cot_message = jnp.concatenate([cot_t, routed.sum(0).astype(BF16)])
    tokens, cot_message = hold((tokens, cot_message))
    across = [comm.pair(cot_message)] if share == 2 else []
    cots = [cot_message] + [comm.pull(cot_message, k, 0) for k in range(1, comm.columns)]

    hidden = tokens[0].T.astype(F32)
    gain_attn = norm_attn.astype(F32)[:, None]
    gain_ffn = norm_ffn.astype(F32)[:, None]
    scale_attn = rms_scale(hidden)
    normed_attn = (hidden * scale_attn * gain_attn).astype(BF16)
    positions = context_index * count + jnp.arange(count, dtype=jnp.int32)
    cosine, sine = rope_tables(positions)
    key_t = rotate_t(mm(w_key, normed_attn, 0, 0), cosine, sine).astype(BF16)
    value_t = mm(w_value, normed_attn, 0, 0).astype(BF16)
    kv_width = key_t.shape[0]
    kv_own = jnp.concatenate([key_t, value_t], 0)
    kv_blocks = [kv_own]
    for s in range(1, n_context):
        pairs = [(i, i + s) for i in range(n_context - s)]
        kv_blocks.append(lax.ppermute(kv_own, "context", pairs))
    query_t = rotate_t(mm(w_query, normed_attn, 0, 0), cosine, sine)
    query_t = (query_t * HEAD_DIM**-0.5).astype(BF16)

    weights = prepare_weights(parity, w_gate, w_up, w_down, hidden_units // n_context, share)
    router_t = jnp.zeros((lanes, width), BF16).at[:all_experts].set(w_router.T)
    in_t, gate_w, up_w, down, down_t = weights
    in_t = in_t.reshape(n_experts * 2 * units, width)
    in_first = jnp.concatenate([in_t[: 2 * units], router_t])
    if across:
        across, in_t, in_first = hold((across, in_t, in_first))
        across = across + [comm.pull(across[0], k, 0) for k in range(1, comm.columns)]
        cots, across[0], in_t = hold((cots, across[0], in_t))
    cots, across = [[[(0, x, 0)] for x in part] for part in (cots, across)]
    others = comm.from_core(cots) if comm.cores == 2 else []
    kv_blocks, in_t, in_first, gate_w, up_w, down, down_t = hold(
        (kv_blocks, in_t, in_first, gate_w, up_w, down, down_t)
    )
    out_t, out_low, lse = attention_forward(context_index, query_t, kv_blocks)
    middle = hidden + mm(w_out, out_low, 0, 0)
    scale_ffn = rms_scale(middle)
    normed_ffn = (middle * scale_ffn * gain_ffn).astype(BF16)
    across = [block[0][1] for block in across]
    across, normed_ffn = hold((across, normed_ffn))
    rows, across = comm.gather_group(normed_ffn, across)
    across = [[(0, x, 0)] for x in across]
    if comm.cores == 2 and across:
        others = others + comm.from_core(across)
    cots = cots + across + others

    routed_all = jnp.concatenate(
        [block[0][1][block[0][2] + width : block[0][2] + width + lanes] for block in cots]
    )
    n_blocks = len(cots)
    before = jnp.triu(jnp.ones((count, count), BF16), 1)
    ranking = mm(routed_all, before, 1, 0)
    chosen = routed_all.astype(F32)
    kept = jnp.where(ranking < capacity, chosen, 0.0)

    def side_by_side(array):
        array = array.reshape(n_blocks, lanes, count)
        return jnp.concatenate([array[b] for b in range(n_blocks)], 1)

    chosen, kept = side_by_side(chosen), side_by_side(kept)

    row_count = width // comm.n_expert

    def for_experts(*arrays):
        out = []
        for j in range(comm.cores):
            for k in range(comm.columns):
                column, core = expert_index // comm.cores, expert_index % comm.cores
                column = (column - k) % comm.columns
                target = column * comm.cores + (core + j) % comm.cores
                pieces = [
                    lax.dynamic_slice_in_dim(array, target * row_count, row_count, 0)
                    for array in arrays
                ]
                out.append(jnp.concatenate(pieces))
        return out

    def to_experts(pieces):
        peers = [(j, k) for j in range(comm.cores) for k in range(comm.columns)]
        return pieces[:1] + [comm.pull(x, k, j) for x, (j, k) in zip(pieces[1:], peers[1:])]

    columns_sent = for_experts(normed_attn, out_low)
    chosen, columns_sent = hold((chosen, columns_sent))

    own = Experts(rows, cots, width, units, share, chunks, n_dp)
    groups, at = [], 0
    for n in (1, (n_experts - 1) // 2, n_experts - 1 - (n_experts - 1) // 2):
        if n:
            groups.append((at, n))
            at += n
    acts, dgates, dups, dscales, kept_parts, arrived, crossing = ([] for _ in range(7))
    scales = None

    def pass_on(g, values):
        if g >= len(groups):
            return values
        terms, values = hold((arrived[g], values))
        terms = [kept_parts[g]] + terms

        def part(k):
            return sum(term[k].astype(F32) for term in terms)

        sent = comm.send_context([part(k).astype(BF16) for k in range(1, chunks)], share)
        crossing.append([part(0).astype(BF16)] + sent)
        return values

    for g, (first, n) in enumerate(groups):
        if g == 0:
            gates_all, scales, *done = own.act(
                places, first, n, kept, chosen, in_first, down, make_gates=True
            )
        else:
            done = own.act(places, first, n, kept, scales, in_t, down)
        for target, value in zip((acts, dgates, dups, dscales, kept_parts), done):
            target.append(value)
        arrived.append(comm.send_dp(done[5:]))
        if g == 0:
            scales, columns_sent = hold((scales, columns_sent))
            columns_got = to_experts(columns_sent)
        if g == 1:
            scales = pass_on(0, scales)

    columns_got, acts = hold((columns_got, acts))
    h1_rows = [x[:row_count] for x in columns_got]
    ob_rows = [x[row_count:] for x in columns_got]
    near_count = n_blocks // comm.cores

    def both_cores(call):
        other = None
        if comm.cores == 2:
            other = comm.push(call(near_count, near_count), 0, 1)
        return call(0, near_count), other

    message = both_cores(
        lambda first, n: own.out(places, lanes, down_t, acts, dscales, first, n)
    )
    back_other = None
    if comm.cores == 2:
        back_other = own.back(gate_w, up_w, dgates, dups, near_count, near_count)
        back_other = comm.push(back_other, 0, 1)
    message, dgates = hold((message, dgates))
    dgates, crossing[0] = pass_on(1, (dgates, crossing[0]))
    back_near = own.back(gate_w, up_w, dgates, dups, 0, near_count)
    message = comm.return_hops(*message)
    message, back_near = hold((message, back_near))
    back = comm.return_hops(back_near, back_other)
    returned = comm.return_last(message)
    back = pass_on(2, back)
    grad_normed_ffn = comm.return_last(back)
    result = (middle + returned[:width]).astype(BF16)
    grad_gates = returned[width : width + lanes] + returned[width + lanes :]
    gates_own = gates_all[:, :count]

    upstream = cot_t.astype(F32)
    mean_grad = jnp.sum(gates_own * grad_gates, 0, keepdims=True)
    grad_logits = (gates_own * (grad_gates - mean_grad)).astype(BF16)
    grad_normed_ffn = grad_normed_ffn + mm(router_t, grad_logits, 0, 0)
    grad_gain_ffn = jnp.sum(grad_normed_ffn * middle * scale_ffn, 1)
    grad_middle = upstream + norm_back(grad_normed_ffn, middle, scale_ffn, gain_ffn)
    grad_branch = grad_middle.astype(BF16)

    gain_grid = grad_gain_ffn.reshape(-1, count)
    gain_lines = gain_grid.shape[0]
    gain_high = lax.reduce_precision(gain_grid, 8, 7)
    gain_rows = jnp.concatenate([gain_high, gain_grid - gain_high]).astype(BF16)
    gain_rows = jnp.pad(gain_rows, ((0, -2 * gain_lines % 16), (0, 0)))
    branch_all = comm.gather_columns(jnp.concatenate([grad_branch, grad_logits, gain_rows]))
    grad_attn_t = mm(w_out, grad_branch, 1, 0).astype(BF16)

    def attention_half(first, heads):
        return attention_backward(
            context_index, query_t, grad_attn_t, out_t, lse, kv_blocks, first, heads
        )

    def to_keys(grad_kv):
        return lax.all_to_all(grad_kv, "context", 0, 0, tiled=True)

    size_down = units // chunks // n_dp
    tiles = width // units

    def total_of(terms):
        total = jnp.concatenate([sum(x.astype(F32) for x in group) for group in terms])
        n = total.shape[0]
        part = total[:, : tiles * size_down].reshape(n, tiles, size_down, units)
        down = jnp.swapaxes(part, 1, 2).reshape(n, size_down, width)
        part = total[:, tiles * size_down :]
        return down, part.reshape(n, 2, share, part.shape[1] // 2 // share, units)

    def send_pair(part):
        if share == 1:
            return part[:, :, 0], None
        keep = lax.dynamic_index_in_dim(part, parity, 2, False)
        send = lax.dynamic_index_in_dim(part, 1 - parity, 2, False)
        return keep, comm.pair(send.astype(BF16))

    def both_columns(keep, other):
        if other is None:
            return keep
        other = other.astype(F32)
        first = jnp.where(parity == 0, keep, other)
        second = jnp.where(parity == 0, other, keep)
        chunk = hidden_units // n_context
        pieces = []
        for q in range(chunks):
            pieces += [x[..., q * chunk : (q + 1) * chunk] for x in (first, second)]
        return jnp.concatenate(pieces, -1)

    early = crossing[:-1]
    early, grad_attn_t = hold((early, grad_attn_t))
    totals = [total_of(early)] if early else []
    pairs = [send_pair(part) for _, part in totals]
    half = KV_HEADS // 2
    grad_query_a, grad_kv_a = attention_half(0, half)
    kv_a = to_keys(grad_kv_a)
    branch_all, grad_attn_t = hold((branch_all, grad_attn_t))
    branch_all = comm.gather_cores(branch_all)
    grad_query_b, grad_kv_b = attention_half(half, half)
    kv_a, grad_kv_b, branch_all, crossing[-1] = hold((kv_a, grad_kv_b, branch_all, crossing[-1]))
    kv_b = to_keys(grad_kv_b)

    out_terms = comm.scatter_rows(ob_rows, branch_all, width)
    h2_rows = [
        lax.dynamic_slice_in_dim(array, at + expert_index * row_count, row_count, 0)
        for j in range(comm.cores)
        for ((_, array, at),) in rows[j * near_count : j * near_count + comm.columns]
    ]
    router_rows = sum(mm(a, b[width : width + lanes], 1, 1) for a, b in zip(h2_rows, branch_all))
    gain_total = sum(x[width + lanes :].astype(F32) for x in branch_all)
    gain_total = gain_total[:gain_lines] + gain_total[gain_lines : 2 * gain_lines]
    gain_part = lax.dynamic_slice_in_dim(
        gain_total.reshape(width), expert_index * row_count, row_count, 0
    )
    rest = jnp.zeros((row_count, LANES - lanes - 1), F32)
    extra = jnp.concatenate([router_rows, gain_part[:, None], rest], 1).astype(BF16)
    extra = extra.reshape(n_context * n_dp, -1, LANES)

    grad_query_raw = jnp.concatenate(
        [rotate_t(x, cosine, -sine).astype(BF16) for x in (grad_query_a, grad_query_b)]
    )
    query_terms = comm.scatter_rows(h1_rows, comm.gather_expert(grad_query_raw), width)
    late = crossing[-1]
    pairs, kv_b = hold((pairs, kv_b))
    totals.append(total_of([late]))
    pairs.append(send_pair(totals[-1][1]))
    kv_sums = [jnp.sum(x.astype(F32), 0) for x in (kv_a, kv_b)]
    grad_key_raw = [rotate_t(kv_sum[0], cosine, -sine).astype(BF16) for kv_sum in kv_sums]
    grad_kv_raw = jnp.concatenate(grad_key_raw + [kv_sum[1].astype(BF16) for kv_sum in kv_sums])
    near_kv = comm.gather_columns(grad_kv_raw)
    near_kv, out_terms, query_terms = hold((near_kv, out_terms, query_terms))
    out_sum, query_sum = comm.scatter_rest(out_terms), comm.scatter_rest(query_terms)
    kv_terms = comm.scatter_rows(h1_rows, comm.gather_cores(near_kv), 2 * kv_width)
    extra, kv_terms[0] = hold((extra, kv_terms[0]))
    extra = lax.all_to_all(extra, ("context", "dp"), 0, 0, tiled=True)
    extra = jnp.sum(extra.astype(F32), 0)
    kv_rows = comm.scatter_rest(kv_terms)
    key_sum, value_sum = kv_rows[:, :kv_width], kv_rows[:, kv_width:]

    down_sum = jnp.concatenate([down for down, _ in totals])
    parts = [both_columns(*pair) for pair in pairs]
    gate_sum = jnp.concatenate([part[:, 0] for part in parts])
    up_sum = jnp.concatenate([part[:, 1] for part in parts])

    shard = (expert_index * n_context + context_index) * n_dp + dp_index
    shard_rows = query_sum.shape[0]

    def shard_of(array):
        return lax.dynamic_slice_in_dim(array, shard * shard_rows, shard_rows, 0).astype(F32)

    gain_sum = (
        jnp.sum(shard_of(w_query) * query_sum, 1)
        + jnp.sum(shard_of(w_key) * key_sum, 1)
        + jnp.sum(shard_of(w_value) * value_sum, 1)
    ) / shard_of(norm_attn)

    grad_normed_attn = mm(w_query, grad_query_raw, 1, 0)
    grad_normed_attn = grad_normed_attn + mm(w_key, grad_kv_raw[:kv_width], 1, 0)
    grad_normed_attn = grad_normed_attn + mm(w_value, grad_kv_raw[kv_width:], 1, 0)
    grad_hidden = grad_middle + norm_back(grad_normed_attn, hidden, scale_attn, gain_attn)
    return (
        result.T[None],
        grad_hidden.astype(BF16).T[None],
        gain_sum,
        query_sum,
        key_sum,
        value_sum,
        out_sum,
        extra[:, lanes],
        extra[:, :all_experts],
        gate_sum,
        up_sum,
        down_sum,
    )


def solution(mesh):
    rows = P(("expert", "dp"), "context", None)
    dense = P(("expert", "context", "dp"), None)
    vector = P(("expert", "context", "dp"))
    experts = P("expert", None, None)
    expert_grads = P("expert", ("context", "dp"), None)
    return jax.shard_map(
        body,
        mesh=mesh,
        in_specs=(rows, rows, rows) + (P(),) * 7 + (experts,) * 3,
        out_specs=(rows, rows, vector, dense, dense, dense, dense, vector, dense)
        + (expert_grads,) * 3,
        check_vma=False,
    )
```
